128 devices in a mesh: space: 16 (over y, x), band: 8 (over z, core).
Axes of the slice: x: 4, y: 4, z: 4, core: 2. Of those that a mesh axis runs over, the one named last changes fastest.
Arguments:
- vectors: float32 [65536, 1024], P('space', 'band')
- blocks: float32 [256, 7, 256, 256], P('space'), may hold values from -0.125 to 0.125
- neighbours: int32 [256, 7], P('space'), may hold values from 0 to 255, as said below
Outputs:
- rotated: float32 [65536, 1024], P('space', 'band')
The draws below stay inside these ranges and needn't reach their ends.
Inputs may be any that keep to these rules, and one draw needn't show every extreme that they name: neighbours[e, k] lies within 2 places of e in the cyclic order of the elements; for every e, neighbours[e, 1] = e - 2 and neighbours[e, 2] = e + 2, taken modulo 256.
All inputs are finite; a program needn't handle non-finite values.
Results may differ from the reference program's by a relative error of at most 0.000098.
Values sent between devices are 32-bit elements; how exact they have to be, the bound alone decides.
No kernel may reach another device: no remote copies, remote signals or barrier semaphores. Data moves between devices by JAX's collectives and lax.ppermute only.
A program may use at most 128 MiB of HBM per device.

```python
import math
import jax
import jax.numpy as jnp
from jax import lax

BASIS = 256
VECTORS = 1024
REACH = 2
ELEMENTS = 256
ORDER = 65536


def draw_neighbours(key, part):
    element_ids = jnp.arange(ELEMENTS, dtype=jnp.int32)[:, None]
    offsets = jax.random.randint(jax.random.fold_in(key, 11), (ELEMENTS, 7), -REACH, REACH + 1, dtype=jnp.int32)
    offsets = offsets.at[:, 1].set(-REACH).at[:, 2].set(REACH)
    return ((element_ids + offsets + ELEMENTS) % ELEMENTS).astype(jnp.int32)


def draw_vectors(key, part):
    key_base = jax.random.fold_in(key, 21)
    key_rows = jax.random.fold_in(key, 22)
    key_cols = jax.random.fold_in(key, 23)
    row_index = jnp.arange(ORDER, dtype=jnp.float32)[:, None]
    rising = jnp.exp(math.log(3.0) * row_index / ORDER)
    row_scale = jnp.exp(jax.random.uniform(key_rows, (ORDER, 1), jnp.float32, 0.0, math.log(10.0))) * rising
    base = jnp.clip(jax.random.normal(key_base, (ORDER, VECTORS), jnp.float32), -6.0, 6.0)
    col_scale = jnp.exp(jax.random.uniform(key_cols, (1, VECTORS), jnp.float32, 0.0, math.log(10.0)))
    return base * row_scale * col_scale


def levels(stream_key, dims, cuts, low, largest):
    level, own = 1.0, jax.random.fold_in(stream_key, 6)
    for axis_at, parts in cuts:
        heights = jnp.exp(jax.random.uniform(jax.random.fold_in(own, axis_at), (parts,), jnp.float32, low / len(cuts), largest / len(cuts)))
        level = level * jnp.repeat(heights, dims[axis_at] // parts).reshape([-1 if axis == axis_at else 1 for axis in range(len(dims))])
    return level


def bell_draw(stream_key, extent, spread, reach, split=(), kind=jnp.bfloat16):
    factor_of = levels(stream_key, extent, split, -0.22, 0.18) if split else 1.0
    values = jax.random.normal(stream_key, extent, jnp.float32) * spread * factor_of
    return jnp.minimum(jnp.maximum(values, -reach), reach).astype(kind)


def setup_inputs(seed: int = 0) -> dict:
    seeds = jax.random.split(jax.random.key(seed), 4)
    return {
        "vectors": draw_vectors(jax.random.fold_in(seeds[3], 71), 0),
        "blocks": bell_draw(seeds[1], (ELEMENTS, 7, BASIS, BASIS), (7 * BASIS) ** -0.5, 0.125, ((0, 16),), jnp.float32),
        "neighbours": draw_neighbours(jax.random.fold_in(seeds[3], 71), 0),
    }


def apply_operator(field, blocks, neighbours):
    elements = field.reshape(ELEMENTS, BASIS, VECTORS)

    def element_term(pair):
        element_blocks, element_ids = pair
        picked = elements[element_ids]
        return jnp.einsum('kij,kjm->im', element_blocks, picked, precision=lax.Precision.HIGHEST)
    result = lax.map(element_term, (blocks, neighbours))
    return result.reshape(ORDER, VECTORS)

def reference(vectors, blocks, neighbours):
    first_step = (apply_operator(vectors, blocks, neighbours) - 0.5 * vectors) / 1.5
    filtered = 2.0 * (apply_operator(first_step, blocks, neighbours) - 0.5 * first_step) / 1.5 - vectors
    gram = jnp.dot(filtered.T, filtered, precision=lax.Precision.HIGHEST, preferred_element_type=jnp.float32)
    scale = jnp.trace(gram) / VECTORS
    normed = gram / scale
    identity = jnp.eye(VECTORS, dtype=jnp.float32)
    squared = jnp.dot(normed, normed, precision=lax.Precision.HIGHEST, preferred_element_type=jnp.float32)
    poly = (15.0 * identity - 10.0 * normed + 3.0 * squared) / 8.0
    result = jnp.dot(filtered, poly, precision=lax.Precision.HIGHEST, preferred_element_type=jnp.float32)
    return result * jnp.sqrt(ORDER / scale)
```

```python
import functools
import jax
import jax.numpy as jnp
from jax import lax
from jax.experimental import pallas as pl
from jax.experimental.pallas import tpu as pltpu
from jax.sharding import PartitionSpec as P

VECTORS = 1024
REACH = 2
TILE = 256
PAIRS = [(i, j) for i in range(4) for j in range(i, 4)]
F32 = jnp.float32
BF16 = jnp.bfloat16


def split(x):
    hi = x.astype(BF16)
    lo = (x - hi.astype(F32)).astype(BF16)
    return hi, lo


def dot(a, b):
    return jnp.dot(a, b, preferred_element_type=F32)


def operator_kernel(step_kind, edge, elem_dev, slots_ref, blocks_ref, *refs):
    refs = list(refs)
    own_ref = refs.pop(0)
    before_ref = refs.pop(0) if edge else None
    after_ref = refs.pop(0) if edge else None
    base_ref = refs.pop(0) if step_kind == 2 else None
    if edge:
        refs.pop(0)
    out_ref, wide_ref = refs
    step = pl.program_id(0)

    def put(slot, value):
        hi, lo = split(value)
        wide_ref[slot, :, 0:128] = hi
        wide_ref[slot, :, 128:256] = lo

    @pl.when(step == 0)
    def _():
        if edge:
            for r in range(REACH):
                put(r, before_ref[r])
                put(REACH + elem_dev + r, after_ref[r])
            for r in range(2 * REACH):
                put(REACH + r, own_ref[r])
                put(elem_dev - REACH + r, own_ref[elem_dev - 2 * REACH + r])
        else:
            for r in range(elem_dev):
                put(REACH + r, own_ref[r])

    elem = element_of(step, edge, elem_dev)
    highs, lows, wides = [], [], []
    for k in range(7):
        hi, lo = split(blocks_ref[0, k])
        highs.append(hi)
        lows.append(lo)
        wides.append(wide_ref[slots_ref[elem * 7 + k]])
    left = jnp.concatenate(
        [jnp.concatenate(highs, axis=1), jnp.concatenate(lows, axis=1)], axis=0
    )
    prod = dot(left, jnp.concatenate(wides, axis=0))
    total = (prod[256:, 128:] + prod[256:, :128]) + (prod[:256, 128:] + prod[:256, :128])
    own = own_ref[elem]
    if step_kind == 1:
        out_ref[0] = (total - 0.5 * own) / 1.5
    else:
        out_ref[0] = 2.0 * (total - 0.5 * own) / 1.5 - base_ref[0]


def element_of(step, edge, elem_dev):
    if edge:
        return step + jnp.where(step >= REACH, elem_dev - 2 * REACH, 0)
    return step + REACH


def apply_operator(step_kind, edge, slots, blocks, own, halos=(), base=None, into=None):
    elem_dev = own.shape[0]
    count = 2 * REACH if edge else elem_dev - 2 * REACH
    pick = lambda s, *_: element_of(s, edge, elem_dev)
    panel_spec = pl.BlockSpec((1, 256, 128), lambda s, *_: (pick(s), 0, 0))
    whole = lambda x: pl.BlockSpec(x.shape, lambda s, *_: (0, 0, 0), pipeline_mode=pl.Buffered(1))
    args = [slots, blocks, own]
    specs = [
        pl.BlockSpec((1, 7, 256, 256), lambda s, *_: (pick(s), 0, 0, 0)),
        whole(own),
    ]
    if edge:
        args += list(halos)
        specs += [whole(h) for h in halos]
    if step_kind == 2:
        args.append(base)
        specs.append(panel_spec)
    aliases = {}
    if edge:
        aliases = {len(args): 0}
        args.append(into)
        specs.append(pl.BlockSpec(memory_space=pl.ANY))
    return pl.pallas_call(
        functools.partial(operator_kernel, step_kind, edge, elem_dev),
        out_shape=jax.ShapeDtypeStruct(own.shape, F32),
        grid_spec=pltpu.PrefetchScalarGridSpec(
            num_scalar_prefetch=1,
            grid=(count,),
            in_specs=specs,
            out_specs=panel_spec,
            scratch_shapes=[pltpu.VMEM((elem_dev + 2 * REACH, 256, 256), BF16)],
        ),
        input_output_aliases=aliases,
        compiler_params=pltpu.CompilerParams(vmem_limit_bytes=40 << 20),
        name=f"operator{step_kind}{'edge' if edge else 'mid'}",
    )(*args)


def gram_kernel(core_ref, rows_ref, keep_ref, send_ref, hi_ref, lo_ref):
    for b in range(8):
        hi, lo = split(rows_ref[b])
        hi_ref[:, b * 128 : (b + 1) * 128] = hi
        lo_ref[:, b * 128 : (b + 1) * 128] = lo
    core = core_ref[0]
    for n, (i, j) in enumerate(PAIRS):
        a, b = slice(i * TILE, (i + 1) * TILE), slice(j * TILE, (j + 1) * TILE)
        left = jnp.concatenate([hi_ref[:, a], hi_ref[:, a], lo_ref[:, a]], axis=0)
        right = jnp.concatenate([hi_ref[:, b], lo_ref[:, b], hi_ref[:, b]], axis=0)
        block = lax.dot_general(left, right, (((0,), (0,)), ((), ())), preferred_element_type=F32)
        half, at = n // 5, 2 * (n % 5)
        for target, wanted in ((keep_ref, half), (send_ref, 1 - half)):

            @pl.when(core == wanted)
            def _():
                target[at] = block[:, :128]
                target[at + 1] = block[:, 128:]


def local_gram(core, rows):
    half = jax.ShapeDtypeStruct((10, 256, 128), F32)
    vmem = pl.BlockSpec(memory_space=pltpu.VMEM)
    return pl.pallas_call(
        gram_kernel,
        out_shape=(half, half),
        in_specs=[pl.BlockSpec(memory_space=pltpu.SMEM), vmem],
        out_specs=(vmem, vmem),
        scratch_shapes=[pltpu.VMEM((512, 1024), BF16), pltpu.VMEM((512, 1024), BF16)],
        compiler_params=pltpu.CompilerParams(vmem_limit_bytes=40 << 20),
        name="gram",
    )(core, rows)


def turn_kernel(order, core_ref, mine_ref, theirs_ref, rows_ref, out_ref, nh_ref, nl_ref, fh_ref, fl_ref, y_ref):
    first = core_ref[0] == 0
    row = lax.broadcasted_iota(jnp.int32, (256, 128), 0)
    col = lax.broadcasted_iota(jnp.int32, (256, 128), 1)

    def packed(n, h):
        half, at = n // 5, 2 * (n % 5) + h
        here = first if half == 0 else jnp.logical_not(first)
        return jnp.where(here, mine_ref[at], theirs_ref[at])

    diag = jnp.zeros((256, 128), F32)
    for n, (i, j) in enumerate(PAIRS):
        if i == j:
            for h in range(2):
                diag += jnp.where(row == col + 128 * h, packed(n, h), 0.0)
    scale = jnp.sum(diag) / VECTORS
    for n, (i, j) in enumerate(PAIRS):
        for h in range(2):
            hi, lo = split(packed(n, h) / scale)
            c = j * TILE + h * 128
            nh_ref[i * TILE : (i + 1) * TILE, c : c + 128] = hi
            nl_ref[i * TILE : (i + 1) * TILE, c : c + 128] = lo
            if i != j:
                nh_ref[c : c + 128, i * TILE : (i + 1) * TILE] = hi.T
                nl_ref[c : c + 128, i * TILE : (i + 1) * TILE] = lo.T

    def times_normed(hi, lo, j):
        cols = slice(j * TILE, (j + 1) * TILE)
        left = jnp.concatenate([hi, hi, lo], axis=1)
        right = jnp.concatenate([nh_ref[:, cols], nl_ref[:, cols], nh_ref[:, cols]], axis=0)
        return dot(left, right)

    for b in range(8):
        hi, lo = split(rows_ref[b])
        fh_ref[:, b * 128 : (b + 1) * 128] = hi
        fl_ref[:, b * 128 : (b + 1) * 128] = lo
    for j in range(4):
        y_ref[:, j * TILE : (j + 1) * TILE] = times_normed(fh_ref[...], fl_ref[...], j)
    for b in range(8):
        cols = slice(b * 128, (b + 1) * 128)
        hi, lo = split(3.0 * y_ref[:, cols] - 10.0 * rows_ref[b])
        fh_ref[:, cols] = hi
        fl_ref[:, cols] = lo
    stretch = jnp.sqrt(jnp.full((8, 128), order, F32) / scale)[0:1]
    for j in range(4):
        z = times_normed(fh_ref[...], fl_ref[...], j)
        for h in range(2):
            b = 2 * j + h
            out_ref[b] = (15.0 * rows_ref[b] + z[:, h * 128 : (h + 1) * 128]) / 8.0 * stretch


def turn(core, mine, theirs, rows, order):
    vmem = pl.BlockSpec(memory_space=pltpu.VMEM)
    return pl.pallas_call(
        functools.partial(turn_kernel, order),
        out_shape=jax.ShapeDtypeStruct(rows.shape, F32),
        in_specs=[pl.BlockSpec(memory_space=pltpu.SMEM), vmem, vmem, vmem],
        out_specs=vmem,
        scratch_shapes=[
            pltpu.VMEM((1024, 1024), BF16),
            pltpu.VMEM((1024, 1024), BF16),
            pltpu.VMEM((512, 1024), BF16),
            pltpu.VMEM((512, 1024), BF16),
            pltpu.VMEM((512, 1024), F32),
        ],
        compiler_params=pltpu.CompilerParams(vmem_limit_bytes=40 << 20),
        name="turn",
    )(core, mine, theirs, rows)


def halos_of(first, last):
    size = lax.axis_size("space")
    up = [(i, (i + 1) % size) for i in range(size)]
    down = [(j, i) for i, j in up]
    return lax.ppermute(last, "space", up), lax.ppermute(first, "space", down)


def per_device(vectors, blocks, neighbours):
    elem_dev, basis = blocks.shape[0], blocks.shape[2]
    panel = vectors.shape[1]
    space_count, band_count = lax.axis_size("space"), lax.axis_size("band")
    total_elements = elem_dev * space_count
    local_ids = jnp.arange(elem_dev, dtype=jnp.int32)
    global_ids = lax.axis_index("space") * elem_dev + local_ids
    offsets = (neighbours - global_ids[:, None] + REACH + total_elements) % total_elements
    slots = (local_ids[:, None] + offsets).reshape(-1)

    start = vectors.reshape(elem_dev, basis, panel)
    halos = halos_of(start[:REACH], start[-REACH:])
    step = apply_operator(1, False, slots, blocks, start)
    step = apply_operator(1, True, slots, blocks, start, halos, into=step)
    halos = halos_of(step[:REACH], step[-REACH:])
    field = apply_operator(2, False, slots, blocks, step, base=start)
    field = apply_operator(2, True, slots, blocks, step, halos, base=start, into=field)

    share = elem_dev * basis // band_count
    rows = lax.all_to_all(field.reshape(band_count, share, panel), "band", split_axis=0, concat_axis=0, tiled=True)

    core = lax.axis_index("band") % 2
    core_arr = core.reshape(1)
    swap = [(i, i ^ 1) for i in range(band_count)]
    both = ("space", "band")
    groups = [[d for d in range(space_count * band_count) if d % 2 == c] for c in range(2)]
    peers = len(groups[0])
    keep, send = local_gram(core_arr, rows)
    half = keep + lax.ppermute(send, "band", swap)
    pieces = half.reshape(peers, -1, panel)
    pieces = lax.all_to_all(pieces, both, split_axis=0, concat_axis=0, axis_index_groups=groups, tiled=True)
    mine = jnp.sum(pieces, axis=0)
    copies = jnp.broadcast_to(mine[None], pieces.shape)
    copies = lax.all_to_all(copies, both, split_axis=0, concat_axis=0, axis_index_groups=groups, tiled=True)
    mine = copies.reshape(half.shape)
    theirs = lax.ppermute(mine, "band", swap)

    turned = turn(core_arr, mine, theirs, rows, float(total_elements * basis))
    turned = lax.all_to_all(turned, "band", split_axis=0, concat_axis=0, tiled=True)
    return turned.reshape(elem_dev * basis, panel)


def solution(mesh):
    return jax.shard_map(
        per_device,
        mesh=mesh,
        in_specs=(P("space", "band"), P("space", None, None, None), P("space", None)),
        out_specs=P("space", "band"),
        check_vma=False,
    )
```

```python
import functools
import jax
import jax.numpy as jnp
from jax import lax
from jax.experimental import pallas as pl
from jax.experimental.pallas import tpu as pltpu
from jax.sharding import PartitionSpec as P

VECTORS = 1024
REACH = 2
TILE = 256
PAIRS = [(i, j) for i in range(4) for j in range(i, 4)]
SPAN = 2 * REACH + 1
TOTAL = 256
RING = 8
BUILD_LIMIT = 24 << 20
STEP_LIMIT = 16 << 20
F32 = jnp.float32
BF16 = jnp.bfloat16


def split(x):
    hi = x.astype(BF16)
    lo = (x - hi.astype(F32)).astype(BF16)
    return hi, lo


def dot(a, b):
    return jnp.dot(a, b, preferred_element_type=F32)


def spread(wide_ref, slot, value):
    hi, lo = split(value)
    wide_ref[slot, :, 0:128] = hi
    wide_ref[slot, :, 128:256] = lo


def apply_one(op_ref, wide_ref, elem):
    near = wide_ref[pl.ds(elem, SPAN)].reshape(SPAN * 256, 256)
    prod = dot(op_ref[elem], near)
    return (prod[256:, 128:] + prod[256:, :128]) + (prod[:256, 128:] + prod[:256, :128])


def first_of(total, own):
    return (total - 0.5 * own) / 1.5


def second_of(total, own, base):
    return 2.0 * (total - 0.5 * own) / 1.5 - base


def build_kernel(count, near_ref, first_ref, blocks_ref, own_ref, step_ref, op_ref, wide_ref, ring_ref, sums_ref, sem):
    def fetch(n):
        elem = lax.rem(n + REACH, count)
        return pltpu.make_async_copy(blocks_ref.at[elem], ring_ref.at[lax.rem(n, RING)], sem.at[lax.rem(n, RING)])

    for n in range(RING):
        fetch(n).start()
    for r in range(count):
        spread(wide_ref, REACH + r, own_ref[r])

    def combine(n, u):
        elem = lax.rem(n + REACH, count)
        at = lax.rem(n, RING)
        fetch(n).wait()
        sums_ref[u, 0] = ring_ref[at, 1]
        sums_ref[u, SPAN - 1] = ring_ref[at, 2]
        for o in range(1, SPAN - 1):
            sums_ref[u, o] = jnp.zeros((256, 256), F32)
        for k in (0, 3, 4, 5, 6):
            o = lax.rem(near_ref[elem, k] - first_ref[0] - elem + REACH + 2 * TOTAL, TOTAL)
            sums_ref[u, o] = sums_ref[u, o] + ring_ref[at, k]
        for o in range(SPAN):
            hi, lo = split(sums_ref[u, o])
            op_ref[elem, :256, o * 256 : (o + 1) * 256] = hi
            op_ref[elem, 256:, o * 256 : (o + 1) * 256] = lo
        return elem

    def refill(n):
        @pl.when(n + RING < count)
        def _():
            fetch(n + RING).start()

    def inner(g, _):
        for u in range(2):
            n = 2 * g + u
            elem = combine(n, u)
            refill(n)
            step_ref[elem] = first_of(apply_one(op_ref, wide_ref, elem), own_ref[elem])
        return 0

    def outer(n, _):
        combine(n, 0)
        return 0

    lax.fori_loop(0, (count - 2 * REACH) // 2, inner, 0)
    lax.fori_loop(count - 2 * REACH, count, outer, 0)


def edges_of(count):
    return [*range(REACH), *range(count - REACH, count)]


def edge_kernel(kind, count, op_ref, own_ref, before_ref, after_ref, *refs):
    refs = list(refs)
    base_ref = refs.pop(0) if kind == 2 else None
    refs.pop(0)
    out_ref, wide_ref, made_ref, sem = refs
    for r in range(REACH):
        spread(wide_ref, r, before_ref[r])
        spread(wide_ref, REACH + count + r, after_ref[r])
    for r in range(2 * REACH):
        spread(wide_ref, REACH + r, own_ref[r])
        spread(wide_ref, count - REACH + r, own_ref[count - 2 * REACH + r])
    copies = []
    for at, elem in enumerate(edges_of(count)):
        total = apply_one(op_ref, wide_ref, elem)
        own = own_ref[elem]
        made_ref[at] = first_of(total, own) if kind == 1 else second_of(total, own, base_ref[elem])
        copies.append(pltpu.make_async_copy(made_ref.at[at], out_ref.at[elem], sem.at[at]))
        copies[-1].start()
    for copy in copies:
        copy.wait()


def inner_kernel(count, op_ref, own_ref, base_ref, out_ref, wide_ref):
    for r in range(count):
        spread(wide_ref, REACH + r, own_ref[r])

    def body(g, _):
        for u in range(4):
            elem = REACH + 4 * g + u
            out_ref[elem] = second_of(apply_one(op_ref, wide_ref, elem), own_ref[elem], base_ref[elem])
        return 0

    lax.fori_loop(0, (count - 2 * REACH) // 4, body, 0)


VMEM_SPEC = pl.BlockSpec(memory_space=pltpu.VMEM)
SMEM_SPEC = pl.BlockSpec(memory_space=pltpu.SMEM)
ANY_SPEC = pl.BlockSpec(memory_space=pl.ANY)


def build_operator(near, first, blocks, own):
    count = own.shape[0]
    return pl.pallas_call(
        functools.partial(build_kernel, count),
        out_shape=(
            jax.ShapeDtypeStruct(own.shape, F32),
            jax.ShapeDtypeStruct((count, 512, SPAN * 256), BF16),
        ),
        in_specs=[SMEM_SPEC, SMEM_SPEC, ANY_SPEC, VMEM_SPEC],
        out_specs=(VMEM_SPEC, VMEM_SPEC),
        scratch_shapes=[
            pltpu.VMEM((count + 2 * REACH, 256, 256), BF16),
            pltpu.VMEM((RING, 7, 256, 256), F32),
            pltpu.VMEM((2, SPAN, 256, 256), F32),
            pltpu.SemaphoreType.DMA((RING,)),
        ],
        compiler_params=pltpu.CompilerParams(vmem_limit_bytes=BUILD_LIMIT),
        name="build",
    )(near, first, blocks, own)


def step_edges(kind, op, own, halos, into, base=None):
    count = own.shape[0]
    args = [op, own, *halos] + ([base] if kind == 2 else []) + [into]
    return pl.pallas_call(
        functools.partial(edge_kernel, kind, count),
        out_shape=jax.ShapeDtypeStruct(own.shape, F32),
        in_specs=[VMEM_SPEC] * (len(args) - 1) + [ANY_SPEC],
        out_specs=ANY_SPEC,
        scratch_shapes=[
            pltpu.VMEM((count + 2 * REACH, 256, 256), BF16),
            pltpu.VMEM((2 * REACH, 256, 128), F32),
            pltpu.SemaphoreType.DMA((2 * REACH,)),
        ],
        input_output_aliases={len(args) - 1: 0},
        compiler_params=pltpu.CompilerParams(vmem_limit_bytes=STEP_LIMIT),
        name=f"edges{kind}",
    )(*args)


def step_inner(op, own, base):
    count = own.shape[0]
    return pl.pallas_call(
        functools.partial(inner_kernel, count),
        out_shape=jax.ShapeDtypeStruct(own.shape, F32),
        in_specs=[VMEM_SPEC] * 3,
        out_specs=VMEM_SPEC,
        scratch_shapes=[pltpu.VMEM((count + 2 * REACH, 256, 256), BF16)],
        compiler_params=pltpu.CompilerParams(vmem_limit_bytes=STEP_LIMIT),
        name="inner",
    )(op, own, base)


def gram_kernel(core_ref, rows_ref, keep_ref, send_ref, hi_ref, lo_ref):
    for b in range(8):
        hi, lo = split(rows_ref[b])
        hi_ref[:, b * 128 : (b + 1) * 128] = hi
        lo_ref[:, b * 128 : (b + 1) * 128] = lo
    core = core_ref[0]
    for n, (i, j) in enumerate(PAIRS):
        a, b = slice(i * TILE, (i + 1) * TILE), slice(j * TILE, (j + 1) * TILE)
        left = jnp.concatenate([hi_ref[:, a], hi_ref[:, a], lo_ref[:, a]], axis=0)
        right = jnp.concatenate([hi_ref[:, b], lo_ref[:, b], hi_ref[:, b]], axis=0)
        block = lax.dot_general(left, right, (((0,), (0,)), ((), ())), preferred_element_type=F32)
        half, at = n // 5, 2 * (n % 5)
        for target, wanted in ((keep_ref, half), (send_ref, 1 - half)):

            @pl.when(core == wanted)
            def _():
                target[at] = block[:, :128]
                target[at + 1] = block[:, 128:]


def local_gram(core, rows):
    half = jax.ShapeDtypeStruct((10, 256, 128), F32)
    vmem = pl.BlockSpec(memory_space=pltpu.VMEM)
    return pl.pallas_call(
        gram_kernel,
        out_shape=(half, half),
        in_specs=[pl.BlockSpec(memory_space=pltpu.SMEM), vmem],
        out_specs=(vmem, vmem),
        scratch_shapes=[pltpu.VMEM((512, 1024), BF16), pltpu.VMEM((512, 1024), BF16)],
        compiler_params=pltpu.CompilerParams(vmem_limit_bytes=40 << 20),
        name="gram",
    )(core, rows)


def turn_kernel(order, core_ref, mine_ref, theirs_ref, rows_ref, out_ref, nh_ref, nl_ref, fh_ref, fl_ref, y_ref):
    first = core_ref[0] == 0
    row = lax.broadcasted_iota(jnp.int32, (256, 128), 0)
    col = lax.broadcasted_iota(jnp.int32, (256, 128), 1)

    def packed(n, h):
        half, at = n // 5, 2 * (n % 5) + h
        here = first if half == 0 else jnp.logical_not(first)
        return jnp.where(here, mine_ref[at], theirs_ref[at])

    diag = jnp.zeros((256, 128), F32)
    for n, (i, j) in enumerate(PAIRS):
        if i == j:
            for h in range(2):
                diag += jnp.where(row == col + 128 * h, packed(n, h), 0.0)
    scale = jnp.sum(diag) / VECTORS
    for n, (i, j) in enumerate(PAIRS):
        for h in range(2):
            hi, lo = split(packed(n, h) / scale)
            c = j * TILE + h * 128
            nh_ref[i * TILE : (i + 1) * TILE, c : c + 128] = hi
            nl_ref[i * TILE : (i + 1) * TILE, c : c + 128] = lo
            if i != j:
                nh_ref[c : c + 128, i * TILE : (i + 1) * TILE] = hi.T
                nl_ref[c : c + 128, i * TILE : (i + 1) * TILE] = lo.T

    def times_normed(hi, lo, j):
        cols = slice(j * TILE, (j + 1) * TILE)
        left = jnp.concatenate([hi, hi, lo], axis=1)
        right = jnp.concatenate([nh_ref[:, cols], nl_ref[:, cols], nh_ref[:, cols]], axis=0)
        return dot(left, right)

    for b in range(8):
        hi, lo = split(rows_ref[b])
        fh_ref[:, b * 128 : (b + 1) * 128] = hi
        fl_ref[:, b * 128 : (b + 1) * 128] = lo
    for j in range(4):
        y_ref[:, j * TILE : (j + 1) * TILE] = times_normed(fh_ref[...], fl_ref[...], j)
    for b in range(8):
        cols = slice(b * 128, (b + 1) * 128)
        hi, lo = split(3.0 * y_ref[:, cols] - 10.0 * rows_ref[b])
        fh_ref[:, cols] = hi
        fl_ref[:, cols] = lo
    stretch = jnp.sqrt(jnp.full((8, 128), order, F32) / scale)[0:1]
    for j in range(4):
        z = times_normed(fh_ref[...], fl_ref[...], j)
        for h in range(2):
            b = 2 * j + h
            out_ref[b] = (15.0 * rows_ref[b] + z[:, h * 128 : (h + 1) * 128]) / 8.0 * stretch


def turn(core, mine, theirs, rows, order):
    vmem = pl.BlockSpec(memory_space=pltpu.VMEM)
    return pl.pallas_call(
        functools.partial(turn_kernel, order),
        out_shape=jax.ShapeDtypeStruct(rows.shape, F32),
        in_specs=[pl.BlockSpec(memory_space=pltpu.SMEM), vmem, vmem, vmem],
        out_specs=vmem,
        scratch_shapes=[
            pltpu.VMEM((1024, 1024), BF16),
            pltpu.VMEM((1024, 1024), BF16),
            pltpu.VMEM((512, 1024), BF16),
            pltpu.VMEM((512, 1024), BF16),
            pltpu.VMEM((512, 1024), F32),
        ],
        compiler_params=pltpu.CompilerParams(vmem_limit_bytes=40 << 20),
        name="turn",
    )(core, mine, theirs, rows)


def halos_of(first, last):
    size = lax.axis_size("space")
    up = [(i, (i + 1) % size) for i in range(size)]
    down = [(j, i) for i, j in up]
    return lax.ppermute(last, "space", up), lax.ppermute(first, "space", down)


def per_device(vectors, blocks, neighbours):
    elem_dev, basis = blocks.shape[0], blocks.shape[2]
    panel = vectors.shape[1]
    space_count, band_count = lax.axis_size("space"), lax.axis_size("band")
    total_elements = elem_dev * space_count
    first = (lax.axis_index("space") * elem_dev).reshape(1)

    start = vectors.reshape(elem_dev, basis, panel)
    halos = halos_of(start[:REACH], start[-REACH:])
    step, op = build_operator(neighbours, first, blocks, start)
    step = step_edges(1, op, start, halos, step)
    halos = halos_of(step[:REACH], step[-REACH:])
    field = step_inner(op, step, start)
    field = step_edges(2, op, step, halos, field, base=start)

    share = elem_dev * basis // band_count
    rows = lax.all_to_all(field.reshape(band_count, share, panel), "band", split_axis=0, concat_axis=0, tiled=True)

    core = lax.axis_index("band") % 2
    core_arr = core.reshape(1)
    swap = [(i, i ^ 1) for i in range(band_count)]
    both = ("space", "band")
    groups = [[d for d in range(space_count * band_count) if d % 2 == c] for c in range(2)]
    peers = len(groups[0])
    keep, send = local_gram(core_arr, rows)
    half = keep + lax.ppermute(send, "band", swap)
    pieces = half.reshape(peers, -1, panel)
    pieces = lax.all_to_all(pieces, both, split_axis=0, concat_axis=0, axis_index_groups=groups, tiled=True)
    mine = jnp.sum(pieces, axis=0)
    copies = jnp.broadcast_to(mine[None], pieces.shape)
    copies = lax.all_to_all(copies, both, split_axis=0, concat_axis=0, axis_index_groups=groups, tiled=True)
    mine = copies.reshape(half.shape)
    theirs = lax.ppermute(mine, "band", swap)

    turned = turn(core_arr, mine, theirs, rows, float(total_elements * basis))
    turned = lax.all_to_all(turned, "band", split_axis=0, concat_axis=0, tiled=True)
    return turned.reshape(elem_dev * basis, panel)


def solution(mesh):
    return jax.shard_map(
        per_device,
        mesh=mesh,
        in_specs=(P("space", "band"), P("space", None, None, None), P("space", None)),
        out_specs=P("space", "band"),
        check_vma=False,
    )
```

```python
import functools
import jax
import jax.numpy as jnp
from jax import lax
from jax.experimental import pallas as pl
from jax.experimental.pallas import tpu as pltpu
from jax.sharding import PartitionSpec as P

VECTORS = 1024
REACH = 2
TILE = 256
PAIRS = [(i, j) for i in range(4) for j in range(i, 4)]
SPAN = 2 * REACH + 1
TOTAL = 256
RING = 8
BUILD_LIMIT = 26 << 20
STEP_LIMIT = 16 << 20
TURN_LIMIT = 32 << 20
F32 = jnp.float32
BF16 = jnp.bfloat16


def split(x):
    hi = x.astype(BF16)
    lo = (x - hi.astype(F32)).astype(BF16)
    return hi, lo


def dot(a, b):
    return jnp.dot(a, b, preferred_element_type=F32)


def spread(wide_ref, slot, value):
    hi, lo = split(value)
    wide_ref[slot, :, 0:128] = hi
    wide_ref[slot, :, 128:256] = lo


def apply_one(op_ref, wide_ref, elem):
    near = wide_ref[pl.ds(elem, SPAN)].reshape(SPAN * 256, 256)
    prod = dot(op_ref[elem], near)
    return (prod[256:, 128:] + prod[256:, :128]) + (prod[:256, 128:] + prod[:256, :128])


def first_of(total, own):
    return (total - 0.5 * own) / 1.5


def second_of(total, own, base):
    return 2.0 * (total - 0.5 * own) / 1.5 - base


def build_kernel(count, near_ref, at_ref, blocks_ref, vectors_ref, step_ref, op_ref, wide_ref, ring_ref, sums_ref, own_ref, sem, own_sem):
    def fetch(n):
        elem = lax.rem(n + REACH, count)
        return pltpu.make_async_copy(blocks_ref.at[elem], ring_ref.at[lax.rem(n, RING)], sem.at[lax.rem(n, RING)])

    first = (at_ref[1] * 4 + at_ref[0]) * count
    load = pltpu.make_async_copy(vectors_ref, own_ref, own_sem)
    load.start()
    for n in range(RING):
        fetch(n).start()
    load.wait()
    for r in range(count):
        spread(wide_ref, REACH + r, own_ref[r])

    def combine(n, u):
        elem = lax.rem(n + REACH, count)
        at = lax.rem(n, RING)
        fetch(n).wait()
        sums_ref[u, 0] = ring_ref[at, 1]
        sums_ref[u, SPAN - 1] = ring_ref[at, 2]
        for o in range(1, SPAN - 1):
            sums_ref[u, o] = jnp.zeros((256, 256), F32)
        for k in (0, 3, 4, 5, 6):
            o = lax.rem(near_ref[k, elem] - first - elem + REACH + 2 * TOTAL, TOTAL)
            sums_ref[u, o] = sums_ref[u, o] + ring_ref[at, k]
        for o in range(SPAN):
            hi, lo = split(sums_ref[u, o])
            op_ref[elem, :256, o * 256 : (o + 1) * 256] = hi
            op_ref[elem, 256:, o * 256 : (o + 1) * 256] = lo
        return elem

    def refill(n):
        @pl.when(n + RING < count)
        def _():
            fetch(n + RING).start()

    def inner(g, _):
        for u in range(2):
            n = 2 * g + u
            elem = combine(n, u)
            refill(n)
            step_ref[elem - REACH] = first_of(apply_one(op_ref, wide_ref, elem), own_ref[elem])
        return 0

    def outer(n, _):
        combine(n, 0)
        return 0

    lax.fori_loop(0, (count - 2 * REACH) // 2, inner, 0)
    lax.fori_loop(count - 2 * REACH, count, outer, 0)


def edges_of(count):
    return [*range(REACH), *range(count - REACH, count)]


def first_edge_kernel(count, op_ref, own_ref, before_ref, after_ref, low_ref, high_ref, wide_ref):
    for r in range(REACH):
        spread(wide_ref, r, before_ref[r])
        spread(wide_ref, REACH + count + r, after_ref[r])
    for r in range(2 * REACH):
        spread(wide_ref, REACH + r, own_ref[r])
        spread(wide_ref, count - REACH + r, own_ref[count - 2 * REACH + r])
    for at, elem in enumerate(edges_of(count)):
        out_ref = low_ref if at < REACH else high_ref
        out_ref[at % REACH] = first_of(apply_one(op_ref, wide_ref, elem), own_ref[elem])


def side_of(elem, count, c):
    return lax.rem(elem // (count // 2) + c, 2), lax.rem(elem, count // 2)


def second_edge_kernel(count, at_ref, op_ref, mid_ref, low_ref, high_ref, before_ref, after_ref, base_ref, _, out_ref, wide_ref, made_ref, sem):
    for r in range(REACH):
        spread(wide_ref, r, before_ref[r])
        spread(wide_ref, REACH + r, low_ref[r])
        spread(wide_ref, 2 * REACH + r, mid_ref[r])
        spread(wide_ref, count - REACH + r, mid_ref[count - 3 * REACH + r])
        spread(wide_ref, count + r, high_ref[r])
        spread(wide_ref, REACH + count + r, after_ref[r])
    copies = []
    for at, elem in enumerate(edges_of(count)):
        own = (low_ref if at < REACH else high_ref)[at % REACH]
        made_ref[at] = second_of(apply_one(op_ref, wide_ref, elem), own, base_ref[elem])
        side, place = side_of(elem, count, at_ref[3])
        copies.append(pltpu.make_async_copy(made_ref.at[at], out_ref.at[side, place], sem.at[at]))
        copies[-1].start()
    for copy in copies:
        copy.wait()


def inner_kernel(count, at_ref, op_ref, mid_ref, low_ref, high_ref, base_ref, out_ref, wide_ref):
    for r in range(REACH):
        spread(wide_ref, REACH + r, low_ref[r])
        spread(wide_ref, count + r, high_ref[r])
    for r in range(count - 2 * REACH):
        spread(wide_ref, 2 * REACH + r, mid_ref[r])

    def body(g, _):
        for u in range(4):
            at = 4 * g + u
            elem = REACH + at
            side, place = side_of(elem, count, at_ref[3])
            out_ref[side, place] = second_of(apply_one(op_ref, wide_ref, elem), mid_ref[at], base_ref[elem])
        return 0

    lax.fori_loop(0, (count - 2 * REACH) // 4, body, 0)


VMEM_SPEC = pl.BlockSpec(memory_space=pltpu.VMEM)
SMEM_SPEC = pl.BlockSpec(memory_space=pltpu.SMEM)
ANY_SPEC = pl.BlockSpec(memory_space=pl.ANY)
HBM_SPEC = pl.BlockSpec(memory_space=pltpu.HBM)


def shaped(*shape, dtype=F32):
    return jax.ShapeDtypeStruct(shape, dtype)


def call(kernel, name, outs, specs, scratch, args, limit, **kwargs):
    return pl.pallas_call(
        kernel,
        out_shape=outs,
        in_specs=specs,
        out_specs=kwargs.pop("out_specs", jax.tree.map(lambda _: VMEM_SPEC, outs)),
        scratch_shapes=scratch,
        compiler_params=pltpu.CompilerParams(vmem_limit_bytes=limit),
        name=name,
        **kwargs,
    )(*args)


def wide_scratch(count):
    return pltpu.VMEM((count + 2 * REACH, 256, 256), BF16)


def build_operator(near, here, blocks, own):
    count = own.shape[0]
    return call(
        functools.partial(build_kernel, count),
        "build",
        (shaped(count - 2 * REACH, 256, 128), shaped(count, 512, SPAN * 256, dtype=BF16)),
        [SMEM_SPEC, SMEM_SPEC, HBM_SPEC, HBM_SPEC],
        [
            wide_scratch(count),
            pltpu.VMEM((RING, 7, 256, 256), F32),
            pltpu.VMEM((2, SPAN, 256, 256), F32),
            pltpu.VMEM(own.shape, F32),
            pltpu.SemaphoreType.DMA((RING,)),
            pltpu.SemaphoreType.DMA,
        ],
        (near, here, blocks, own),
        BUILD_LIMIT,
    )


def first_edges(op, own, halos):
    count = own.shape[0]
    edge = shaped(REACH, 256, 128)
    return call(
        functools.partial(first_edge_kernel, count), "edges1", (edge, edge), [VMEM_SPEC] * 4,
        [wide_scratch(count)], (op, own, *halos), STEP_LIMIT,
    )


def second_inner(here, op, mid, low, high, base):
    count = base.shape[0]
    return call(
        functools.partial(inner_kernel, count), "inner", shaped(2, count // 2, 256, 128), [SMEM_SPEC] + [VMEM_SPEC] * 5,
        [wide_scratch(count)], (here, op, mid, low, high, base), STEP_LIMIT,
    )


def second_edges(here, op, mid, low, high, halos, base, into):
    count = base.shape[0]
    return call(
        functools.partial(second_edge_kernel, count), "edges2", shaped(*into.shape),
        [SMEM_SPEC] + [VMEM_SPEC] * 7 + [ANY_SPEC],
        [wide_scratch(count), pltpu.VMEM((2 * REACH, 256, 128), F32), pltpu.SemaphoreType.DMA((2 * REACH,))],
        (here, op, mid, low, high, *halos, base, into), STEP_LIMIT,
        out_specs=ANY_SPEC, input_output_aliases={8: 0},
    )


def pair_kernel(at_ref, both_ref, got_ref, *out_refs):
    z = at_ref[2]
    for k in range(4):
        chip = lax.rem(z + k, 4)
        out_refs[k][0] = both_ref[0, chip]
        out_refs[k][1] = got_ref[chip]


def share_kernel(axis, count, at_ref, *refs):
    ins, outs, sum_ref = refs[:count], refs[count:-1], refs[-1]
    total = ins[0][...]
    for ref in ins[1:]:
        total = total + ref[...]
    sum_ref[...] = total
    size = outs[0].shape[0]
    for k in range(4):
        part = lax.rem(at_ref[axis] + k, 4)
        outs[k][...] = sum_ref[pl.ds(pl.multiple_of(part * size, size), size)]


def shares(here, axis, shift, arrays):
    size, panel = arrays[0].shape
    part = shaped(size // 4, panel)
    outs = call(
        functools.partial(share_kernel, axis, len(arrays)), f"share{axis}", (part,) * 4,
        [SMEM_SPEC] + [VMEM_SPEC] * len(arrays), [pltpu.VMEM((size, panel), F32)], (here, *arrays), STEP_LIMIT,
    )
    got = {k: shift(outs[k], k) for k in SHIFTS}
    return [outs[0]] + [got[k] for k in (1, 2, 3)]


def lanes(start, size):
    return pl.ds(pl.multiple_of(start, size), size)


def half_of_gram(half, hi_ref, lo_ref, out_ref):
    for m in range(5):
        (i0, j0), (i1, j1) = PAIRS[m], PAIRS[m + 5]
        i = lanes(jnp.where(half == 0, i0, i1) * TILE, TILE)
        j = lanes(jnp.where(half == 0, j0, j1) * TILE, TILE)
        left_hi, right_hi = hi_ref[:, i], hi_ref[:, j]
        left = jnp.concatenate([left_hi, left_hi, lo_ref[:, i]], axis=0)
        right = jnp.concatenate([right_hi, lo_ref[:, j], right_hi], axis=0)
        block = lax.dot_general(left, right, (((0,), (0,)), ((), ())), preferred_element_type=F32)
        out_ref[2 * m] = block[:, :128]
        out_ref[2 * m + 1] = block[:, 128:]


def gram_send_kernel(at_ref, *refs):
    parts, (rows_ref, hi_ref, lo_ref, out_ref) = refs[:4], refs[4:]
    z, c = at_ref[2], at_ref[3]
    for k in range(4):
        for j in range(2):
            band = lax.rem(z + 4 - k, 4) * 2 + lax.rem(c + j, 2)
            value = parts[k][j]
            rows_ref[band] = value
            hi, lo = split(value)
            hi_ref[:, lanes(band * 128, 128)] = hi
            lo_ref[:, lanes(band * 128, 128)] = lo
    half_of_gram(1 - c, hi_ref, lo_ref, out_ref)


def gram_keep_kernel(at_ref, hi_ref, lo_ref, out_ref):
    half_of_gram(at_ref[3], hi_ref, lo_ref, out_ref)


def times_normed(hi, lo, nh, nl):
    return dot(jnp.concatenate([hi, hi, lo], axis=1), jnp.concatenate([nh, nl, nh], axis=0))


def normed_kernel(order, at_ref, mine_ref, theirs_ref, rows_ref, hi_ref, lo_ref, nh_ref, nl_ref, gh_ref, gl_ref, stretch_ref, gram_ref, y_ref):
    x, y, c = at_ref[0], at_ref[1], at_ref[3]
    for kx in range(4):
        for ky in range(4):
            piece = lax.rem(x + 4 - kx, 4) * 4 + lax.rem(y + 4 - ky, 4)
            rows = pl.ds(pl.multiple_of(piece * 160, 160), 160)
            gram_ref[c, rows] = mine_ref[kx * 4 + ky]
            gram_ref[1 - c, rows] = theirs_ref[kx * 4 + ky]

    def packed(n, h):
        at = 2 * (n % 5) + h
        return gram_ref[n // 5, at * 256 : (at + 1) * 256]

    row = lax.broadcasted_iota(jnp.int32, (256, 128), 0)
    col = lax.broadcasted_iota(jnp.int32, (256, 128), 1)
    diag = jnp.zeros((256, 128), F32)
    for n, (i, j) in enumerate(PAIRS):
        if i == j:
            for h in range(2):
                diag += jnp.where(row == col + 128 * h, packed(n, h), 0.0)
    scale = jnp.sum(diag) / VECTORS
    for n, (i, j) in enumerate(PAIRS):
        for h in range(2):
            hi, lo = split(packed(n, h) / scale)
            at = j * TILE + h * 128
            nh_ref[i * TILE : (i + 1) * TILE, at : at + 128] = hi
            nl_ref[i * TILE : (i + 1) * TILE, at : at + 128] = lo
            if i != j:
                nh_ref[at : at + 128, i * TILE : (i + 1) * TILE] = hi.T
                nl_ref[at : at + 128, i * TILE : (i + 1) * TILE] = lo.T
    for j in range(4):
        cols = slice(j * TILE, (j + 1) * TILE)
        y_ref[:, cols] = times_normed(hi_ref[...], lo_ref[...], nh_ref[:, cols], nl_ref[:, cols])
    for b in range(8):
        cols = slice(b * 128, (b + 1) * 128)
        hi, lo = split(3.0 * y_ref[:, cols] - 10.0 * rows_ref[b])
        gh_ref[:, cols] = hi
        gl_ref[:, cols] = lo
    stretch_ref[...] = jnp.sqrt(jnp.full((8, 128), order, F32) / scale)


def turned_kernel(k, at_ref, rows_ref, gh_ref, gl_ref, nh_ref, nl_ref, stretch_ref, out_ref):
    z, c = at_ref[2], at_ref[3]
    chip = lax.rem(z + k, 4)
    cols = lanes(chip * TILE, TILE)
    prod = times_normed(gh_ref[...], gl_ref[...], nh_ref[:, cols], nl_ref[:, cols])
    for j in range(2):
        part = 15.0 * rows_ref[2 * chip + j] + prod[:, j * 128 : (j + 1) * 128]
        out_ref[lax.rem(c + j, 2)] = part / 8.0 * stretch_ref[0:1]


def place_kernel(at_ref, *refs):
    parts, got_ref, out_ref, sem = refs[:4], refs[4], refs[5], refs[6]
    z, c = at_ref[2], at_ref[3]
    copies = []
    for k in range(4):
        chip = lax.rem(z + 4 - k, 4)
        copies.append(pltpu.make_async_copy(parts[k].at[0], out_ref.at[c * 4 + chip], sem.at[k]))
        copies.append(pltpu.make_async_copy(got_ref.at[k], out_ref.at[(1 - c) * 4 + chip], sem.at[4 + k]))
    for copy in copies:
        copy.start()
    for copy in copies:
        copy.wait()


SHIFTS = (2, 1, 3)


def swap_cores(x):
    return lax.ppermute(x, "band", [(i, i ^ 1) for i in range(8)])


def shift_z(x, k):
    return lax.ppermute(x, "band", [(i, (i + 2 * k) % 8) for i in range(8)])


def shift_x(x, k):
    return lax.ppermute(x, "space", [(i, (i & 12) | ((i + k) & 3)) for i in range(16)])


def shift_y(x, k):
    return lax.ppermute(x, "space", [(i, (i + 4 * k) % 16) for i in range(16)])


def gathered(x, shift):
    got = {k: shift(x, k) for k in SHIFTS}
    return jnp.stack([x] + [got[k] for k in (1, 2, 3)])


def halos_of(first, last):
    size = lax.axis_size("space")
    up = [(i, (i + 1) % size) for i in range(size)]
    down = [(j, i) for i, j in up]
    return lax.ppermute(last, "space", up), lax.ppermute(first, "space", down)


def per_device(vectors, blocks, neighbours):
    elem_dev, basis = blocks.shape[0], blocks.shape[2]
    panel = vectors.shape[1]
    order = float(elem_dev * basis * lax.axis_size("space"))
    space, band = lax.axis_index("space"), lax.axis_index("band")
    x, y, z, c = space & 3, space >> 2, band >> 1, band & 1
    here = jnp.stack([x, y, z, c]).astype(jnp.int32)

    start = vectors.reshape(elem_dev, basis, panel)
    halos = halos_of(start[:REACH], start[-REACH:])
    mid, op = build_operator(neighbours.T, here, blocks, start)
    low, high = first_edges(op, start, halos)
    halos = halos_of(low, high)
    field = second_inner(here, op, mid, low, high, start)
    field = second_edges(here, op, mid, low, high, halos, start, field)

    share = elem_dev * basis // 8
    both = field.reshape(2, 4, share, panel)
    got = swap_cores(both[1])
    pairs = call(
        pair_kernel, "pair", (shaped(2, share, panel),) * 4, [SMEM_SPEC] + [VMEM_SPEC] * 2, [], (here, both, got), STEP_LIMIT
    )
    parts = {k: shift_z(pairs[k], k) for k in SHIFTS}
    parts[0] = pairs[0]
    half = shaped(10, 256, 128)
    wide = shaped(share, VECTORS, dtype=BF16)
    rows, hi, lo, send = call(
        gram_send_kernel, "gram1", (shaped(8, share, panel), wide, wide, half), [SMEM_SPEC] + [VMEM_SPEC] * 4, [],
        (here, *(parts[k] for k in range(4))), STEP_LIMIT,
    )
    theirs = swap_cores(send)
    keep = call(gram_keep_kernel, "gram2", half, [SMEM_SPEC] + [VMEM_SPEC] * 2, [], (here, hi, lo), STEP_LIMIT)
    pieces = shares(here, 0, shift_x, [keep.reshape(2560, panel), theirs.reshape(2560, panel)])
    pieces = shares(here, 1, shift_y, pieces)
    piece = (pieces[0] + pieces[1]) + (pieces[2] + pieces[3])
    got = [shift_z(piece, k) for k in SHIFTS]
    piece = piece + got[0] + (got[1] + got[2])
    mine = gathered(gathered(piece, shift_y), shift_x).reshape(16, 160, panel)
    theirs = swap_cores(mine)

    square = shaped(VECTORS, VECTORS, dtype=BF16)
    nh, nl, gh, gl, stretch = call(
        functools.partial(normed_kernel, order), "normed", (square, square, wide, wide, shaped(8, 128)),
        [SMEM_SPEC] + [VMEM_SPEC] * 5, [pltpu.VMEM((2, 2560, 128), F32), pltpu.VMEM((share, VECTORS), F32)],
        (here, mine, theirs, rows, hi, lo), TURN_LIMIT,
    )
    turned = [
        call(
            functools.partial(turned_kernel, k), f"turned{k}", shaped(2, share, panel), [SMEM_SPEC] + [VMEM_SPEC] * 6, [],
            (here, rows, gh, gl, nh, nl, stretch), STEP_LIMIT,
        )
        for k in range(4)
    ]
    parts = {k: shift_z(turned[k], k) for k in SHIFTS}
    parts[0] = turned[0]
    got = swap_cores(jnp.stack([parts[k][1] for k in range(4)]))
    placed = call(
        place_kernel, "place", shaped(8, share, panel), [SMEM_SPEC] + [ANY_SPEC] * 5, [pltpu.SemaphoreType.DMA((8,))],
        (here, *(parts[k] for k in range(4)), got), STEP_LIMIT, out_specs=ANY_SPEC,
    )
    return placed.reshape(elem_dev * basis, panel)


def solution(mesh):
    return jax.shard_map(
        per_device,
        mesh=mesh,
        in_specs=(P("space", "band"), P("space", None, None, None), P("space", None)),
        out_specs=P("space", "band"),
        check_vma=False,
    )
```

```python
import functools
import jax
import jax.numpy as jnp
from jax import lax
from jax.experimental import pallas as pl
from jax.experimental.pallas import tpu as pltpu
from jax.sharding import PartitionSpec as P


VECTORS = 1024
REACH = 2
TILE = 256
PAIRS = [(i, j) for i in range(4) for j in range(i, 4)]
SPAN = 2 * REACH + 1
TOTAL = 256
RING = 8
BUILD_LIMIT = 26 << 20
STEP_LIMIT = 16 << 20
OPERATOR_LIMIT = 8 << 20
TURN_LIMIT = 32 << 20
F32 = jnp.float32
BF16 = jnp.bfloat16


def split(x):
    hi = x.astype(BF16)
    lo = (x - hi.astype(F32)).astype(BF16)
    return hi, lo


def dot(a, b):
    return jnp.dot(a, b, preferred_element_type=F32)


def spread(wide_ref, slot, value):
    hi, lo = split(value)
    wide_ref[slot, :, 0:128] = hi
    wide_ref[slot, :, 128:256] = lo


def apply_one(op_ref, wide_ref, elem):
    near = wide_ref[pl.ds(elem, SPAN)].reshape(SPAN * 256, 256)
    prod = dot(op_ref[elem], near)
    return (prod[256:, 128:] + prod[256:, :128]) + (prod[:256, 128:] + prod[:256, :128])


def first_of(total, own):
    return (total - 0.5 * own) / 1.5


def second_of(total, own, base):
    return 2.0 * (total - 0.5 * own) / 1.5 - base


def build_kernel(count, near_ref, at_ref, blocks_ref, vectors_ref, step_ref, op_ref, wide_ref, ring_ref, sums_ref, own_ref, sem, own_sem):
    def fetch(n):
        elem = lax.rem(n + REACH, count)
        return pltpu.make_async_copy(blocks_ref.at[elem], ring_ref.at[lax.rem(n, RING)], sem.at[lax.rem(n, RING)])

    first = (at_ref[1] * 4 + at_ref[0]) * count
    load = pltpu.make_async_copy(vectors_ref, own_ref, own_sem)
    load.start()
    for n in range(RING):
        fetch(n).start()
    load.wait()
    for r in range(count):
        spread(wide_ref, REACH + r, own_ref[r])

    def combine(n, u):
        elem = lax.rem(n + REACH, count)
        at = lax.rem(n, RING)
        fetch(n).wait()
        sums_ref[u, 0] = ring_ref[at, 1]
        sums_ref[u, SPAN - 1] = ring_ref[at, 2]
        for o in range(1, SPAN - 1):
            sums_ref[u, o] = jnp.zeros((256, 256), F32)
        for k in (0, 3, 4, 5, 6):
            o = lax.rem(near_ref[k, elem] - first - elem + REACH + 2 * TOTAL, TOTAL)
            sums_ref[u, o] = sums_ref[u, o] + ring_ref[at, k]
        for o in range(SPAN):
            hi, lo = split(sums_ref[u, o])
            op_ref[elem, :256, o * 256 : (o + 1) * 256] = hi
            op_ref[elem, 256:, o * 256 : (o + 1) * 256] = lo
        return elem

    def refill(n):
        @pl.when(n + RING < count)
        def _():
            fetch(n + RING).start()

    def inner(g, _):
        for u in range(2):
            n = 2 * g + u
            elem = combine(n, u)
            refill(n)
            step_ref[elem - REACH] = first_of(apply_one(op_ref, wide_ref, elem), own_ref[elem])
        return 0

    def outer(n, _):
        combine(n, 0)
        return 0

    lax.fori_loop(0, (count - 2 * REACH) // 2, inner, 0)
    lax.fori_loop(count - 2 * REACH, count, outer, 0)


def edges_of(count):
    return [*range(REACH), *range(count - REACH, count)]


def first_edge_kernel(count, op_ref, own_ref, before_ref, after_ref, low_ref, high_ref, wide_ref):
    for r in range(REACH):
        spread(wide_ref, r, before_ref[r])
        spread(wide_ref, REACH + count + r, after_ref[r])
    for r in range(2 * REACH):
        spread(wide_ref, REACH + r, own_ref[r])
        spread(wide_ref, count - REACH + r, own_ref[count - 2 * REACH + r])
    for at, elem in enumerate(edges_of(count)):
        out_ref = low_ref if at < REACH else high_ref
        out_ref[at % REACH] = first_of(apply_one(op_ref, wide_ref, elem), own_ref[elem])


def second_edge_kernel(count, at_ref, op_ref, mid_ref, low_ref, high_ref, before_ref, after_ref, base_ref, done_ref, *refs):
    own_refs, (other_ref, wide_ref, all_ref) = refs[:4], refs[4:]
    for r in range(REACH):
        spread(wide_ref, r, before_ref[r])
        spread(wide_ref, REACH + r, low_ref[r])
        spread(wide_ref, 2 * REACH + r, mid_ref[r])
        spread(wide_ref, count - REACH + r, mid_ref[count - 3 * REACH + r])
        spread(wide_ref, count + r, high_ref[r])
        spread(wide_ref, REACH + count + r, after_ref[r])
    for at, elem in enumerate(edges_of(count)):
        own = (low_ref if at < REACH else high_ref)[at % REACH]
        all_ref[elem] = second_of(apply_one(op_ref, wide_ref, elem), own, base_ref[elem])
    for at in range(count - 2 * REACH):
        all_ref[REACH + at] = done_ref[at]
    z, c = at_ref[2], at_ref[3]
    half = count // 2
    for k in range(4):
        chip = lax.rem(z + k, 4)
        for r in range(2):
            other_ref[k, r * 256 : (r + 1) * 256] = all_ref[(1 - c) * half + chip * 2 + r]
            own_refs[k][r * 256 : (r + 1) * 256] = all_ref[c * half + chip * 2 + r]


def inner_kernel(count, op_ref, mid_ref, low_ref, high_ref, base_ref, out_ref, wide_ref):
    for r in range(REACH):
        spread(wide_ref, REACH + r, low_ref[r])
        spread(wide_ref, count + r, high_ref[r])
    for r in range(count - 2 * REACH):
        spread(wide_ref, 2 * REACH + r, mid_ref[r])

    def body(g, _):
        for u in range(4):
            at = 4 * g + u
            elem = REACH + at
            out_ref[at] = second_of(apply_one(op_ref, wide_ref, elem), mid_ref[at], base_ref[elem])
        return 0

    lax.fori_loop(0, (count - 2 * REACH) // 4, body, 0)


VMEM_SPEC = pl.BlockSpec(memory_space=pltpu.VMEM)
SMEM_SPEC = pl.BlockSpec(memory_space=pltpu.SMEM)
ANY_SPEC = pl.BlockSpec(memory_space=pl.ANY)
HBM_SPEC = pl.BlockSpec(memory_space=pltpu.HBM)


def shaped(*shape, dtype=F32):
    return jax.ShapeDtypeStruct(shape, dtype)


def call(kernel, outs, specs, scratch, args, limit, **kwargs):
    return pl.pallas_call(
        kernel,
        out_shape=outs,
        in_specs=specs,
        out_specs=kwargs.pop("out_specs", jax.tree.map(lambda _: VMEM_SPEC, outs)),
        scratch_shapes=scratch,
        compiler_params=pltpu.CompilerParams(vmem_limit_bytes=limit),
        **kwargs,
    )(*args)


def wide_scratch(count):
    return pltpu.VMEM((count + 2 * REACH, 256, 256), BF16)


def build_operator(near, here, blocks, own):
    count = own.shape[0]
    return call(
        functools.partial(build_kernel, count),
        (shaped(count - 2 * REACH, 256, 128), shaped(count, 512, SPAN * 256, dtype=BF16)),
        [SMEM_SPEC, SMEM_SPEC, HBM_SPEC, HBM_SPEC],
        [
            wide_scratch(count),
            pltpu.VMEM((RING, 7, 256, 256), F32),
            pltpu.VMEM((2, SPAN, 256, 256), F32),
            pltpu.VMEM(own.shape, F32),
            pltpu.SemaphoreType.DMA((RING,)),
            pltpu.SemaphoreType.DMA,
        ],
        (near, here, blocks, own),
        BUILD_LIMIT,
    )


def first_edges(op, own, halos):
    count = own.shape[0]
    edge = shaped(REACH, 256, 128)
    return call(
        functools.partial(first_edge_kernel, count), (edge, edge), [VMEM_SPEC] * 4,
        [wide_scratch(count)], (op, own, *halos), OPERATOR_LIMIT,
    )


def second_inner(op, mid, low, high, base):
    count = base.shape[0]
    return call(
        functools.partial(inner_kernel, count), shaped(*mid.shape), [VMEM_SPEC] * 5,
        [wide_scratch(count)], (op, mid, low, high, base), OPERATOR_LIMIT,
    )


def second_edges(here, op, mid, low, high, halos, base, done):
    count = base.shape[0]
    chunk = shaped(512, 128)
    outs = call(
        functools.partial(second_edge_kernel, count), (chunk,) * 4 + (shaped(4, 512, 128),),
        [SMEM_SPEC] + [VMEM_SPEC] * 8,
        [wide_scratch(count), pltpu.VMEM(base.shape, F32)],
        (here, op, mid, low, high, *halos, base, done), OPERATOR_LIMIT,
    )
    return outs[:4], outs[4]


def bulk_kernel(*refs):
    own_refs, got_ref, out_refs = refs[:4], refs[4], refs[5:]
    for k in range(1, 4):
        for i, m in enumerate(chunks_for(k)):
            out_refs[k - 1][i, 0] = own_refs[m][...]
            out_refs[k - 1][i, 1] = got_ref[m]


def chunks_for(k):
    return [m for m in range(4) if m != k]


def share_kernel(axis, count, at_ref, *refs):
    ins, outs, sum_ref = refs[:count], refs[count:-1], refs[-1]
    total = ins[0][...]
    for ref in ins[1:]:
        total = total + ref[...]
    sum_ref[...] = total
    size = outs[0].shape[0]
    for k in range(4):
        part = lax.rem(at_ref[axis] + k, 4)
        outs[k][...] = sum_ref[pl.ds(pl.multiple_of(part * size, size), size)]


def shares(here, axis, shift, arrays):
    size, panel = arrays[0].shape
    part = shaped(size // 4, panel)
    outs = call(
        functools.partial(share_kernel, axis, len(arrays)), (part,) * 4,
        [SMEM_SPEC] + [VMEM_SPEC] * len(arrays), [pltpu.VMEM((size, panel), F32)], (here, *arrays), STEP_LIMIT,
    )
    got = {k: shift(outs[k], k) for k in SHIFTS}
    return [outs[0]] + [got[k] for k in (1, 2, 3)]


def lanes(start, size):
    return pl.ds(pl.multiple_of(start, size), size)


def half_of_gram(half, hi_ref, lo_ref, out_ref):
    for m in range(5):
        (i0, j0), (i1, j1) = PAIRS[m], PAIRS[m + 5]
        i = lanes(jnp.where(half == 0, i0, i1) * TILE, TILE)
        j = lanes(jnp.where(half == 0, j0, j1) * TILE, TILE)
        left_hi, right_hi = hi_ref[:, i], hi_ref[:, j]
        left = jnp.concatenate([left_hi, left_hi, lo_ref[:, i]], axis=0)
        right = jnp.concatenate([right_hi, lo_ref[:, j], right_hi], axis=0)
        block = lax.dot_general(left, right, (((0,), (0,)), ((), ())), preferred_element_type=F32)
        out_ref[2 * m] = block[:, :128]
        out_ref[2 * m + 1] = block[:, 128:]


def gram_send_kernel(at_ref, *refs):
    owns, gots, (hi_ref, lo_ref, out_ref) = refs[:4], refs[4:8], refs[8:]
    z, c = at_ref[2], at_ref[3]
    for k in range(4):
        for j in range(2):
            band = lax.rem(z + 4 - k, 4) * 2 + lax.rem(c + j, 2)
            hi, lo = split((owns, gots)[j][k][...])
            hi_ref[:, lanes(band * 128, 128)] = hi
            lo_ref[:, lanes(band * 128, 128)] = lo
    half_of_gram(1 - c, hi_ref, lo_ref, out_ref)


def gram_keep_kernel(at_ref, hi_ref, lo_ref, out_ref):
    half_of_gram(at_ref[3], hi_ref, lo_ref, out_ref)


def times_normed(hi, lo, nh, nl):
    return dot(jnp.concatenate([hi, hi, lo], axis=1), jnp.concatenate([nh, nl, nh], axis=0))


def poly_kernel(order, at_ref, mine_ref, theirs_ref, ph_ref, pl_ref, stretch_ref, gram_ref, nh_ref, nl_ref, poly_ref):
    x, y, z, c = at_ref[0], at_ref[1], at_ref[2], at_ref[3]
    for ky in range(4):
        for kx in range(4):
            piece = lax.rem(y + 4 - ky, 4) * 4 + lax.rem(x + 4 - kx, 4)
            rows = pl.ds(pl.multiple_of(piece * 160, 160), 160)
            gram_ref[c, rows] = mine_ref[ky * 4 + kx]
            gram_ref[1 - c, rows] = theirs_ref[ky * 4 + kx]

    def packed(n, h):
        at = 2 * (n % 5) + h
        return gram_ref[n // 5, at * 256 : (at + 1) * 256]

    row = lax.broadcasted_iota(jnp.int32, (256, 128), 0)
    col = lax.broadcasted_iota(jnp.int32, (256, 128), 1)
    diag = jnp.zeros((256, 128), F32)
    for n, (i, j) in enumerate(PAIRS):
        if i == j:
            for h in range(2):
                diag += jnp.where(row == col + 128 * h, packed(n, h), 0.0)
    scale = jnp.sum(diag) / VECTORS
    for n, (i, j) in enumerate(PAIRS):
        for h in range(2):
            hi, lo = split(packed(n, h) / scale)
            at = j * TILE + h * 128
            nh_ref[i * TILE : (i + 1) * TILE, at : at + 128] = hi
            nl_ref[i * TILE : (i + 1) * TILE, at : at + 128] = lo
            if i != j:
                nh_ref[at : at + 128, i * TILE : (i + 1) * TILE] = hi.T
                nl_ref[at : at + 128, i * TILE : (i + 1) * TILE] = lo.T
    stretch_ref[...] = jnp.sqrt(jnp.full((8, 128), order, F32) / scale)
    right = []
    for j in range(2):
        band = lanes((2 * z + lax.rem(c + j, 2)) * 128, 128)
        right.append((nh_ref[:, band], nl_ref[:, band]))
    nh = jnp.concatenate([right[0][0], right[1][0]], axis=1)
    nl = jnp.concatenate([right[0][1], right[1][1]], axis=1)
    squared = times_normed(nh_ref[...], nl_ref[...], nh, nl)
    poly_ref[...] = 3.0 * squared - 10.0 * (nh.astype(F32) + nl.astype(F32))
    for q in range(4):
        for j in range(2):
            band = lax.rem(z + q, 4) * 2 + lax.rem(c + j, 2)
            part = poly_ref[pl.ds(pl.multiple_of(band * 128, 128), 128)]
            if q == 0:
                r = lax.broadcasted_iota(jnp.int32, (128, 256), 0)
                l = lax.broadcasted_iota(jnp.int32, (128, 256), 1)
                part = part + jnp.where(l == r + 128 * j, 15.0, 0.0)
            hi, lo = split(part / 8.0)
            at = q * 256 + j * 128
            ph_ref[at : at + 128] = hi
            pl_ref[at : at + 128] = lo


def turned_kernel(*refs):
    owns, got_ref, part_owns, part_gots, bulks = refs[:4], refs[4], refs[5:8], refs[8:11], refs[11:14]
    ph_ref, pl_ref, stretch_ref, mine_ref, theirs_ref = refs[14:]

    def piece(r, q, j):
        k = (4 - q) % 4
        if q == 0:
            return owns[r][...] if j == 0 else got_ref[r]
        if r == 0:
            return (part_owns, part_gots)[j][k - 1][...]
        return bulks[k - 1][chunks_for(k).index((r + k) % 4), j]

    ph, low = ph_ref[...], pl_ref[...]
    for r in range(4):
        highs, lows = [], []
        for q in range(4):
            for j in range(2):
                hi, lo = split(piece(r, q, j))
                highs.append(hi)
                lows.append(lo)
        out = times_normed(jnp.concatenate(highs, axis=1), jnp.concatenate(lows, axis=1), ph, low)
        stretch = stretch_ref[0:1]
        mine_ref[r] = out[:, :128] * stretch
        theirs_ref[r] = out[:, 128:] * stretch


def place_kernel(at_ref, mine_ref, got_ref, out_ref, sem):
    z, c = at_ref[2], at_ref[3]
    copies = []
    for k in range(4):
        chip = lax.rem(z + k, 4)
        copies.append(pltpu.make_async_copy(mine_ref.at[k], out_ref.at[c * 4 + chip], sem.at[k]))
        copies.append(pltpu.make_async_copy(got_ref.at[k], out_ref.at[(1 - c) * 4 + chip], sem.at[4 + k]))
    for copy in copies:
        copy.start()
    for copy in copies:
        copy.wait()


SHIFTS = (2, 1, 3)


def swap_cores(x):
    return lax.ppermute(x, "band", [(i, i ^ 1) for i in range(8)])


def shift_z(x, k):
    return lax.ppermute(x, "band", [(i, (i + 2 * k) % 8) for i in range(8)])


def shift_x(x, k):
    return lax.ppermute(x, "space", [(i, (i & 12) | ((i + k) & 3)) for i in range(16)])


def shift_y(x, k):
    return lax.ppermute(x, "space", [(i, (i + 4 * k) % 16) for i in range(16)])


def gathered(x, shift):
    got = {k: shift(x, k) for k in SHIFTS}
    return jnp.stack([x] + [got[k] for k in (1, 2, 3)])


def halos_of(first, last):
    size = lax.axis_size("space")
    up = [(i, (i + 1) % size) for i in range(size)]
    down = [(j, i) for i, j in up]
    return lax.ppermute(last, "space", up), lax.ppermute(first, "space", down)


def steps(vectors, blocks, neighbours):
    elem_dev, basis = blocks.shape[0], blocks.shape[2]
    panel = vectors.shape[1]
    order = float(elem_dev * basis * lax.axis_size("space"))
    space, band = lax.axis_index("space"), lax.axis_index("band")
    x, y, z, c = space & 3, space >> 2, band >> 1, band & 1
    here = jnp.stack([x, y, z, c]).astype(jnp.int32)

    start = vectors.reshape(elem_dev, basis, panel)
    halos = halos_of(start[:REACH], start[-REACH:])
    mid, op = build_operator(neighbours.T, here, blocks, start)
    low, high = first_edges(op, start, halos)
    halos = halos_of(low, high)
    done = second_inner(op, mid, low, high, start)
    own, other = second_edges(here, op, mid, low, high, halos, start, done)

    share = elem_dev * basis // 8
    got = swap_cores(other)
    part_own = {k: shift_z(own[k], k) for k in SHIFTS}
    part_got = {k: shift_z(got[k], k) for k in SHIFTS}
    part_own[0], part_got[0] = own[0], got[0]
    part_own = [part_own[k] for k in range(4)]
    part_got = [part_got[k] for k in range(4)]

    late_own, late_got, part_own, part_got = lax.optimization_barrier((own, got, part_own, part_got))
    bulks = call(bulk_kernel, (shaped(3, 2, share, panel),) * 3, [VMEM_SPEC] * 5, [], (*late_own, late_got), STEP_LIMIT)
    sent = []
    for k in (1, 2, 3):
        sent.append(shift_z(bulks[k - 1], k))
    bulks = sent

    half = shaped(10, 256, 128)
    wide = shaped(share, VECTORS, dtype=BF16)
    hi, lo, send = call(
        gram_send_kernel, (wide, wide, half), [SMEM_SPEC] + [VMEM_SPEC] * 8, [],
        (here, *part_own, *part_got), STEP_LIMIT,
    )
    theirs = swap_cores(send)
    keep = call(gram_keep_kernel, half, [SMEM_SPEC] + [VMEM_SPEC] * 2, [], (here, hi, lo), STEP_LIMIT)
    pieces = shares(here, 1, shift_y, [keep.reshape(2560, panel), theirs.reshape(2560, panel)])
    pieces = shares(here, 0, shift_x, pieces)
    piece = (pieces[0] + pieces[1]) + (pieces[2] + pieces[3])
    sums = [shift_z(piece, k) for k in SHIFTS]
    piece = piece + sums[0] + (sums[1] + sums[2])
    mine = gathered(gathered(piece, shift_x), shift_y).reshape(16, 160, panel)
    theirs = swap_cores(mine)

    poly = shaped(VECTORS, TILE, dtype=BF16)
    ph, low, stretch = call(
        functools.partial(poly_kernel, order), (poly, poly, shaped(8, 128)), [SMEM_SPEC] + [VMEM_SPEC] * 2,
        [
            pltpu.VMEM((2, 2560, 128), F32),
            pltpu.VMEM((VECTORS, VECTORS), BF16),
            pltpu.VMEM((VECTORS, VECTORS), BF16),
            pltpu.VMEM((VECTORS, TILE), F32),
        ],
        (here, mine, theirs), TURN_LIMIT,
    )
    quarter = shaped(4, share, panel)
    mine, theirs = call(
        turned_kernel, (quarter, quarter), [VMEM_SPEC] * 17, [],
        (*own, got, *part_own[1:], *part_got[1:], *bulks, ph, low, stretch), TURN_LIMIT,
    )
    theirs = swap_cores(theirs)
    placed = call(
        place_kernel, shaped(8, share, panel), [SMEM_SPEC] + [ANY_SPEC] * 2, [pltpu.SemaphoreType.DMA((8,))],
        (here, mine, theirs), STEP_LIMIT, out_specs=ANY_SPEC,
    )
    return placed.reshape(elem_dev * basis, panel)


def solution(mesh):
    return jax.shard_map(
        steps,
        mesh=mesh,
        in_specs=(P("space", "band"), P("space", None, None, None), P("space", None)),
        out_specs=P("space", "band"),
        check_vma=False,
    )
```

```python
import functools
import jax
import jax.numpy as jnp
from jax import lax
from jax.experimental import pallas as pl
from jax.experimental.pallas import tpu as pltpu
from jax.sharding import PartitionSpec as P


VECTORS = 1024
REACH = 2
TILE = 256
PAIRS = [(i, j) for i in range(4) for j in range(i, 4)]
SPAN = 2 * REACH + 1
TOTAL = 256
RING = 8
BUILD_LIMIT = 26 << 20
STEP_LIMIT = 16 << 20
OPERATOR_LIMIT = 8 << 20
TURN_LIMIT = 32 << 20
F32 = jnp.float32
BF16 = jnp.bfloat16


def split(x):
    hi = x.astype(BF16)
    lo = (x - hi.astype(F32)).astype(BF16)
    return hi, lo


def dot(a, b):
    return jnp.dot(a, b, preferred_element_type=F32)


def spread(wide_ref, slot, value):
    hi, lo = split(value)
    wide_ref[slot, :, 0:128] = hi
    wide_ref[slot, :, 128:256] = lo


def apply_one(op_ref, wide_ref, elem):
    near = wide_ref[pl.ds(elem, SPAN)].reshape(SPAN * 256, 256)
    prod = dot(op_ref[elem], near)
    return (prod[256:, 128:] + prod[256:, :128]) + (prod[:256, 128:] + prod[:256, :128])


def first_of(total, own):
    return (total - 0.5 * own) / 1.5


def second_of(total, own, base):
    return 2.0 * (total - 0.5 * own) / 1.5 - base


def build_kernel(count, near_ref, at_ref, blocks_ref, vectors_ref, step_ref, op_ref, wide_ref, ring_ref, sums_ref, own_ref, sem, own_sem):
    def fetch(n):
        elem = lax.rem(n + REACH, count)
        return pltpu.make_async_copy(blocks_ref.at[elem], ring_ref.at[lax.rem(n, RING)], sem.at[lax.rem(n, RING)])

    first = (at_ref[1] * 4 + at_ref[0]) * count
    load = pltpu.make_async_copy(vectors_ref, own_ref, own_sem)
    load.start()
    for n in range(RING):
        fetch(n).start()
    load.wait()
    for r in range(count):
        spread(wide_ref, REACH + r, own_ref[r])

    def combine(n, u):
        elem = lax.rem(n + REACH, count)
        at = lax.rem(n, RING)
        fetch(n).wait()
        sums_ref[u, 0] = ring_ref[at, 1]
        sums_ref[u, SPAN - 1] = ring_ref[at, 2]
        for o in range(1, SPAN - 1):
            sums_ref[u, o] = jnp.zeros((256, 256), F32)
        for k in (0, 3, 4, 5, 6):
            o = lax.rem(near_ref[k, elem] - first - elem + REACH + 2 * TOTAL, TOTAL)
            sums_ref[u, o] = sums_ref[u, o] + ring_ref[at, k]
        for o in range(SPAN):
            hi, lo = split(sums_ref[u, o])
            op_ref[elem, :256, o * 256 : (o + 1) * 256] = hi
            op_ref[elem, 256:, o * 256 : (o + 1) * 256] = lo
        return elem

    def refill(n):
        @pl.when(n + RING < count)
        def _():
            fetch(n + RING).start()

    def inner(g, _):
        for u in range(2):
            n = 2 * g + u
            elem = combine(n, u)
            refill(n)
            step_ref[elem - REACH] = first_of(apply_one(op_ref, wide_ref, elem), own_ref[elem])
        return 0

    def outer(n, _):
        combine(n, 0)
        return 0

    lax.fori_loop(0, (count - 2 * REACH) // 2, inner, 0)
    lax.fori_loop(count - 2 * REACH, count, outer, 0)


def edges_of(count):
    return [*range(REACH), *range(count - REACH, count)]


def first_edge_kernel(count, op_ref, own_ref, before_ref, after_ref, low_ref, high_ref, wide_ref):
    for r in range(REACH):
        spread(wide_ref, r, before_ref[r])
        spread(wide_ref, REACH + count + r, after_ref[r])
    for r in range(2 * REACH):
        spread(wide_ref, REACH + r, own_ref[r])
        spread(wide_ref, count - REACH + r, own_ref[count - 2 * REACH + r])
    for at, elem in enumerate(edges_of(count)):
        out_ref = low_ref if at < REACH else high_ref
        out_ref[at % REACH] = first_of(apply_one(op_ref, wide_ref, elem), own_ref[elem])


def second_edge_kernel(count, at_ref, op_ref, mid_ref, low_ref, high_ref, before_ref, after_ref, base_ref, done_ref, *refs):
    own_refs, (other_ref, wide_ref, all_ref) = refs[:4], refs[4:]
    for r in range(REACH):
        spread(wide_ref, r, before_ref[r])
        spread(wide_ref, REACH + r, low_ref[r])
        spread(wide_ref, 2 * REACH + r, mid_ref[r])
        spread(wide_ref, count - REACH + r, mid_ref[count - 3 * REACH + r])
        spread(wide_ref, count + r, high_ref[r])
        spread(wide_ref, REACH + count + r, after_ref[r])
    for at, elem in enumerate(edges_of(count)):
        own = (low_ref if at < REACH else high_ref)[at % REACH]
        all_ref[elem] = second_of(apply_one(op_ref, wide_ref, elem), own, base_ref[elem])
    for at in range(count - 2 * REACH):
        all_ref[REACH + at] = done_ref[at]
    z, c = at_ref[2], at_ref[3]
    half = count // 2
    for k in range(4):
        chip = lax.rem(z + k, 4)
        for r in range(2):
            other_ref[k, r * 256 : (r + 1) * 256] = all_ref[(1 - c) * half + chip * 2 + r]
            own_refs[k][r * 256 : (r + 1) * 256] = all_ref[c * half + chip * 2 + r]


def inner_kernel(count, op_ref, mid_ref, low_ref, high_ref, base_ref, out_ref, wide_ref):
    for r in range(REACH):
        spread(wide_ref, REACH + r, low_ref[r])
        spread(wide_ref, count + r, high_ref[r])
    for r in range(count - 2 * REACH):
        spread(wide_ref, 2 * REACH + r, mid_ref[r])

    def body(g, _):
        for u in range(4):
            at = 4 * g + u
            elem = REACH + at
            out_ref[at] = second_of(apply_one(op_ref, wide_ref, elem), mid_ref[at], base_ref[elem])
        return 0

    lax.fori_loop(0, (count - 2 * REACH) // 4, body, 0)


VMEM_SPEC = pl.BlockSpec(memory_space=pltpu.VMEM)
SMEM_SPEC = pl.BlockSpec(memory_space=pltpu.SMEM)
ANY_SPEC = pl.BlockSpec(memory_space=pl.ANY)
HBM_SPEC = pl.BlockSpec(memory_space=pltpu.HBM)


def shaped(*shape, dtype=F32):
    return jax.ShapeDtypeStruct(shape, dtype)


def call(kernel, outs, specs, scratch, args, limit, **kwargs):
    return pl.pallas_call(
        kernel,
        out_shape=outs,
        in_specs=specs,
        out_specs=kwargs.pop("out_specs", jax.tree.map(lambda _: VMEM_SPEC, outs)),
        scratch_shapes=scratch,
        compiler_params=pltpu.CompilerParams(vmem_limit_bytes=limit),
        **kwargs,
    )(*args)


def wide_scratch(count):
    return pltpu.VMEM((count + 2 * REACH, 256, 256), BF16)


def build_operator(near, here, blocks, own):
    count = own.shape[0]
    return call(
        functools.partial(build_kernel, count),
        (shaped(count - 2 * REACH, 256, 128), shaped(count, 512, SPAN * 256, dtype=BF16)),
        [SMEM_SPEC, SMEM_SPEC, HBM_SPEC, HBM_SPEC],
        [
            wide_scratch(count),
            pltpu.VMEM((RING, 7, 256, 256), F32),
            pltpu.VMEM((2, SPAN, 256, 256), F32),
            pltpu.VMEM(own.shape, F32),
            pltpu.SemaphoreType.DMA((RING,)),
            pltpu.SemaphoreType.DMA,
        ],
        (near, here, blocks, own),
        BUILD_LIMIT,
    )


def first_edges(op, own, halos):
    count = own.shape[0]
    edge = shaped(REACH, 256, 128)
    return call(
        functools.partial(first_edge_kernel, count), (edge, edge), [VMEM_SPEC] * 4,
        [wide_scratch(count)], (op, own, *halos), OPERATOR_LIMIT,
    )


def second_inner(op, mid, low, high, base):
    count = base.shape[0]
    return call(
        functools.partial(inner_kernel, count), shaped(*mid.shape), [VMEM_SPEC] * 5,
        [wide_scratch(count)], (op, mid, low, high, base), OPERATOR_LIMIT,
    )


def second_edges(here, op, mid, low, high, halos, base, done):
    count = base.shape[0]
    chunk = shaped(512, 128)
    outs = call(
        functools.partial(second_edge_kernel, count), (chunk,) * 4 + (shaped(4, 512, 128),),
        [SMEM_SPEC] + [VMEM_SPEC] * 8,
        [wide_scratch(count), pltpu.VMEM(base.shape, F32)],
        (here, op, mid, low, high, *halos, base, done), OPERATOR_LIMIT,
    )
    return outs[:4], outs[4]


def bulk_kernel(*refs):
    own_refs, got_ref, out_refs = refs[:4], refs[4], refs[5:]
    for k in range(1, 4):
        for i, m in enumerate(chunks_for(k)):
            out_refs[k - 1][i, 0] = own_refs[m][...]
            out_refs[k - 1][i, 1] = got_ref[m]


def chunks_for(k):
    return [m for m in range(4) if m != k]


def add_kernel(a_ref, b_ref, out_ref):
    out_ref[...] = a_ref[...] + b_ref[...]


def fold_kernel(parts_ref, out_ref):
    total = parts_ref[0]
    for at in range(1, parts_ref.shape[0]):
        total = total + parts_ref[at]
    out_ref[...] = total


def copy_kernel(piece_ref, out_ref):
    for at in range(out_ref.shape[0]):
        out_ref[at] = piece_ref[...]


def lanes(start, size):
    return pl.ds(pl.multiple_of(start, size), size)


def half_of_gram(half, hi_ref, lo_ref, out_ref):
    for m in range(5):
        (i0, j0), (i1, j1) = PAIRS[m], PAIRS[m + 5]
        i = lanes(jnp.where(half == 0, i0, i1) * TILE, TILE)
        j = lanes(jnp.where(half == 0, j0, j1) * TILE, TILE)
        left_hi, right_hi = hi_ref[:, i], hi_ref[:, j]
        left = jnp.concatenate([left_hi, left_hi, lo_ref[:, i]], axis=0)
        right = jnp.concatenate([right_hi, lo_ref[:, j], right_hi], axis=0)
        block = lax.dot_general(left, right, (((0,), (0,)), ((), ())), preferred_element_type=F32)
        out_ref[2 * m] = block[:, :128]
        out_ref[2 * m + 1] = block[:, 128:]


def gram_send_kernel(at_ref, *refs):
    owns, gots, (hi_ref, lo_ref, out_ref) = refs[:4], refs[4:8], refs[8:]
    z, c = at_ref[2], at_ref[3]
    for k in range(4):
        for j in range(2):
            band = lax.rem(z + 4 - k, 4) * 2 + lax.rem(c + j, 2)
            hi, lo = split((owns, gots)[j][k][...])
            hi_ref[:, lanes(band * 128, 128)] = hi
            lo_ref[:, lanes(band * 128, 128)] = lo
    half_of_gram(1 - c, hi_ref, lo_ref, out_ref)


def gram_keep_kernel(at_ref, hi_ref, lo_ref, out_ref):
    half_of_gram(at_ref[3], hi_ref, lo_ref, out_ref)


def times_normed(hi, lo, nh, nl):
    return dot(jnp.concatenate([hi, hi, lo], axis=1), jnp.concatenate([nh, nl, nh], axis=0))


def poly_kernel(order, at_ref, mine_ref, theirs_ref, ph_ref, pl_ref, stretch_ref, gram_ref, nh_ref, nl_ref, poly_ref):
    z, c = at_ref[2], at_ref[3]
    for ky in range(4):
        for kx in range(4):
            rows = slice((ky * 4 + kx) * 160, (ky * 4 + kx + 1) * 160)
            gram_ref[c, rows] = mine_ref[ky * 4 + kx]
            gram_ref[1 - c, rows] = theirs_ref[ky * 4 + kx]

    def packed(n, h):
        at = 2 * (n % 5) + h
        return gram_ref[n // 5, at * 256 : (at + 1) * 256]

    row = lax.broadcasted_iota(jnp.int32, (256, 128), 0)
    col = lax.broadcasted_iota(jnp.int32, (256, 128), 1)
    diag = jnp.zeros((256, 128), F32)
    for n, (i, j) in enumerate(PAIRS):
        if i == j:
            for h in range(2):
                diag += jnp.where(row == col + 128 * h, packed(n, h), 0.0)
    scale = jnp.sum(diag) / VECTORS
    for n, (i, j) in enumerate(PAIRS):
        for h in range(2):
            hi, lo = split(packed(n, h) / scale)
            at = j * TILE + h * 128
            nh_ref[i * TILE : (i + 1) * TILE, at : at + 128] = hi
            nl_ref[i * TILE : (i + 1) * TILE, at : at + 128] = lo
            if i != j:
                nh_ref[at : at + 128, i * TILE : (i + 1) * TILE] = hi.T
                nl_ref[at : at + 128, i * TILE : (i + 1) * TILE] = lo.T
    stretch_ref[...] = jnp.sqrt(jnp.full((8, 128), order, F32) / scale)
    right = []
    for j in range(2):
        band = lanes((2 * z + lax.rem(c + j, 2)) * 128, 128)
        right.append((nh_ref[:, band], nl_ref[:, band]))
    nh = jnp.concatenate([right[0][0], right[1][0]], axis=1)
    nl = jnp.concatenate([right[0][1], right[1][1]], axis=1)
    squared = times_normed(nh_ref[...], nl_ref[...], nh, nl)
    poly_ref[...] = 3.0 * squared - 10.0 * (nh.astype(F32) + nl.astype(F32))
    for q in range(4):
        for j in range(2):
            band = lax.rem(z + q, 4) * 2 + lax.rem(c + j, 2)
            part = poly_ref[pl.ds(pl.multiple_of(band * 128, 128), 128)]
            if q == 0:
                r = lax.broadcasted_iota(jnp.int32, (128, 256), 0)
                l = lax.broadcasted_iota(jnp.int32, (128, 256), 1)
                part = part + jnp.where(l == r + 128 * j, 15.0, 0.0)
            hi, lo = split(part / 8.0)
            at = q * 256 + j * 128
            ph_ref[at : at + 128] = hi
            pl_ref[at : at + 128] = lo


def turned_kernel(*refs):
    owns, got_ref, part_owns, part_gots, bulks = refs[:4], refs[4], refs[5:8], refs[8:11], refs[11:14]
    ph_ref, pl_ref, stretch_ref, mine_ref, theirs_ref = refs[14:]

    def piece(r, q, j):
        k = (4 - q) % 4
        if q == 0:
            return owns[r][...] if j == 0 else got_ref[r]
        if r == 0:
            return (part_owns, part_gots)[j][k - 1][...]
        return bulks[k - 1][chunks_for(k).index((r + k) % 4), j]

    ph, low = ph_ref[...], pl_ref[...]
    for r in range(4):
        highs, lows = [], []
        for q in range(4):
            for j in range(2):
                hi, lo = split(piece(r, q, j))
                highs.append(hi)
                lows.append(lo)
        out = times_normed(jnp.concatenate(highs, axis=1), jnp.concatenate(lows, axis=1), ph, low)
        stretch = stretch_ref[0:1]
        mine_ref[r] = out[:, :128] * stretch
        theirs_ref[r] = out[:, 128:] * stretch


def place_kernel(at_ref, mine_ref, got_ref, out_ref, sem):
    z, c = at_ref[2], at_ref[3]
    copies = []
    for k in range(4):
        chip = lax.rem(z + k, 4)
        copies.append(pltpu.make_async_copy(mine_ref.at[k], out_ref.at[c * 4 + chip], sem.at[k]))
        copies.append(pltpu.make_async_copy(got_ref.at[k], out_ref.at[(1 - c) * 4 + chip], sem.at[4 + k]))
    for copy in copies:
        copy.start()
    for copy in copies:
        copy.wait()


SHIFTS = (2, 1, 3)


def swap_cores(x):
    return lax.ppermute(x, "band", [(i, i ^ 1) for i in range(8)])


def shift_z(x, k):
    return lax.ppermute(x, "band", [(i, (i + 2 * k) % 8) for i in range(8)])


def halos_of(first, last):
    size = lax.axis_size("space")
    up = [(i, (i + 1) % size) for i in range(size)]
    down = [(j, i) for i, j in up]
    return lax.ppermute(last, "space", up), lax.ppermute(first, "space", down)


def steps(vectors, blocks, neighbours):
    elem_dev, basis = blocks.shape[0], blocks.shape[2]
    panel = vectors.shape[1]
    order = float(elem_dev * basis * lax.axis_size("space"))
    space, band = lax.axis_index("space"), lax.axis_index("band")
    x, y, z, c = space & 3, space >> 2, band >> 1, band & 1
    here = jnp.stack([x, y, z, c]).astype(jnp.int32)

    start = vectors.reshape(elem_dev, basis, panel)
    halos = halos_of(start[:REACH], start[-REACH:])
    mid, op = build_operator(neighbours.T, here, blocks, start)
    low, high = first_edges(op, start, halos)
    halos = halos_of(low, high)
    done = second_inner(op, mid, low, high, start)
    own, other = second_edges(here, op, mid, low, high, halos, start, done)

    share = elem_dev * basis // 8
    got = swap_cores(other)
    part_own = {k: shift_z(own[k], k) for k in SHIFTS}
    part_got = {k: shift_z(got[k], k) for k in SHIFTS}
    part_own[0], part_got[0] = own[0], got[0]
    part_own = [part_own[k] for k in range(4)]
    part_got = [part_got[k] for k in range(4)]

    late_own, late_got, part_own, part_got = lax.optimization_barrier((own, got, part_own, part_got))
    bulks = call(bulk_kernel, (shaped(3, 2, share, panel),) * 3, [VMEM_SPEC] * 5, [], (*late_own, late_got), STEP_LIMIT)
    sent = {}
    for k in (1, 3):
        sent[k] = shift_z(bulks[k - 1], k)

    half = shaped(10, 256, 128)
    wide = shaped(share, VECTORS, dtype=BF16)
    hi, lo, send = call(
        gram_send_kernel, (wide, wide, half), [SMEM_SPEC] + [VMEM_SPEC] * 8, [],
        (here, *part_own, *part_got), STEP_LIMIT,
    )
    theirs = swap_cores(send)
    keep = call(gram_keep_kernel, half, [SMEM_SPEC] + [VMEM_SPEC] * 2, [], (here, hi, lo), STEP_LIMIT)
    total = call(add_kernel, half, [VMEM_SPEC] * 2, [], (keep, theirs), STEP_LIMIT)
    pieces = total.reshape(16, 160, panel)
    pieces = lax.all_to_all(pieces, "space", split_axis=0, concat_axis=0, tiled=True)
    piece = call(fold_kernel, shaped(160, panel), [VMEM_SPEC], [], (pieces,), STEP_LIMIT)
    sums = [shift_z(piece, k) for k in SHIFTS]
    piece = piece + sums[0] + (sums[1] + sums[2])
    late, piece = lax.optimization_barrier((bulks[1], piece))
    sent[2] = shift_z(late, 2)
    bulks = [sent[k] for k in (1, 2, 3)]
    copies = call(copy_kernel, shaped(*pieces.shape), [VMEM_SPEC], [], (piece,), STEP_LIMIT)
    mine = lax.all_to_all(copies, "space", split_axis=0, concat_axis=0, tiled=True)
    theirs = swap_cores(mine)

    poly = shaped(VECTORS, TILE, dtype=BF16)
    ph, low, stretch = call(
        functools.partial(poly_kernel, order), (poly, poly, shaped(8, 128)), [SMEM_SPEC] + [VMEM_SPEC] * 2,
        [
            pltpu.VMEM((2, 2560, 128), F32),
            pltpu.VMEM((VECTORS, VECTORS), BF16),
            pltpu.VMEM((VECTORS, VECTORS), BF16),
            pltpu.VMEM((VECTORS, TILE), F32),
        ],
        (here, mine, theirs), TURN_LIMIT,
    )
    quarter = shaped(4, share, panel)
    mine, theirs = call(
        turned_kernel, (quarter, quarter), [VMEM_SPEC] * 17, [],
        (*own, got, *part_own[1:], *part_got[1:], *bulks, ph, low, stretch), TURN_LIMIT,
    )
    theirs = swap_cores(theirs)
    placed = call(
        place_kernel, shaped(8, share, panel), [SMEM_SPEC] + [ANY_SPEC] * 2, [pltpu.SemaphoreType.DMA((8,))],
        (here, mine, theirs), STEP_LIMIT, out_specs=ANY_SPEC,
    )
    return placed.reshape(elem_dev * basis, panel)


def solution(mesh):
    return jax.shard_map(
        steps,
        mesh=mesh,
        in_specs=(P("space", "band"), P("space", None, None, None), P("space", None)),
        out_specs=P("space", "band"),
        check_vma=False,
    )
```

```python
import functools
import jax
import jax.numpy as jnp
from jax import lax
from jax.experimental import pallas as pl
from jax.experimental.pallas import tpu as pltpu
from jax.sharding import PartitionSpec as P


VECTORS = 1024
REACH = 2
TILE = 256
PAIRS = [(0, 0), (1, 1), (0, 1), (0, 2), (0, 3), (2, 2), (3, 3), (1, 2), (1, 3), (2, 3)]
INNER_ROWS = 384
EDGE_ROWS = 128
SPAN = 2 * REACH + 1
TOTAL = 256
RING = 8
BUILD_LIMIT = 26 << 20
STEP_LIMIT = 16 << 20
OPERATOR_LIMIT = 8 << 20
TURN_LIMIT = 32 << 20
F32 = jnp.float32
BF16 = jnp.bfloat16


def split(x):
    hi = x.astype(BF16)
    lo = (x - hi.astype(F32)).astype(BF16)
    return hi, lo


def dot(a, b):
    return jnp.dot(a, b, preferred_element_type=F32)


def spread(wide_ref, slot, value):
    hi, lo = split(value)
    wide_ref[slot, :, 0:128] = hi
    wide_ref[slot, :, 128:256] = lo


def apply_one(op_ref, wide_ref, elem):
    near = wide_ref[pl.ds(elem, SPAN)].reshape(SPAN * 256, 256)
    prod = dot(op_ref[elem], near)
    return (prod[256:, 128:] + prod[256:, :128]) + (prod[:256, 128:] + prod[:256, :128])


def first_of(total, own):
    return (total - 0.5 * own) / 1.5


def second_of(total, own, base):
    return 2.0 * (total - 0.5 * own) / 1.5 - base


def build_kernel(count, near_ref, at_ref, blocks_ref, vectors_ref, step_ref, op_ref, wide_ref, ring_ref, sums_ref, own_ref, sem, own_sem):
    def fetch(n):
        elem = lax.rem(n + REACH, count)
        return pltpu.make_async_copy(blocks_ref.at[elem], ring_ref.at[lax.rem(n, RING)], sem.at[lax.rem(n, RING)])

    first = (at_ref[1] * 4 + at_ref[0]) * count
    load = pltpu.make_async_copy(vectors_ref, own_ref, own_sem)
    load.start()
    for n in range(RING):
        fetch(n).start()
    load.wait()
    for r in range(count):
        spread(wide_ref, REACH + r, own_ref[r])

    def combine(n, u):
        elem = lax.rem(n + REACH, count)
        at = lax.rem(n, RING)
        fetch(n).wait()
        sums_ref[u, 0] = ring_ref[at, 1]
        sums_ref[u, SPAN - 1] = ring_ref[at, 2]
        for o in range(1, SPAN - 1):
            sums_ref[u, o] = jnp.zeros((256, 256), F32)
        for k in (0, 3, 4, 5, 6):
            o = lax.rem(near_ref[k, elem] - first - elem + REACH + 2 * TOTAL, TOTAL)
            sums_ref[u, o] = sums_ref[u, o] + ring_ref[at, k]
        for o in range(SPAN):
            hi, lo = split(sums_ref[u, o])
            op_ref[elem, :256, o * 256 : (o + 1) * 256] = hi
            op_ref[elem, 256:, o * 256 : (o + 1) * 256] = lo
        return elem

    def refill(n):
        @pl.when(n + RING < count)
        def _():
            fetch(n + RING).start()

    def inner(g, _):
        for u in range(2):
            n = 2 * g + u
            elem = combine(n, u)
            refill(n)
            step_ref[elem - REACH] = first_of(apply_one(op_ref, wide_ref, elem), own_ref[elem])
        return 0

    def outer(n, _):
        combine(n, 0)
        return 0

    lax.fori_loop(0, (count - 2 * REACH) // 2, inner, 0)
    lax.fori_loop(count - 2 * REACH, count, outer, 0)


def edges_of(count):
    return [*range(REACH), *range(count - REACH, count)]


def first_edge_kernel(count, op_ref, own_ref, before_ref, after_ref, low_ref, high_ref, wide_ref):
    for r in range(REACH):
        spread(wide_ref, r, before_ref[r])
        spread(wide_ref, REACH + count + r, after_ref[r])
    for r in range(2 * REACH):
        spread(wide_ref, REACH + r, own_ref[r])
        spread(wide_ref, count - REACH + r, own_ref[count - 2 * REACH + r])
    for at, elem in enumerate(edges_of(count)):
        out_ref = low_ref if at < REACH else high_ref
        out_ref[at % REACH] = first_of(apply_one(op_ref, wide_ref, elem), own_ref[elem])


def deal(at_ref, all_ref, own_refs, other_ref):
    z, c = at_ref[2], at_ref[3]
    size = own_refs[0].shape[0]
    for k in range(4):
        chip = lax.rem(z + k, 4)
        own_refs[k][...] = all_ref[pl.ds(pl.multiple_of((c * 4 + chip) * size, 128), size)]
        other_ref[k] = all_ref[pl.ds(pl.multiple_of(((1 - c) * 4 + chip) * size, 128), size)]


def second_edge_kernel(count, at_ref, op_ref, mid_ref, low_ref, high_ref, before_ref, after_ref, base_ref, *refs):
    own_refs, (other_ref, wide_ref, all_ref) = refs[:4], refs[4:]
    for r in range(REACH):
        spread(wide_ref, r, before_ref[r])
        spread(wide_ref, REACH + r, low_ref[r])
        spread(wide_ref, 2 * REACH + r, mid_ref[r])
        spread(wide_ref, count - REACH + r, mid_ref[count - 3 * REACH + r])
        spread(wide_ref, count + r, high_ref[r])
        spread(wide_ref, REACH + count + r, after_ref[r])
    for at, elem in enumerate(edges_of(count)):
        own = (low_ref if at < REACH else high_ref)[at % REACH]
        all_ref[at * 256 : (at + 1) * 256] = second_of(apply_one(op_ref, wide_ref, elem), own, base_ref[elem])
    deal(at_ref, all_ref, own_refs, other_ref)


def inner_kernel(count, at_ref, op_ref, mid_ref, low_ref, high_ref, base_ref, *refs):
    own_refs, (other_ref, wide_ref, all_ref) = refs[:4], refs[4:]
    for r in range(REACH):
        spread(wide_ref, REACH + r, low_ref[r])
        spread(wide_ref, count + r, high_ref[r])
    for r in range(count - 2 * REACH):
        spread(wide_ref, 2 * REACH + r, mid_ref[r])

    def body(g, _):
        for u in range(4):
            at = 4 * g + u
            elem = REACH + at
            rows = pl.ds(pl.multiple_of(at * 256, 256), 256)
            all_ref[rows] = second_of(apply_one(op_ref, wide_ref, elem), mid_ref[at], base_ref[elem])
        return 0

    lax.fori_loop(0, (count - 2 * REACH) // 4, body, 0)
    deal(at_ref, all_ref, own_refs, other_ref)


VMEM_SPEC = pl.BlockSpec(memory_space=pltpu.VMEM)
SMEM_SPEC = pl.BlockSpec(memory_space=pltpu.SMEM)
ANY_SPEC = pl.BlockSpec(memory_space=pl.ANY)
HBM_SPEC = pl.BlockSpec(memory_space=pltpu.HBM)


def shaped(*shape, dtype=F32):
    return jax.ShapeDtypeStruct(shape, dtype)


def call(kernel, outs, specs, scratch, args, limit, **kwargs):
    return pl.pallas_call(
        kernel,
        out_shape=outs,
        in_specs=specs,
        out_specs=kwargs.pop("out_specs", jax.tree.map(lambda _: VMEM_SPEC, outs)),
        scratch_shapes=scratch,
        compiler_params=pltpu.CompilerParams(vmem_limit_bytes=limit),
        **kwargs,
    )(*args)


def wide_scratch(count):
    return pltpu.VMEM((count + 2 * REACH, 256, 256), BF16)


def build_operator(near, here, blocks, own):
    count = own.shape[0]
    return call(
        functools.partial(build_kernel, count),
        (shaped(count - 2 * REACH, 256, 128), shaped(count, 512, SPAN * 256, dtype=BF16)),
        [SMEM_SPEC, SMEM_SPEC, HBM_SPEC, HBM_SPEC],
        [
            wide_scratch(count),
            pltpu.VMEM((RING, 7, 256, 256), F32),
            pltpu.VMEM((2, SPAN, 256, 256), F32),
            pltpu.VMEM(own.shape, F32),
            pltpu.SemaphoreType.DMA((RING,)),
            pltpu.SemaphoreType.DMA,
        ],
        (near, here, blocks, own),
        BUILD_LIMIT,
    )


def first_edges(op, own, halos):
    count = own.shape[0]
    edge = shaped(REACH, 256, 128)
    return call(
        functools.partial(first_edge_kernel, count), (edge, edge), [VMEM_SPEC] * 4,
        [wide_scratch(count)], (op, own, *halos), OPERATOR_LIMIT,
    )


def second_inner(here, op, mid, low, high, base):
    count = base.shape[0]
    outs = call(
        functools.partial(inner_kernel, count), (shaped(INNER_ROWS, 128),) * 4 + (shaped(4, INNER_ROWS, 128),),
        [SMEM_SPEC] + [VMEM_SPEC] * 5,
        [wide_scratch(count), pltpu.VMEM((8 * INNER_ROWS, 128), F32)],
        (here, op, mid, low, high, base), OPERATOR_LIMIT,
    )
    return outs[:4], outs[4]


def second_edges(here, op, mid, low, high, halos, base):
    count = base.shape[0]
    outs = call(
        functools.partial(second_edge_kernel, count), (shaped(EDGE_ROWS, 128),) * 4 + (shaped(4, EDGE_ROWS, 128),),
        [SMEM_SPEC] + [VMEM_SPEC] * 7,
        [wide_scratch(count), pltpu.VMEM((8 * EDGE_ROWS, 128), F32)],
        (here, op, mid, low, high, *halos, base), OPERATOR_LIMIT,
    )
    return outs[:4], outs[4]


def bulk_kernel(*refs):
    inner_refs, edge_refs, inner_got, edge_got, out_refs = refs[:4], refs[4:8], refs[8], refs[9], refs[10:]
    for k in range(1, 4):
        for i, m in enumerate(chunks_for(k)):
            out_refs[k - 1][i, 0, :INNER_ROWS] = inner_refs[m][...]
            out_refs[k - 1][i, 0, INNER_ROWS:] = edge_refs[m][...]
            out_refs[k - 1][i, 1, :INNER_ROWS] = inner_got[m]
            out_refs[k - 1][i, 1, INNER_ROWS:] = edge_got[m]


def chunks_for(k):
    return [m for m in range(4) if m != k]


def add_kernel(a_ref, b_ref, out_ref):
    out_ref[...] = a_ref[...] + b_ref[...]


def fold_kernel(parts_ref, out_ref):
    total = parts_ref[0]
    for at in range(1, parts_ref.shape[0]):
        total = total + parts_ref[at]
    out_ref[...] = total


def copy_kernel(piece_ref, out_ref):
    for at in range(out_ref.shape[0]):
        out_ref[at] = piece_ref[...]


def lanes(start, size):
    return pl.ds(pl.multiple_of(start, size), size)


def places_of(m):
    if m < 2:
        return [(3 * m, 0, 0), (3 * m + 1, 0, 1), (3 * m + 2, 1, 1)]
    return [(6 + 4 * (m - 2) + 2 * a + b, a, b) for a in range(2) for b in range(2)]


def half_of_gram(half, hi_ref, lo_ref, out_ref):
    for m in range(5):
        (i0, j0), (i1, j1) = PAIRS[m], PAIRS[m + 5]
        i = lanes(jnp.where(half == 0, i0, i1) * TILE, TILE)
        j = lanes(jnp.where(half == 0, j0, j1) * TILE, TILE)
        left_hi, right_hi = hi_ref[:, i], hi_ref[:, j]
        left = jnp.concatenate([left_hi, left_hi, lo_ref[:, i]], axis=0)
        right = jnp.concatenate([right_hi, lo_ref[:, j], right_hi], axis=0)
        block = lax.dot_general(left, right, (((0,), (0,)), ((), ())), preferred_element_type=F32)
        for at, a, b in places_of(m):
            out_ref[at] = block[a * 128 : (a + 1) * 128, b * 128 : (b + 1) * 128]


def gram_send_kernel(at_ref, inner_ref, edge_ref, inner_got, edge_got, *refs):
    arrived, (hi_ref, lo_ref, out_ref) = refs[:12], refs[12:]
    z, c = at_ref[2], at_ref[3]
    for k in range(4):
        for j in range(2):
            band = lax.rem(z + 4 - k, 4) * 2 + lax.rem(c + j, 2)
            if k:
                inner, edge = arrived[6 * j + k - 1][...], arrived[6 * j + 3 + k - 1][...]
            elif j:
                inner, edge = inner_got[0], edge_got[0]
            else:
                inner, edge = inner_ref[...], edge_ref[...]
            for value, rows in ((inner, slice(0, INNER_ROWS)), (edge, slice(INNER_ROWS, 512))):
                hi, lo = split(value)
                hi_ref[rows, lanes(band * 128, 128)] = hi
                lo_ref[rows, lanes(band * 128, 128)] = lo
    half_of_gram(1 - c, hi_ref, lo_ref, out_ref)


def gram_keep_kernel(at_ref, hi_ref, lo_ref, out_ref):
    half_of_gram(at_ref[3], hi_ref, lo_ref, out_ref)


def times_normed(hi, lo, nh, nl):
    return dot(jnp.concatenate([hi, hi, lo], axis=1), jnp.concatenate([nh, nl, nh], axis=0))


def poly_kernel(order, at_ref, mine_ref, theirs_ref, ph_ref, pl_ref, stretch_ref, gram_ref, nh_ref, nl_ref, poly_ref):
    z, c = at_ref[2], at_ref[3]
    gram_ref[c] = mine_ref[...]
    gram_ref[1 - c] = theirs_ref[...]
    row = lax.broadcasted_iota(jnp.int32, (128, 128), 0)
    col = lax.broadcasted_iota(jnp.int32, (128, 128), 1)
    diag = jnp.zeros((128, 128), F32)
    for half in range(2):
        for m in range(2):
            for at, a, b in places_of(m):
                if a == b:
                    diag += jnp.where(row == col, gram_ref[half, at], 0.0)
    scale = jnp.sum(diag) / VECTORS
    for n, (i, j) in enumerate(PAIRS):
        for at, a, b in places_of(n % 5):
            hi, lo = split(gram_ref[n // 5, at] / scale)
            p, q = i * TILE + a * 128, j * TILE + b * 128
            nh_ref[p : p + 128, q : q + 128] = hi
            nl_ref[p : p + 128, q : q + 128] = lo
            if p != q:
                nh_ref[q : q + 128, p : p + 128] = hi.T
                nl_ref[q : q + 128, p : p + 128] = lo.T
    stretch_ref[...] = jnp.sqrt(jnp.full((8, 128), order, F32) / scale)
    right = []
    for j in range(2):
        band = lanes((2 * z + lax.rem(c + j, 2)) * 128, 128)
        right.append((nh_ref[:, band], nl_ref[:, band]))
    nh = jnp.concatenate([right[0][0], right[1][0]], axis=1)
    nl = jnp.concatenate([right[0][1], right[1][1]], axis=1)
    squared = times_normed(nh_ref[...], nl_ref[...], nh, nl)
    poly_ref[...] = 3.0 * squared - 10.0 * (nh.astype(F32) + nl.astype(F32))
    for q in range(4):
        for j in range(2):
            band = lax.rem(z + q, 4) * 2 + lax.rem(c + j, 2)
            part = poly_ref[pl.ds(pl.multiple_of(band * 128, 128), 128)]
            if q == 0:
                r = lax.broadcasted_iota(jnp.int32, (128, 256), 0)
                l = lax.broadcasted_iota(jnp.int32, (128, 256), 1)
                part = part + jnp.where(l == r + 128 * j, 15.0, 0.0)
            hi, lo = split(part / 8.0)
            at = q * 256 + j * 128
            ph_ref[at : at + 128] = hi
            pl_ref[at : at + 128] = lo


def turned_kernel(*refs):
    inner_refs, edge_refs, inner_got, edge_got = refs[:4], refs[4:8], refs[8], refs[9]
    arrived, bulks = refs[10:22], refs[22:25]
    ph_ref, pl_ref, stretch_ref, mine_ref, theirs_ref = refs[25:]

    def piece(r, q, j):
        k = (4 - q) % 4
        if q == 0 and j == 0:
            pair = (inner_refs[r][...], edge_refs[r][...])
        elif q == 0:
            pair = (inner_got[r], edge_got[r])
        elif r == 0:
            pair = (arrived[6 * j + k - 1][...], arrived[6 * j + 3 + k - 1][...])
        else:
            return bulks[k - 1][chunks_for(k).index((r + k) % 4), j]
        return jnp.concatenate(pair, axis=0)

    ph, low = ph_ref[...], pl_ref[...]
    for r in range(4):
        highs, lows = [], []
        for q in range(4):
            for j in range(2):
                hi, lo = split(piece(r, q, j))
                highs.append(hi)
                lows.append(lo)
        out = times_normed(jnp.concatenate(highs, axis=1), jnp.concatenate(lows, axis=1), ph, low)
        stretch = stretch_ref[0:1]
        mine_ref[r] = out[:, :128] * stretch
        theirs_ref[r] = out[:, 128:] * stretch


def place_kernel(theirs, at_ref, rows_ref, *refs):
    out_ref, sem = refs[-2:]
    z, c = at_ref[2], at_ref[3]
    half = 1 - c if theirs else c
    copies = []
    for k in range(4):
        chip = lax.rem(z + k, 4)
        inner = pl.ds(pl.multiple_of(512 + (half * 4 + chip) * INNER_ROWS, 128), INNER_ROWS)
        edge = pl.ds(pl.multiple_of(half * 3584 + chip * EDGE_ROWS, 128), EDGE_ROWS)
        copies.append(pltpu.make_async_copy(rows_ref.at[k, pl.ds(0, INNER_ROWS)], out_ref.at[inner], sem.at[k]))
        copies.append(pltpu.make_async_copy(rows_ref.at[k, pl.ds(INNER_ROWS, EDGE_ROWS)], out_ref.at[edge], sem.at[4 + k]))
    for copy in copies:
        copy.start()
    for copy in copies:
        copy.wait()


def place(here, rows, into=None):
    extra = () if into is None else (into,)
    return call(
        functools.partial(place_kernel, into is not None), shaped(4096, 128), [SMEM_SPEC, ANY_SPEC] + [ANY_SPEC] * len(extra),
        [pltpu.SemaphoreType.DMA((8,))], (here, rows, *extra), STEP_LIMIT,
        out_specs=ANY_SPEC, input_output_aliases={2: 0} if extra else {},
    )


SHIFTS = (2, 1, 3)


def swap_cores(x):
    return lax.ppermute(x, "band", [(i, i ^ 1) for i in range(8)])


def shift_z(x, k):
    return lax.ppermute(x, "band", [(i, (i + 2 * k) % 8) for i in range(8)])


def halos_of(first, last):
    size = lax.axis_size("space")
    up = [(i, (i + 1) % size) for i in range(size)]
    down = [(j, i) for i, j in up]
    before = lax.ppermute(last, "space", up)
    return before, lax.ppermute(first, "space", down)


def steps(vectors, blocks, neighbours):
    elem_dev, basis = blocks.shape[0], blocks.shape[2]
    panel = vectors.shape[1]
    order = float(elem_dev * basis * lax.axis_size("space"))
    space, band = lax.axis_index("space"), lax.axis_index("band")
    x, y, z, c = space & 3, space >> 2, band >> 1, band & 1
    here = jnp.stack([x, y, z, c]).astype(jnp.int32)

    start = vectors.reshape(elem_dev, basis, panel)
    halos = halos_of(start[:REACH], start[-REACH:])
    mid, op = build_operator(neighbours.T, here, blocks, start)
    low, high = first_edges(op, start, halos)
    halos = halos_of(low, high)
    inner, other = second_inner(here, op, mid, low, high, start)
    inner_got = swap_cores(other)
    arrived = {}
    for j, rows in enumerate((inner, inner_got)):
        for k in SHIFTS:
            arrived[j, 0, k] = shift_z(rows[k], k)
    edge, other = second_edges(here, op, mid, low, high, halos, start)
    edge_got = swap_cores(other)
    for j, rows in enumerate((edge, edge_got)):
        for k in SHIFTS:
            arrived[j, 1, k] = shift_z(rows[k], k)
    arrived = [arrived[j, e, k] for j in range(2) for e in range(2) for k in (1, 2, 3)]

    share = elem_dev * basis // 8
    held = (*inner, *edge, inner_got, edge_got)
    late, arrived = lax.optimization_barrier((held, arrived))
    bulks = call(bulk_kernel, (shaped(3, 2, share, panel),) * 3, [VMEM_SPEC] * 10, [], late, STEP_LIMIT)
    sent = {}
    for k in (1, 3):
        sent[k] = shift_z(bulks[k - 1], k)

    half = shaped(18, 128, 128)
    wide = shaped(share, VECTORS, dtype=BF16)
    hi, lo, send = call(
        gram_send_kernel, (wide, wide, half), [SMEM_SPEC] + [VMEM_SPEC] * 16, [],
        (here, inner[0], edge[0], inner_got, edge_got, *arrived), STEP_LIMIT,
    )
    theirs = swap_cores(send)
    keep = call(gram_keep_kernel, half, [SMEM_SPEC] + [VMEM_SPEC] * 2, [], (here, hi, lo), STEP_LIMIT)
    total = call(add_kernel, half, [VMEM_SPEC] * 2, [], (keep, theirs), STEP_LIMIT)
    pieces = total.reshape(16, 144, panel)
    pieces = lax.all_to_all(pieces, "space", split_axis=0, concat_axis=0, tiled=True)
    piece = call(fold_kernel, shaped(144, panel), [VMEM_SPEC], [], (pieces,), STEP_LIMIT)
    sums = [shift_z(piece, k) for k in SHIFTS]
    piece = piece + sums[0] + (sums[1] + sums[2])
    late, piece = lax.optimization_barrier((bulks[1], piece))
    sent[2] = shift_z(late, 2)
    bulks = [sent[k] for k in (1, 2, 3)]
    copies = call(copy_kernel, shaped(*pieces.shape), [VMEM_SPEC], [], (piece,), STEP_LIMIT)
    mine = lax.all_to_all(copies, "space", split_axis=0, concat_axis=0, tiled=True)
    mine = mine.reshape(half.shape)
    theirs = swap_cores(mine)

    poly = shaped(VECTORS, TILE, dtype=BF16)
    ph, low, stretch = call(
        functools.partial(poly_kernel, order), (poly, poly, shaped(8, 128)), [SMEM_SPEC] + [VMEM_SPEC] * 2,
        [
            pltpu.VMEM((2, *half.shape), F32),
            pltpu.VMEM((VECTORS, VECTORS), BF16),
            pltpu.VMEM((VECTORS, VECTORS), BF16),
            pltpu.VMEM((VECTORS, TILE), F32),
        ],
        (here, mine, theirs), TURN_LIMIT,
    )
    quarter = shaped(4, share, panel)
    mine, theirs = call(
        turned_kernel, (quarter, quarter), [VMEM_SPEC] * 28, [],
        (*held, *arrived, *bulks, ph, low, stretch), TURN_LIMIT,
    )
    theirs = swap_cores(theirs)
    return place(here, theirs, place(here, mine))


def solution(mesh):
    return jax.shard_map(
        steps,
        mesh=mesh,
        in_specs=(P("space", "band"), P("space", None, None, None), P("space", None)),
        out_specs=P("space", "band"),
        check_vma=False,
    )
```

```python
import functools
import jax
import jax.numpy as jnp
from jax import lax
from jax.experimental import pallas as pl
from jax.experimental.pallas import tpu as pltpu
from jax.sharding import PartitionSpec as P


VECTORS = 1024
REACH = 2
TILE = 256
PAIRS = [(0, 0), (1, 1), (0, 1), (0, 2), (0, 3), (2, 2), (3, 3), (1, 2), (1, 3), (2, 3)]
INNER_ROWS = 384
EDGE_ROWS = 128
SPAN = 2 * REACH + 1
TOTAL = 256
RING = 8
BUILD_LIMIT = 26 << 20
STEP_LIMIT = 16 << 20
OPERATOR_LIMIT = 8 << 20
TURN_LIMIT = 32 << 20
F32 = jnp.float32
BF16 = jnp.bfloat16


def split(x):
    hi = x.astype(BF16)
    lo = (x - hi.astype(F32)).astype(BF16)
    return hi, lo


def dot(a, b):
    return jnp.dot(a, b, preferred_element_type=F32)


def spread(wide_ref, slot, value):
    hi, lo = split(value)
    wide_ref[slot, :, 0:128] = hi
    wide_ref[slot, :, 128:256] = lo


def apply_one(op_ref, wide_ref, elem):
    near = wide_ref[pl.ds(elem, SPAN)].reshape(SPAN * 256, 256)
    prod = dot(op_ref[elem], near)
    return (prod[256:, 128:] + prod[256:, :128]) + (prod[:256, 128:] + prod[:256, :128])


def first_of(total, own):
    return (total - 0.5 * own) / 1.5


def second_of(total, own, base):
    return 2.0 * (total - 0.5 * own) / 1.5 - base


def build_kernel(count, near_ref, at_ref, blocks_ref, vectors_ref, step_ref, op_ref, wide_ref, ring_ref, sums_ref, own_ref, sem, own_sem):
    def fetch(n):
        elem = lax.rem(n + REACH, count)
        return pltpu.make_async_copy(blocks_ref.at[elem], ring_ref.at[lax.rem(n, RING)], sem.at[lax.rem(n, RING)])

    first = (at_ref[1] * 4 + at_ref[0]) * count
    load = pltpu.make_async_copy(vectors_ref, own_ref, own_sem)
    load.start()
    for n in range(RING):
        fetch(n).start()
    load.wait()
    for r in range(count):
        spread(wide_ref, REACH + r, own_ref[r])

    def combine(n, u):
        elem = lax.rem(n + REACH, count)
        at = lax.rem(n, RING)
        fetch(n).wait()
        sums_ref[u, 0] = ring_ref[at, 1]
        sums_ref[u, SPAN - 1] = ring_ref[at, 2]
        for o in range(1, SPAN - 1):
            sums_ref[u, o] = jnp.zeros((256, 256), F32)
        for k in (0, 3, 4, 5, 6):
            o = lax.rem(near_ref[k, elem] - first - elem + REACH + 2 * TOTAL, TOTAL)
            sums_ref[u, o] = sums_ref[u, o] + ring_ref[at, k]
        for o in range(SPAN):
            hi, lo = split(sums_ref[u, o])
            op_ref[elem, :256, o * 256 : (o + 1) * 256] = hi
            op_ref[elem, 256:, o * 256 : (o + 1) * 256] = lo
        return elem

    def refill(n):
        @pl.when(n + RING < count)
        def _():
            fetch(n + RING).start()

    def inner(g, _):
        for u in range(2):
            n = 2 * g + u
            elem = combine(n, u)
            refill(n)
            step_ref[elem - REACH] = first_of(apply_one(op_ref, wide_ref, elem), own_ref[elem])
        return 0

    def outer(n, _):
        combine(n, 0)
        return 0

    lax.fori_loop(0, (count - 2 * REACH) // 2, inner, 0)
    lax.fori_loop(count - 2 * REACH, count, outer, 0)


def edges_of(count):
    return [*range(REACH), *range(count - REACH, count)]


def first_edge_kernel(count, op_ref, own_ref, before_ref, after_ref, low_ref, high_ref, wide_ref):
    for r in range(REACH):
        spread(wide_ref, r, before_ref[r])
        spread(wide_ref, REACH + count + r, after_ref[r])
    for r in range(2 * REACH):
        spread(wide_ref, REACH + r, own_ref[r])
        spread(wide_ref, count - REACH + r, own_ref[count - 2 * REACH + r])
    for at, elem in enumerate(edges_of(count)):
        out_ref = low_ref if at < REACH else high_ref
        out_ref[at % REACH] = first_of(apply_one(op_ref, wide_ref, elem), own_ref[elem])


def deal(at_ref, all_ref, own_refs, other_ref):
    z, c = at_ref[2], at_ref[3]
    size = own_refs[0].shape[0]
    for k in range(4):
        chip = lax.rem(z + k, 4)
        own_refs[k][...] = all_ref[pl.ds(pl.multiple_of((c * 4 + chip) * size, 128), size)]
        other_ref[k] = all_ref[pl.ds(pl.multiple_of(((1 - c) * 4 + chip) * size, 128), size)]


def second_edge_kernel(count, at_ref, op_ref, mid_ref, low_ref, high_ref, before_ref, after_ref, base_ref, *refs):
    own_refs, (other_ref, wide_ref, all_ref) = refs[:4], refs[4:]
    for r in range(REACH):
        spread(wide_ref, r, before_ref[r])
        spread(wide_ref, REACH + r, low_ref[r])
        spread(wide_ref, 2 * REACH + r, mid_ref[r])
        spread(wide_ref, count - REACH + r, mid_ref[count - 3 * REACH + r])
        spread(wide_ref, count + r, high_ref[r])
        spread(wide_ref, REACH + count + r, after_ref[r])
    for at, elem in enumerate(edges_of(count)):
        own = (low_ref if at < REACH else high_ref)[at % REACH]
        all_ref[at * 256 : (at + 1) * 256] = second_of(apply_one(op_ref, wide_ref, elem), own, base_ref[elem])
    deal(at_ref, all_ref, own_refs, other_ref)


def inner_kernel(count, at_ref, op_ref, mid_ref, low_ref, high_ref, base_ref, *refs):
    own_refs, (other_ref, wide_ref, all_ref) = refs[:4], refs[4:]
    for r in range(REACH):
        spread(wide_ref, REACH + r, low_ref[r])
        spread(wide_ref, count + r, high_ref[r])
    for r in range(count - 2 * REACH):
        spread(wide_ref, 2 * REACH + r, mid_ref[r])

    def body(g, _):
        for u in range(4):
            at = 4 * g + u
            elem = REACH + at
            rows = pl.ds(pl.multiple_of(at * 256, 256), 256)
            all_ref[rows] = second_of(apply_one(op_ref, wide_ref, elem), mid_ref[at], base_ref[elem])
        return 0

    lax.fori_loop(0, (count - 2 * REACH) // 4, body, 0)
    deal(at_ref, all_ref, own_refs, other_ref)


VMEM_SPEC = pl.BlockSpec(memory_space=pltpu.VMEM)
SMEM_SPEC = pl.BlockSpec(memory_space=pltpu.SMEM)
ANY_SPEC = pl.BlockSpec(memory_space=pl.ANY)
HBM_SPEC = pl.BlockSpec(memory_space=pltpu.HBM)


def shaped(*shape, dtype=F32):
    return jax.ShapeDtypeStruct(shape, dtype)


def call(kernel, outs, specs, scratch, args, limit, **kwargs):
    return pl.pallas_call(
        kernel,
        out_shape=outs,
        in_specs=specs,
        out_specs=kwargs.pop("out_specs", jax.tree.map(lambda _: VMEM_SPEC, outs)),
        scratch_shapes=scratch,
        compiler_params=pltpu.CompilerParams(vmem_limit_bytes=limit),
        **kwargs,
    )(*args)


def wide_scratch(count):
    return pltpu.VMEM((count + 2 * REACH, 256, 256), BF16)


def build_operator(near, here, blocks, own):
    count = own.shape[0]
    return call(
        functools.partial(build_kernel, count),
        (shaped(count - 2 * REACH, 256, 128), shaped(count, 512, SPAN * 256, dtype=BF16)),
        [SMEM_SPEC, SMEM_SPEC, HBM_SPEC, HBM_SPEC],
        [
            wide_scratch(count),
            pltpu.VMEM((RING, 7, 256, 256), F32),
            pltpu.VMEM((2, SPAN, 256, 256), F32),
            pltpu.VMEM(own.shape, F32),
            pltpu.SemaphoreType.DMA((RING,)),
            pltpu.SemaphoreType.DMA,
        ],
        (near, here, blocks, own),
        BUILD_LIMIT,
    )


def first_edges(op, own, halos):
    count = own.shape[0]
    edge = shaped(REACH, 256, 128)
    return call(
        functools.partial(first_edge_kernel, count), (edge, edge), [VMEM_SPEC] * 4,
        [wide_scratch(count)], (op, own, *halos), OPERATOR_LIMIT,
    )


def second_inner(here, op, mid, low, high, base):
    count = base.shape[0]
    outs = call(
        functools.partial(inner_kernel, count), (shaped(INNER_ROWS, 128),) * 4 + (shaped(4, INNER_ROWS, 128),),
        [SMEM_SPEC] + [VMEM_SPEC] * 5,
        [wide_scratch(count), pltpu.VMEM((8 * INNER_ROWS, 128), F32)],
        (here, op, mid, low, high, base), OPERATOR_LIMIT,
    )
    return outs[:4], outs[4]


def second_edges(here, op, mid, low, high, halos, base):
    count = base.shape[0]
    outs = call(
        functools.partial(second_edge_kernel, count), (shaped(EDGE_ROWS, 128),) * 4 + (shaped(4, EDGE_ROWS, 128),),
        [SMEM_SPEC] + [VMEM_SPEC] * 7,
        [wide_scratch(count), pltpu.VMEM((8 * EDGE_ROWS, 128), F32)],
        (here, op, mid, low, high, *halos, base), OPERATOR_LIMIT,
    )
    return outs[:4], outs[4]


def bulk_kernel(*refs):
    inner_refs, edge_refs, inner_got, edge_got, out_refs = refs[:4], refs[4:8], refs[8], refs[9], refs[10:]
    for k, out_ref in zip((1, 3), out_refs):
        for i, m in enumerate(chunks_for(k)):
            out_ref[i, 0, :INNER_ROWS] = inner_refs[m][...]
            out_ref[i, 0, INNER_ROWS:] = edge_refs[m][...]
            out_ref[i, 1, :INNER_ROWS] = inner_got[m]
            out_ref[i, 1, INNER_ROWS:] = edge_got[m]


def relay_kernel(below_ref, above_ref, below_inner, below_edge, above_inner, above_edge, up_ref, down_ref):
    up_ref[0] = below_ref[chunks_for(1).index(3), 0]
    up_ref[1] = below_ref[chunks_for(1).index(0), 0]
    up_ref[2, :INNER_ROWS] = below_inner[...]
    up_ref[2, INNER_ROWS:] = below_edge[...]
    down_ref[0, :INNER_ROWS] = above_inner[...]
    down_ref[0, INNER_ROWS:] = above_edge[...]
    down_ref[1] = above_ref[chunks_for(3).index(0), 1]
    down_ref[2] = above_ref[chunks_for(3).index(1), 1]


def chunks_for(k):
    return [m for m in range(4) if m != k]


def add_kernel(a_ref, b_ref, out_ref):
    out_ref[...] = a_ref[...] + b_ref[...]


def fold_kernel(parts_ref, out_ref):
    total = parts_ref[0]
    for at in range(1, parts_ref.shape[0]):
        total = total + parts_ref[at]
    out_ref[...] = total


def copy_kernel(piece_ref, out_ref):
    for at in range(out_ref.shape[0]):
        out_ref[at] = piece_ref[...]


def lanes(start, size):
    return pl.ds(pl.multiple_of(start, size), size)


def places_of(m):
    if m < 2:
        return [(3 * m, 0, 0), (3 * m + 1, 0, 1), (3 * m + 2, 1, 1)]
    return [(6 + 4 * (m - 2) + 2 * a + b, a, b) for a in range(2) for b in range(2)]


def half_of_gram(half, hi_ref, lo_ref, out_ref):
    for m in range(5):
        (i0, j0), (i1, j1) = PAIRS[m], PAIRS[m + 5]
        i = lanes(jnp.where(half == 0, i0, i1) * TILE, TILE)
        j = lanes(jnp.where(half == 0, j0, j1) * TILE, TILE)
        left_hi, right_hi = hi_ref[:, i], hi_ref[:, j]
        left = jnp.concatenate([left_hi, left_hi, lo_ref[:, i]], axis=0)
        right = jnp.concatenate([right_hi, lo_ref[:, j], right_hi], axis=0)
        block = lax.dot_general(left, right, (((0,), (0,)), ((), ())), preferred_element_type=F32)
        for at, a, b in places_of(m):
            out_ref[at] = block[a * 128 : (a + 1) * 128, b * 128 : (b + 1) * 128]


def gram_send_kernel(at_ref, inner_ref, edge_ref, inner_got, edge_got, *refs):
    arrived, (hi_ref, lo_ref, out_ref) = refs[:12], refs[12:]
    z, c = at_ref[2], at_ref[3]
    for k in range(4):
        for j in range(2):
            band = lax.rem(z + 4 - k, 4) * 2 + lax.rem(c + j, 2)
            if k:
                inner, edge = arrived[6 * j + k - 1][...], arrived[6 * j + 3 + k - 1][...]
            elif j:
                inner, edge = inner_got[0], edge_got[0]
            else:
                inner, edge = inner_ref[...], edge_ref[...]
            for value, rows in ((inner, slice(0, INNER_ROWS)), (edge, slice(INNER_ROWS, 512))):
                hi, lo = split(value)
                hi_ref[rows, lanes(band * 128, 128)] = hi
                lo_ref[rows, lanes(band * 128, 128)] = lo
    half_of_gram(1 - c, hi_ref, lo_ref, out_ref)


def gram_keep_kernel(at_ref, hi_ref, lo_ref, out_ref):
    half_of_gram(at_ref[3], hi_ref, lo_ref, out_ref)


def times_normed(hi, lo, nh, nl):
    return dot(jnp.concatenate([hi, hi, lo], axis=1), jnp.concatenate([nh, nl, nh], axis=0))


def poly_kernel(order, at_ref, mine_ref, theirs_ref, ph_ref, pl_ref, stretch_ref, gram_ref, nh_ref, nl_ref, poly_ref):
    z, c = at_ref[2], at_ref[3]
    gram_ref[c] = mine_ref[...]
    gram_ref[1 - c] = theirs_ref[...]
    row = lax.broadcasted_iota(jnp.int32, (128, 128), 0)
    col = lax.broadcasted_iota(jnp.int32, (128, 128), 1)
    diag = jnp.zeros((128, 128), F32)
    for half in range(2):
        for m in range(2):
            for at, a, b in places_of(m):
                if a == b:
                    diag += jnp.where(row == col, gram_ref[half, at], 0.0)
    scale = jnp.sum(diag) / VECTORS
    for n, (i, j) in enumerate(PAIRS):
        for at, a, b in places_of(n % 5):
            hi, lo = split(gram_ref[n // 5, at] / scale)
            p, q = i * TILE + a * 128, j * TILE + b * 128
            nh_ref[p : p + 128, q : q + 128] = hi
            nl_ref[p : p + 128, q : q + 128] = lo
            if p != q:
                nh_ref[q : q + 128, p : p + 128] = hi.T
                nl_ref[q : q + 128, p : p + 128] = lo.T
    stretch_ref[...] = jnp.sqrt(jnp.full((8, 128), order, F32) / scale)
    right = []
    for j in range(2):
        band = lanes((2 * z + lax.rem(c + j, 2)) * 128, 128)
        right.append((nh_ref[:, band], nl_ref[:, band]))
    nh = jnp.concatenate([right[0][0], right[1][0]], axis=1)
    nl = jnp.concatenate([right[0][1], right[1][1]], axis=1)
    squared = times_normed(nh_ref[...], nl_ref[...], nh, nl)
    poly_ref[...] = 3.0 * squared - 10.0 * (nh.astype(F32) + nl.astype(F32))
    for q in range(4):
        for j in range(2):
            band = lax.rem(z + q, 4) * 2 + lax.rem(c + j, 2)
            part = poly_ref[pl.ds(pl.multiple_of(band * 128, 128), 128)]
            if q == 0:
                r = lax.broadcasted_iota(jnp.int32, (128, 256), 0)
                l = lax.broadcasted_iota(jnp.int32, (128, 256), 1)
                part = part + jnp.where(l == r + 128 * j, 15.0, 0.0)
            hi, lo = split(part / 8.0)
            at = q * 256 + j * 128
            ph_ref[at : at + 128] = hi
            pl_ref[at : at + 128] = lo


def turned_kernel(*refs):
    inner_refs, edge_refs, inner_got, edge_got = refs[:4], refs[4:8], refs[8], refs[9]
    arrived, bulks = refs[10:22], refs[22:26]
    ph_ref, pl_ref, stretch_ref, mine_ref, theirs_ref = refs[26:]

    def piece(r, q, j):
        k = (4 - q) % 4
        if q == 0 and j == 0:
            pair = (inner_refs[r][...], edge_refs[r][...])
        elif q == 0:
            pair = (inner_got[r], edge_got[r])
        elif r == 0:
            pair = (arrived[6 * j + k - 1][...], arrived[6 * j + 3 + k - 1][...])
        elif q == 2:
            return bulks[2 + j][r - 1]
        else:
            return bulks[k // 2][chunks_for(k).index((r + k) % 4), j]
        return jnp.concatenate(pair, axis=0)

    ph, low = ph_ref[...], pl_ref[...]
    for r in range(4):
        highs, lows = [], []
        for q in range(4):
            for j in range(2):
                hi, lo = split(piece(r, q, j))
                highs.append(hi)
                lows.append(lo)
        out = times_normed(jnp.concatenate(highs, axis=1), jnp.concatenate(lows, axis=1), ph, low)
        stretch = stretch_ref[0:1]
        mine_ref[r] = out[:, :128] * stretch
        theirs_ref[r] = out[:, 128:] * stretch


def place_kernel(theirs, at_ref, rows_ref, *refs):
    out_ref, sem = refs[-2:]
    z, c = at_ref[2], at_ref[3]
    half = 1 - c if theirs else c
    copies = []
    for k in range(4):
        chip = lax.rem(z + k, 4)
        inner = pl.ds(pl.multiple_of(512 + (half * 4 + chip) * INNER_ROWS, 128), INNER_ROWS)
        edge = pl.ds(pl.multiple_of(half * 3584 + chip * EDGE_ROWS, 128), EDGE_ROWS)
        copies.append(pltpu.make_async_copy(rows_ref.at[k, pl.ds(0, INNER_ROWS)], out_ref.at[inner], sem.at[k]))
        copies.append(pltpu.make_async_copy(rows_ref.at[k, pl.ds(INNER_ROWS, EDGE_ROWS)], out_ref.at[edge], sem.at[4 + k]))
    for copy in copies:
        copy.start()
    for copy in copies:
        copy.wait()


def place(here, rows, into=None):
    extra = () if into is None else (into,)
    return call(
        functools.partial(place_kernel, into is not None), shaped(4096, 128), [SMEM_SPEC, ANY_SPEC] + [ANY_SPEC] * len(extra),
        [pltpu.SemaphoreType.DMA((8,))], (here, rows, *extra), STEP_LIMIT,
        out_specs=ANY_SPEC, input_output_aliases={2: 0} if extra else {},
    )


SHIFTS = (2, 1, 3)


def swap_cores(x):
    return lax.ppermute(x, "band", [(i, i ^ 1) for i in range(8)])


def shift_z(x, k):
    return lax.ppermute(x, "band", [(i, (i + 2 * k) % 8) for i in range(8)])


def halos_of(first, last):
    size = lax.axis_size("space")
    up = [(i, (i + 1) % size) for i in range(size)]
    down = [(j, i) for i, j in up]
    before = lax.ppermute(last, "space", up)
    return before, lax.ppermute(first, "space", down)


def steps(vectors, blocks, neighbours):
    elem_dev, basis = blocks.shape[0], blocks.shape[2]
    panel = vectors.shape[1]
    order = float(elem_dev * basis * lax.axis_size("space"))
    space, band = lax.axis_index("space"), lax.axis_index("band")
    x, y, z, c = space & 3, space >> 2, band >> 1, band & 1
    here = jnp.stack([x, y, z, c]).astype(jnp.int32)

    start = vectors.reshape(elem_dev, basis, panel)
    halos = halos_of(start[:REACH], start[-REACH:])
    mid, op = build_operator(neighbours.T, here, blocks, start)
    low, high = first_edges(op, start, halos)
    halos = halos_of(low, high)
    inner, other = second_inner(here, op, mid, low, high, start)
    inner_got = swap_cores(other)
    arrived = {}
    for j, rows in enumerate((inner, inner_got)):
        for k in SHIFTS:
            arrived[j, 0, k] = shift_z(rows[k], k)
    edge, other = second_edges(here, op, mid, low, high, halos, start)
    edge_got = swap_cores(other)
    for j, rows in enumerate((edge, edge_got)):
        for k in SHIFTS:
            arrived[j, 1, k] = shift_z(rows[k], k)
    arrived = [arrived[j, e, k] for j in range(2) for e in range(2) for k in (1, 2, 3)]

    share = elem_dev * basis // 8
    held = (*inner, *edge, inner_got, edge_got)
    late, arrived = lax.optimization_barrier((held, arrived))
    bulks = call(bulk_kernel, (shaped(3, 2, share, panel),) * 2, [VMEM_SPEC] * 10, [], late, STEP_LIMIT)
    sent = []
    for k, bulk in zip((1, 3), bulks):
        sent.append(shift_z(bulk, k))

    half = shaped(18, 128, 128)
    wide = shaped(share, VECTORS, dtype=BF16)
    hi, lo, send = call(
        gram_send_kernel, (wide, wide, half), [SMEM_SPEC] + [VMEM_SPEC] * 16, [],
        (here, inner[0], edge[0], inner_got, edge_got, *arrived), STEP_LIMIT,
    )
    theirs = swap_cores(send)
    keep = call(gram_keep_kernel, half, [SMEM_SPEC] + [VMEM_SPEC] * 2, [], (here, hi, lo), STEP_LIMIT)
    total = call(add_kernel, half, [VMEM_SPEC] * 2, [], (keep, theirs), STEP_LIMIT)
    pieces = total.reshape(16, 144, panel)
    pieces = lax.all_to_all(pieces, "space", split_axis=0, concat_axis=0, tiled=True)
    piece = call(fold_kernel, shaped(144, panel), [VMEM_SPEC], [], (pieces,), STEP_LIMIT)
    sums = [shift_z(piece, k) for k in SHIFTS]
    piece = piece + sums[0] + (sums[1] + sums[2])
    below, above, piece = lax.optimization_barrier((*sent, piece))
    relays = call(
        relay_kernel, (shaped(3, share, panel),) * 2, [VMEM_SPEC] * 6, [],
        (below, above, arrived[0], arrived[3], arrived[8], arrived[11]), STEP_LIMIT,
    )
    bulks = [below, above]
    for k, relay in zip((1, 3), relays):
        bulks.append(shift_z(relay, k))
    copies = call(copy_kernel, shaped(*pieces.shape), [VMEM_SPEC], [], (piece,), STEP_LIMIT)
    mine = lax.all_to_all(copies, "space", split_axis=0, concat_axis=0, tiled=True)
    mine = mine.reshape(half.shape)
    theirs = swap_cores(mine)

    poly = shaped(VECTORS, TILE, dtype=BF16)
    ph, low, stretch = call(
        functools.partial(poly_kernel, order), (poly, poly, shaped(8, 128)), [SMEM_SPEC] + [VMEM_SPEC] * 2,
        [
            pltpu.VMEM((2, *half.shape), F32),
            pltpu.VMEM((VECTORS, VECTORS), BF16),
            pltpu.VMEM((VECTORS, VECTORS), BF16),
            pltpu.VMEM((VECTORS, TILE), F32),
        ],
        (here, mine, theirs), TURN_LIMIT,
    )
    quarter = shaped(4, share, panel)
    mine, theirs = call(
        turned_kernel, (quarter, quarter), [VMEM_SPEC] * 29, [],
        (*held, *arrived, *bulks, ph, low, stretch), TURN_LIMIT,
    )
    theirs = swap_cores(theirs)
    return place(here, theirs, place(here, mine))


def solution(mesh):
    return jax.shard_map(
        steps,
        mesh=mesh,
        in_specs=(P("space", "band"), P("space", None, None, None), P("space", None)),
        out_specs=P("space", "band"),
        check_vma=False,
    )
```

```python
import functools
import jax
import jax.numpy as jnp
from jax import lax
from jax.experimental import pallas as pl
from jax.experimental.pallas import tpu as pltpu
from jax.sharding import PartitionSpec as P


VECTORS = 1024
REACH = 2
TILE = 256
PAIRS = [(0, 0), (1, 1), (0, 1), (0, 2), (0, 3), (2, 2), (3, 3), (1, 2), (1, 3), (2, 3)]
INNER_ROWS = 384
EDGE_ROWS = 128
SPAN = 2 * REACH + 1
TOTAL = 256
RING = 8
BUILD_LIMIT = 30 << 20
STEP_LIMIT = 16 << 20
OPERATOR_LIMIT = 8 << 20
TURN_LIMIT = 32 << 20
F32 = jnp.float32
BF16 = jnp.bfloat16


def split(x):
    hi = x.astype(BF16)
    lo = (x - hi.astype(F32)).astype(BF16)
    return hi, lo


def dot(a, b):
    return jnp.dot(a, b, preferred_element_type=F32)


def spread(wide_ref, slot, value):
    hi, lo = split(value)
    wide_ref[slot, :, 0:128] = hi
    wide_ref[slot, :, 128:256] = lo


def apply_one(op_ref, wide_ref, elem):
    return apply_left(op_ref[elem], wide_ref, elem)


def apply_left(left, wide_ref, elem):
    near = wide_ref[pl.ds(elem, SPAN)].reshape(SPAN * 256, 256)
    prod = dot(left, near)
    return (prod[256:, 128:] + prod[256:, :128]) + (prod[:256, 128:] + prod[:256, :128])


def first_of(total, own):
    return (total - 0.5 * own) / 1.5


def second_of(total, own, base):
    return 2.0 * (total - 0.5 * own) / 1.5 - base


def build_kernel(count, near_ref, at_ref, blocks_ref, vectors_ref, step_ref, op_ref, wide_ref, ring_ref, own_ref, sums_a, sums_b, left_a, left_b, sem, own_sem):
    def fetch(n):
        elem = lax.rem(n + REACH, count)
        return pltpu.make_async_copy(blocks_ref.at[elem], ring_ref.at[lax.rem(n, RING)], sem.at[lax.rem(n, RING)])

    first = (at_ref[1] * 4 + at_ref[0]) * count
    load = pltpu.make_async_copy(vectors_ref, own_ref, own_sem)
    load.start()
    for n in range(RING):
        fetch(n).start()
    load.wait()
    for r in range(count):
        spread(wide_ref, REACH + r, own_ref[r])

    def combine(n, sums_ref, left_ref):
        elem = lax.rem(n + REACH, count)
        at = lax.rem(n, RING)
        sums_ref[0] = ring_ref[at, 1]
        sums_ref[SPAN - 1] = ring_ref[at, 2]
        for o in range(1, SPAN - 1):
            sums_ref[o] = jnp.zeros((256, 256), F32)
        for k in (0, 3, 4, 5, 6):
            o = lax.rem(near_ref[k, elem] - first - elem + REACH + 2 * TOTAL, TOTAL)
            sums_ref[o] = sums_ref[o] + ring_ref[at, k]
        for o in range(SPAN):
            hi, lo = split(sums_ref[o])
            cols = slice(o * 256, (o + 1) * 256)
            op_ref[elem, :256, cols] = hi
            op_ref[elem, 256:, cols] = lo
            left_ref[:256, cols] = hi
            left_ref[256:, cols] = lo

    def refill(n):
        @pl.when(n + RING < count)
        def _():
            fetch(n + RING).start()

    def step(n, left_ref):
        total = apply_left(left_ref[...], wide_ref, n + REACH)
        step_ref[n] = first_of(total, own_ref[n + REACH])

    def inner(g, _):
        n = 2 * g
        fetch(n + 1).wait()
        fetch(n + 2).wait()
        step(n, left_a)
        combine(n + 1, sums_b, left_b)
        step(n + 1, left_b)
        combine(n + 2, sums_a, left_a)
        refill(n + 1)
        refill(n + 2)
        return 0

    def outer(n, _):
        fetch(n).wait()
        combine(n, sums_a, left_a)
        return 0

    fetch(0).wait()
    combine(0, sums_a, left_a)
    refill(0)
    lax.fori_loop(0, (count - 2 * REACH) // 2, inner, 0)
    lax.fori_loop(count - 2 * REACH + 1, count, outer, 0)


def edges_of(count):
    return [*range(REACH), *range(count - REACH, count)]


def first_edge_kernel(count, op_ref, own_ref, before_ref, after_ref, low_ref, high_ref, wide_ref):
    for r in range(REACH):
        spread(wide_ref, r, before_ref[r])
        spread(wide_ref, REACH + count + r, after_ref[r])
    for r in range(2 * REACH):
        spread(wide_ref, REACH + r, own_ref[r])
        spread(wide_ref, count - REACH + r, own_ref[count - 2 * REACH + r])
    for at, elem in enumerate(edges_of(count)):
        out_ref = low_ref if at < REACH else high_ref
        out_ref[at % REACH] = first_of(apply_one(op_ref, wide_ref, elem), own_ref[elem])


def deal(at_ref, all_ref, own_refs, other_ref):
    z, c = at_ref[2], at_ref[3]
    size = own_refs[0].shape[0]
    for k in range(4):
        chip = lax.rem(z + k, 4)
        own_refs[k][...] = all_ref[pl.ds(pl.multiple_of((c * 4 + chip) * size, 128), size)]
        other_ref[k] = all_ref[pl.ds(pl.multiple_of(((1 - c) * 4 + chip) * size, 128), size)]


def second_edge_kernel(count, at_ref, op_ref, mid_ref, low_ref, high_ref, before_ref, after_ref, base_ref, *refs):
    own_refs, (other_ref, wide_ref, all_ref) = refs[:4], refs[4:]
    for r in range(REACH):
        spread(wide_ref, r, before_ref[r])
        spread(wide_ref, REACH + r, low_ref[r])
        spread(wide_ref, 2 * REACH + r, mid_ref[r])
        spread(wide_ref, count - REACH + r, mid_ref[count - 3 * REACH + r])
        spread(wide_ref, count + r, high_ref[r])
        spread(wide_ref, REACH + count + r, after_ref[r])
    for at, elem in enumerate(edges_of(count)):
        own = (low_ref if at < REACH else high_ref)[at % REACH]
        all_ref[at * 256 : (at + 1) * 256] = second_of(apply_one(op_ref, wide_ref, elem), own, base_ref[elem])
    deal(at_ref, all_ref, own_refs, other_ref)


def inner_kernel(count, at_ref, op_ref, mid_ref, low_ref, high_ref, base_ref, *refs):
    own_refs, (other_ref, wide_ref, all_ref) = refs[:4], refs[4:]
    for r in range(REACH):
        spread(wide_ref, REACH + r, low_ref[r])
        spread(wide_ref, count + r, high_ref[r])
    for r in range(count - 2 * REACH):
        spread(wide_ref, 2 * REACH + r, mid_ref[r])

    def body(g, _):
        for u in range(4):
            at = 4 * g + u
            elem = REACH + at
            rows = pl.ds(pl.multiple_of(at * 256, 256), 256)
            all_ref[rows] = second_of(apply_one(op_ref, wide_ref, elem), mid_ref[at], base_ref[elem])
        return 0

    lax.fori_loop(0, (count - 2 * REACH) // 4, body, 0)
    deal(at_ref, all_ref, own_refs, other_ref)


VMEM_SPEC = pl.BlockSpec(memory_space=pltpu.VMEM)
SMEM_SPEC = pl.BlockSpec(memory_space=pltpu.SMEM)
ANY_SPEC = pl.BlockSpec(memory_space=pl.ANY)
HBM_SPEC = pl.BlockSpec(memory_space=pltpu.HBM)


def shaped(*shape, dtype=F32):
    return jax.ShapeDtypeStruct(shape, dtype)


def call(kernel, outs, specs, scratch, args, limit, **kwargs):
    return pl.pallas_call(
        kernel,
        out_shape=outs,
        in_specs=specs,
        out_specs=kwargs.pop("out_specs", jax.tree.map(lambda _: VMEM_SPEC, outs)),
        scratch_shapes=scratch,
        compiler_params=pltpu.CompilerParams(vmem_limit_bytes=limit),
        **kwargs,
    )(*args)


def wide_scratch(count):
    return pltpu.VMEM((count + 2 * REACH, 256, 256), BF16)


def build_operator(near, here, blocks, own):
    count = own.shape[0]
    return call(
        functools.partial(build_kernel, count),
        (shaped(count - 2 * REACH, 256, 128), shaped(count, 512, SPAN * 256, dtype=BF16)),
        [SMEM_SPEC, SMEM_SPEC, HBM_SPEC, HBM_SPEC],
        [
            wide_scratch(count),
            pltpu.VMEM((RING, 7, 256, 256), F32),
            pltpu.VMEM(own.shape, F32),
            pltpu.VMEM((SPAN, 256, 256), F32),
            pltpu.VMEM((SPAN, 256, 256), F32),
            pltpu.VMEM((512, SPAN * 256), BF16),
            pltpu.VMEM((512, SPAN * 256), BF16),
            pltpu.SemaphoreType.DMA((RING,)),
            pltpu.SemaphoreType.DMA,
        ],
        (near, here, blocks, own),
        BUILD_LIMIT,
    )


def first_edges(op, own, halos):
    count = own.shape[0]
    edge = shaped(REACH, 256, 128)
    return call(
        functools.partial(first_edge_kernel, count), (edge, edge), [VMEM_SPEC] * 4,
        [wide_scratch(count)], (op, own, *halos), OPERATOR_LIMIT,
    )


def second_inner(here, op, mid, low, high, base):
    count = base.shape[0]
    outs = call(
        functools.partial(inner_kernel, count), (shaped(INNER_ROWS, 128),) * 4 + (shaped(4, INNER_ROWS, 128),),
        [SMEM_SPEC] + [VMEM_SPEC] * 5,
        [wide_scratch(count), pltpu.VMEM((8 * INNER_ROWS, 128), F32)],
        (here, op, mid, low, high, base), OPERATOR_LIMIT,
    )
    return outs[:4], outs[4]


def second_edges(here, op, mid, low, high, halos, base):
    count = base.shape[0]
    outs = call(
        functools.partial(second_edge_kernel, count), (shaped(EDGE_ROWS, 128),) * 4 + (shaped(4, EDGE_ROWS, 128),),
        [SMEM_SPEC] + [VMEM_SPEC] * 7,
        [wide_scratch(count), pltpu.VMEM((8 * EDGE_ROWS, 128), F32)],
        (here, op, mid, low, high, *halos, base), OPERATOR_LIMIT,
    )
    return outs[:4], outs[4]


def bulk_kernel(*refs):
    inner_refs, edge_refs, inner_got, edge_got, out_refs = refs[:4], refs[4:8], refs[8], refs[9], refs[10:]
    for k, out_ref in zip((1, 3), out_refs):
        for i, m in enumerate(relayed_for(k)):
            out_ref[i, 0, :INNER_ROWS] = inner_refs[m][...]
            out_ref[i, 0, INNER_ROWS:] = edge_refs[m][...]
            out_ref[i, 1, :INNER_ROWS] = inner_got[m]
            out_ref[i, 1, INNER_ROWS:] = edge_got[m]


def relay_kernel(below_ref, above_ref, below_inner, below_edge, above_inner, above_edge, inner_ref, edge_ref, inner_got, edge_got, up_ref, down_ref):
    for out_ref in (up_ref, down_ref):
        out_ref[3, :INNER_ROWS] = inner_ref[...]
        out_ref[3, INNER_ROWS:] = edge_ref[...]
        out_ref[4, :INNER_ROWS] = inner_got[2]
        out_ref[4, INNER_ROWS:] = edge_got[2]
    up_ref[0] = below_ref[relayed_for(1).index(3), 0]
    up_ref[1] = below_ref[relayed_for(1).index(0), 0]
    up_ref[2, :INNER_ROWS] = below_inner[...]
    up_ref[2, INNER_ROWS:] = below_edge[...]
    down_ref[0, :INNER_ROWS] = above_inner[...]
    down_ref[0, INNER_ROWS:] = above_edge[...]
    down_ref[1] = above_ref[relayed_for(3).index(0), 1]
    down_ref[2] = above_ref[relayed_for(3).index(1), 1]


def relayed_for(k):
    return [m for m in (0, 1, 3) if m != k]


def add_kernel(a_ref, b_ref, out_ref):
    out_ref[...] = a_ref[...] + b_ref[...]


def fold_kernel(parts_ref, out_ref):
    total = parts_ref[0]
    for at in range(1, parts_ref.shape[0]):
        total = total + parts_ref[at]
    out_ref[...] = total


def copy_kernel(piece_ref, out_ref):
    for at in range(out_ref.shape[0]):
        out_ref[at] = piece_ref[...]


def lanes(start, size):
    return pl.ds(pl.multiple_of(start, size), size)


def places_of(m):
    if m < 2:
        return [(3 * m, 0, 0), (3 * m + 1, 0, 1), (3 * m + 2, 1, 1)]
    return [(6 + 4 * (m - 2) + 2 * a + b, a, b) for a in range(2) for b in range(2)]


def half_of_gram(half, hi_ref, lo_ref, out_ref):
    for m in range(5):
        (i0, j0), (i1, j1) = PAIRS[m], PAIRS[m + 5]
        i = lanes(jnp.where(half == 0, i0, i1) * TILE, TILE)
        j = lanes(jnp.where(half == 0, j0, j1) * TILE, TILE)
        left_hi, right_hi = hi_ref[:, i], hi_ref[:, j]
        left = jnp.concatenate([left_hi, left_hi, lo_ref[:, i]], axis=0)
        right = jnp.concatenate([right_hi, lo_ref[:, j], right_hi], axis=0)
        block = lax.dot_general(left, right, (((0,), (0,)), ((), ())), preferred_element_type=F32)
        for at, a, b in places_of(m):
            out_ref[at] = block[a * 128 : (a + 1) * 128, b * 128 : (b + 1) * 128]


def gram_send_kernel(at_ref, inner_ref, edge_ref, inner_got, edge_got, *refs):
    arrived, (hi_ref, lo_ref, out_ref) = refs[:12], refs[12:]
    z, c = at_ref[2], at_ref[3]
    for k in range(4):
        for j in range(2):
            band = lax.rem(z + 4 - k, 4) * 2 + lax.rem(c + j, 2)
            if k:
                inner, edge = arrived[6 * j + k - 1][...], arrived[6 * j + 3 + k - 1][...]
            elif j:
                inner, edge = inner_got[0], edge_got[0]
            else:
                inner, edge = inner_ref[...], edge_ref[...]
            for value, rows in ((inner, slice(0, INNER_ROWS)), (edge, slice(INNER_ROWS, 512))):
                hi, lo = split(value)
                hi_ref[rows, lanes(band * 128, 128)] = hi
                lo_ref[rows, lanes(band * 128, 128)] = lo
    half_of_gram(1 - c, hi_ref, lo_ref, out_ref)


def gram_keep_kernel(at_ref, hi_ref, lo_ref, out_ref):
    half_of_gram(at_ref[3], hi_ref, lo_ref, out_ref)


def times_normed(hi, lo, nh, nl):
    return dot(jnp.concatenate([hi, hi, lo], axis=1), jnp.concatenate([nh, nl, nh], axis=0))


def poly_kernel(order, at_ref, mine_ref, theirs_ref, ph_ref, pl_ref, stretch_ref, gram_ref, nh_ref, nl_ref, poly_ref):
    z, c = at_ref[2], at_ref[3]
    gram_ref[c] = mine_ref[...]
    gram_ref[1 - c] = theirs_ref[...]
    row = lax.broadcasted_iota(jnp.int32, (128, 128), 0)
    col = lax.broadcasted_iota(jnp.int32, (128, 128), 1)
    diag = jnp.zeros((128, 128), F32)
    for half in range(2):
        for m in range(2):
            for at, a, b in places_of(m):
                if a == b:
                    diag += jnp.where(row == col, gram_ref[half, at], 0.0)
    scale = jnp.sum(diag) / VECTORS
    for n, (i, j) in enumerate(PAIRS):
        for at, a, b in places_of(n % 5):
            hi, lo = split(gram_ref[n // 5, at] / scale)
            p, q = i * TILE + a * 128, j * TILE + b * 128
            nh_ref[p : p + 128, q : q + 128] = hi
            nl_ref[p : p + 128, q : q + 128] = lo
            if p != q:
                nh_ref[q : q + 128, p : p + 128] = hi.T
                nl_ref[q : q + 128, p : p + 128] = lo.T
    stretch_ref[...] = jnp.sqrt(jnp.full((8, 128), order, F32) / scale)
    right = []
    for j in range(2):
        band = lanes((2 * z + lax.rem(c + j, 2)) * 128, 128)
        right.append((nh_ref[:, band], nl_ref[:, band]))
    nh = jnp.concatenate([right[0][0], right[1][0]], axis=1)
    nl = jnp.concatenate([right[0][1], right[1][1]], axis=1)
    squared = times_normed(nh_ref[...], nl_ref[...], nh, nl)
    poly_ref[...] = 3.0 * squared - 10.0 * (nh.astype(F32) + nl.astype(F32))
    for q in range(4):
        for j in range(2):
            band = lax.rem(z + q, 4) * 2 + lax.rem(c + j, 2)
            part = poly_ref[pl.ds(pl.multiple_of(band * 128, 128), 128)]
            if q == 0:
                r = lax.broadcasted_iota(jnp.int32, (128, 256), 0)
                l = lax.broadcasted_iota(jnp.int32, (128, 256), 1)
                part = part + jnp.where(l == r + 128 * j, 15.0, 0.0)
            hi, lo = split(part / 8.0)
            at = q * 256 + j * 128
            ph_ref[at : at + 128] = hi
            pl_ref[at : at + 128] = lo


def turned_kernel(*refs):
    inner_refs, edge_refs, inner_got, edge_got = refs[:4], refs[4:8], refs[8], refs[9]
    arrived, bulks = refs[10:22], refs[22:26]
    ph_ref, pl_ref, stretch_ref, mine_ref, theirs_ref = refs[26:]

    def piece(r, q, j):
        k = (4 - q) % 4
        if q == 0 and j == 0:
            pair = (inner_refs[r][...], edge_refs[r][...])
        elif q == 0:
            pair = (inner_got[r], edge_got[r])
        elif r == 0:
            pair = (arrived[6 * j + k - 1][...], arrived[6 * j + 3 + k - 1][...])
        elif q == 2:
            return bulks[2 + j][r - 1]
        elif (r + k) % 4 == 2:
            return bulks[2 + k // 2][3 + j]
        else:
            return bulks[k // 2][relayed_for(k).index((r + k) % 4), j]
        return jnp.concatenate(pair, axis=0)

    ph, low = ph_ref[...], pl_ref[...]
    for r in range(4):
        highs, lows = [], []
        for q in range(4):
            for j in range(2):
                hi, lo = split(piece(r, q, j))
                highs.append(hi)
                lows.append(lo)
        out = times_normed(jnp.concatenate(highs, axis=1), jnp.concatenate(lows, axis=1), ph, low)
        stretch = stretch_ref[0:1]
        mine_ref[r] = out[:, :128] * stretch
        theirs_ref[r] = out[:, 128:] * stretch


def place_kernel(theirs, at_ref, rows_ref, *refs):
    out_ref, sem = refs[-2:]
    z, c = at_ref[2], at_ref[3]
    half = 1 - c if theirs else c
    copies = []
    for k in range(4):
        chip = lax.rem(z + k, 4)
        inner = pl.ds(pl.multiple_of(512 + (half * 4 + chip) * INNER_ROWS, 128), INNER_ROWS)
        edge = pl.ds(pl.multiple_of(half * 3584 + chip * EDGE_ROWS, 128), EDGE_ROWS)
        copies.append(pltpu.make_async_copy(rows_ref.at[k, pl.ds(0, INNER_ROWS)], out_ref.at[inner], sem.at[k]))
        copies.append(pltpu.make_async_copy(rows_ref.at[k, pl.ds(INNER_ROWS, EDGE_ROWS)], out_ref.at[edge], sem.at[4 + k]))
    for copy in copies:
        copy.start()
    for copy in copies:
        copy.wait()


def place(here, rows, into=None):
    extra = () if into is None else (into,)
    return call(
        functools.partial(place_kernel, into is not None), shaped(4096, 128), [SMEM_SPEC, ANY_SPEC] + [ANY_SPEC] * len(extra),
        [pltpu.SemaphoreType.DMA((8,))], (here, rows, *extra), STEP_LIMIT,
        out_specs=ANY_SPEC, input_output_aliases={2: 0} if extra else {},
    )


SHIFTS = (2, 1, 3)


def swap_cores(x):
    return lax.ppermute(x, "band", [(i, i ^ 1) for i in range(8)])


def shift_z(x, k):
    return lax.ppermute(x, "band", [(i, (i + 2 * k) % 8) for i in range(8)])


def halos_of(first, last):
    size = lax.axis_size("space")
    up = [(i, (i + 1) % size) for i in range(size)]
    down = [(j, i) for i, j in up]
    before = lax.ppermute(last, "space", up)
    return before, lax.ppermute(first, "space", down)


def steps(vectors, blocks, neighbours):
    elem_dev, basis = blocks.shape[0], blocks.shape[2]
    panel = vectors.shape[1]
    order = float(elem_dev * basis * lax.axis_size("space"))
    space, band = lax.axis_index("space"), lax.axis_index("band")
    x, y, z, c = space & 3, space >> 2, band >> 1, band & 1
    here = jnp.stack([x, y, z, c]).astype(jnp.int32)

    start = vectors.reshape(elem_dev, basis, panel)
    halos = halos_of(start[:REACH], start[-REACH:])
    mid, op = build_operator(neighbours.T, here, blocks, start)
    low, high = first_edges(op, start, halos)
    halos = halos_of(low, high)
    inner, other = second_inner(here, op, mid, low, high, start)
    inner_got = swap_cores(other)
    arrived = {}
    for j, rows in enumerate((inner, inner_got)):
        for k in SHIFTS:
            arrived[j, 0, k] = shift_z(rows[k], k)
    edge, other = second_edges(here, op, mid, low, high, halos, start)
    edge_got = swap_cores(other)
    for j, rows in enumerate((edge, edge_got)):
        for k in SHIFTS:
            arrived[j, 1, k] = shift_z(rows[k], k)
    arrived = [arrived[j, e, k] for j in range(2) for e in range(2) for k in (1, 2, 3)]

    share = elem_dev * basis // 8
    held = (*inner, *edge, inner_got, edge_got)
    late, arrived = lax.optimization_barrier((held, arrived))
    bulks = call(bulk_kernel, (shaped(2, 2, share, panel),) * 2, [VMEM_SPEC] * 10, [], late, STEP_LIMIT)
    sent = []
    for k, bulk in zip((1, 3), bulks):
        sent.append(shift_z(bulk, k))

    half = shaped(18, 128, 128)
    wide = shaped(share, VECTORS, dtype=BF16)
    hi, lo, send = call(
        gram_send_kernel, (wide, wide, half), [SMEM_SPEC] + [VMEM_SPEC] * 16, [],
        (here, inner[0], edge[0], inner_got, edge_got, *arrived), STEP_LIMIT,
    )
    theirs = swap_cores(send)
    keep = call(gram_keep_kernel, half, [SMEM_SPEC] + [VMEM_SPEC] * 2, [], (here, hi, lo), STEP_LIMIT)
    total = call(add_kernel, half, [VMEM_SPEC] * 2, [], (keep, theirs), STEP_LIMIT)
    pieces = total.reshape(16, 144, panel)
    pieces = lax.all_to_all(pieces, "space", split_axis=0, concat_axis=0, tiled=True)
    piece = call(fold_kernel, shaped(144, panel), [VMEM_SPEC], [], (pieces,), STEP_LIMIT)
    sums = [shift_z(piece, k) for k in SHIFTS]
    piece = piece + sums[0] + (sums[1] + sums[2])
    below, above, piece = lax.optimization_barrier((*sent, piece))
    relays = call(
        relay_kernel, (shaped(5, share, panel),) * 2, [VMEM_SPEC] * 10, [],
        (below, above, arrived[0], arrived[3], arrived[8], arrived[11], inner[2], edge[2], inner_got, edge_got), STEP_LIMIT,
    )
    bulks = [below, above]
    for k, relay in zip((1, 3), relays):
        bulks.append(shift_z(relay, k))
    copies = call(copy_kernel, shaped(*pieces.shape), [VMEM_SPEC], [], (piece,), STEP_LIMIT)
    mine = lax.all_to_all(copies, "space", split_axis=0, concat_axis=0, tiled=True)
    mine = mine.reshape(half.shape)
    theirs = swap_cores(mine)

    poly = shaped(VECTORS, TILE, dtype=BF16)
    ph, low, stretch = call(
        functools.partial(poly_kernel, order), (poly, poly, shaped(8, 128)), [SMEM_SPEC] + [VMEM_SPEC] * 2,
        [
            pltpu.VMEM((2, *half.shape), F32),
            pltpu.VMEM((VECTORS, VECTORS), BF16),
            pltpu.VMEM((VECTORS, VECTORS), BF16),
            pltpu.VMEM((VECTORS, TILE), F32),
        ],
        (here, mine, theirs), TURN_LIMIT,
    )
    quarter = shaped(4, share, panel)
    mine, theirs = call(
        turned_kernel, (quarter, quarter), [VMEM_SPEC] * 29, [],
        (*held, *arrived, *bulks, ph, low, stretch), TURN_LIMIT,
    )
    theirs = swap_cores(theirs)
    return place(here, theirs, place(here, mine))


def solution(mesh):
    return jax.shard_map(
        steps,
        mesh=mesh,
        in_specs=(P("space", "band"), P("space", None, None, None), P("space", None)),
        out_specs=P("space", "band"),
        check_vma=False,
    )
```

```python
import functools
import jax
import jax.numpy as jnp
from jax import lax
from jax.experimental import pallas as pl
from jax.experimental.pallas import tpu as pltpu
from jax.sharding import PartitionSpec as P


VECTORS = 1024
REACH = 2
TILE = 256
PAIRS = [(0, 0), (1, 1), (0, 1), (0, 2), (0, 3), (2, 2), (3, 3), (1, 2), (1, 3), (2, 3)]
INNER_ROWS = 384
EDGE_ROWS = 128
SPAN = 2 * REACH + 1
TOTAL = 256
RING = 8
BUILD_LIMIT = 30 << 20
STEP_LIMIT = 16 << 20
OPERATOR_LIMIT = 8 << 20
TURN_LIMIT = 32 << 20
F32 = jnp.float32
BF16 = jnp.bfloat16


def split(x):
    hi = x.astype(BF16)
    lo = (x - hi.astype(F32)).astype(BF16)
    return hi, lo


def dot(a, b):
    return jnp.dot(a, b, preferred_element_type=F32)


def spread(wide_ref, slot, value):
    hi, lo = split(value)
    wide_ref[slot, :, 0:128] = hi
    wide_ref[slot, :, 128:256] = lo


def apply_one(op_ref, wide_ref, elem):
    return apply_left(op_ref[elem], wide_ref, elem)


def apply_left(left, wide_ref, elem):
    near = wide_ref[pl.ds(elem, SPAN)].reshape(SPAN * 256, 256)
    prod = dot(left, near)
    return (prod[256:, 128:] + prod[256:, :128]) + (prod[:256, 128:] + prod[:256, :128])


def first_of(total, own):
    return (total - 0.5 * own) / 1.5


def second_of(total, own, base):
    return 2.0 * (total - 0.5 * own) / 1.5 - base


def build_kernel(count, near_ref, at_ref, blocks_ref, vectors_ref, step_ref, op_ref, wide_ref, ring_ref, own_ref, sums_a, sums_b, left_a, left_b, sem, own_sem):
    def fetch(n):
        elem = lax.rem(n + REACH, count)
        return pltpu.make_async_copy(blocks_ref.at[elem], ring_ref.at[lax.rem(n, RING)], sem.at[lax.rem(n, RING)])

    first = (at_ref[1] * 4 + at_ref[0]) * count
    load = pltpu.make_async_copy(vectors_ref, own_ref, own_sem)
    load.start()
    for n in range(RING):
        fetch(n).start()
    load.wait()
    for r in range(count):
        spread(wide_ref, REACH + r, own_ref[r])

    def combine(n, sums_ref, left_ref):
        elem = lax.rem(n + REACH, count)
        at = lax.rem(n, RING)
        sums_ref[0] = ring_ref[at, 1]
        sums_ref[SPAN - 1] = ring_ref[at, 2]
        for o in range(1, SPAN - 1):
            sums_ref[o] = jnp.zeros((256, 256), F32)
        for k in (0, 3, 4, 5, 6):
            o = lax.rem(near_ref[k, elem] - first - elem + REACH + 2 * TOTAL, TOTAL)
            sums_ref[o] = sums_ref[o] + ring_ref[at, k]
        for o in range(SPAN):
            hi, lo = split(sums_ref[o])
            cols = slice(o * 256, (o + 1) * 256)
            op_ref[elem, :256, cols] = hi
            op_ref[elem, 256:, cols] = lo
            left_ref[:256, cols] = hi
            left_ref[256:, cols] = lo

    def refill(n):
        @pl.when(n + RING < count)
        def _():
            fetch(n + RING).start()

    def step(n, left_ref):
        total = apply_left(left_ref[...], wide_ref, n + REACH)
        step_ref[n] = first_of(total, own_ref[n + REACH])

    def inner(g, _):
        n = 2 * g
        fetch(n + 1).wait()
        fetch(n + 2).wait()
        step(n, left_a)
        combine(n + 1, sums_b, left_b)
        step(n + 1, left_b)
        combine(n + 2, sums_a, left_a)
        refill(n + 1)
        refill(n + 2)
        return 0

    def outer(n, _):
        fetch(n).wait()
        combine(n, sums_a, left_a)
        return 0

    fetch(0).wait()
    combine(0, sums_a, left_a)
    refill(0)
    lax.fori_loop(0, (count - 2 * REACH) // 2, inner, 0)
    lax.fori_loop(count - 2 * REACH + 1, count, outer, 0)


def edges_of(count):
    return [*range(REACH), *range(count - REACH, count)]


def first_edge_kernel(count, op_ref, own_ref, before_ref, after_ref, low_ref, high_ref, wide_ref):
    for r in range(REACH):
        spread(wide_ref, r, before_ref[r])
        spread(wide_ref, REACH + count + r, after_ref[r])
    for r in range(2 * REACH):
        spread(wide_ref, REACH + r, own_ref[r])
        spread(wide_ref, count - REACH + r, own_ref[count - 2 * REACH + r])
    for at, elem in enumerate(edges_of(count)):
        out_ref = low_ref if at < REACH else high_ref
        out_ref[at % REACH] = first_of(apply_one(op_ref, wide_ref, elem), own_ref[elem])


def deal(at_ref, all_ref, own_refs, other_ref):
    z, c = at_ref[2], at_ref[3]
    size = own_refs[0].shape[0]
    for k in range(4):
        chip = lax.rem(z + k, 4)
        own_refs[k][...] = all_ref[pl.ds(pl.multiple_of((c * 4 + chip) * size, 128), size)]
        other_ref[k] = all_ref[pl.ds(pl.multiple_of(((1 - c) * 4 + chip) * size, 128), size)]


def second_edge_kernel(count, at_ref, op_ref, mid_ref, low_ref, high_ref, before_ref, after_ref, base_ref, *refs):
    own_refs, (other_ref, wide_ref, all_ref) = refs[:4], refs[4:]
    for r in range(REACH):
        spread(wide_ref, r, before_ref[r])
        spread(wide_ref, REACH + r, low_ref[r])
        spread(wide_ref, 2 * REACH + r, mid_ref[r])
        spread(wide_ref, count - REACH + r, mid_ref[count - 3 * REACH + r])
        spread(wide_ref, count + r, high_ref[r])
        spread(wide_ref, REACH + count + r, after_ref[r])
    for at, elem in enumerate(edges_of(count)):
        own = (low_ref if at < REACH else high_ref)[at % REACH]
        all_ref[at * 256 : (at + 1) * 256] = second_of(apply_one(op_ref, wide_ref, elem), own, base_ref[elem])
    deal(at_ref, all_ref, own_refs, other_ref)


def inner_kernel(count, at_ref, op_ref, mid_ref, low_ref, high_ref, base_ref, *refs):
    own_refs, (other_ref, wide_ref, all_ref) = refs[:4], refs[4:]
    for r in range(REACH):
        spread(wide_ref, REACH + r, low_ref[r])
        spread(wide_ref, count + r, high_ref[r])
    for r in range(count - 2 * REACH):
        spread(wide_ref, 2 * REACH + r, mid_ref[r])

    def body(g, _):
        for u in range(4):
            at = 4 * g + u
            elem = REACH + at
            rows = pl.ds(pl.multiple_of(at * 256, 256), 256)
            all_ref[rows] = second_of(apply_one(op_ref, wide_ref, elem), mid_ref[at], base_ref[elem])
        return 0

    lax.fori_loop(0, (count - 2 * REACH) // 4, body, 0)
    deal(at_ref, all_ref, own_refs, other_ref)


VMEM_SPEC = pl.BlockSpec(memory_space=pltpu.VMEM)
SMEM_SPEC = pl.BlockSpec(memory_space=pltpu.SMEM)
ANY_SPEC = pl.BlockSpec(memory_space=pl.ANY)
HBM_SPEC = pl.BlockSpec(memory_space=pltpu.HBM)


def shaped(*shape, dtype=F32):
    return jax.ShapeDtypeStruct(shape, dtype)


def call(kernel, outs, specs, scratch, args, limit, **kwargs):
    return pl.pallas_call(
        kernel,
        out_shape=outs,
        in_specs=specs,
        out_specs=kwargs.pop("out_specs", jax.tree.map(lambda _: VMEM_SPEC, outs)),
        scratch_shapes=scratch,
        compiler_params=pltpu.CompilerParams(vmem_limit_bytes=limit),
        **kwargs,
    )(*args)


def wide_scratch(count):
    return pltpu.VMEM((count + 2 * REACH, 256, 256), BF16)


def build_operator(near, here, blocks, own):
    count = own.shape[0]
    return call(
        functools.partial(build_kernel, count),
        (shaped(count - 2 * REACH, 256, 128), shaped(count, 512, SPAN * 256, dtype=BF16)),
        [SMEM_SPEC, SMEM_SPEC, HBM_SPEC, HBM_SPEC],
        [
            wide_scratch(count),
            pltpu.VMEM((RING, 7, 256, 256), F32),
            pltpu.VMEM(own.shape, F32),
            pltpu.VMEM((SPAN, 256, 256), F32),
            pltpu.VMEM((SPAN, 256, 256), F32),
            pltpu.VMEM((512, SPAN * 256), BF16),
            pltpu.VMEM((512, SPAN * 256), BF16),
            pltpu.SemaphoreType.DMA((RING,)),
            pltpu.SemaphoreType.DMA,
        ],
        (near, here, blocks, own),
        BUILD_LIMIT,
    )


def first_edges(op, own, halos):
    count = own.shape[0]
    edge = shaped(REACH, 256, 128)
    return call(
        functools.partial(first_edge_kernel, count), (edge, edge), [VMEM_SPEC] * 4,
        [wide_scratch(count)], (op, own, *halos), OPERATOR_LIMIT,
    )


def second_inner(here, op, mid, low, high, base):
    count = base.shape[0]
    outs = call(
        functools.partial(inner_kernel, count), (shaped(INNER_ROWS, 128),) * 4 + (shaped(4, INNER_ROWS, 128),),
        [SMEM_SPEC] + [VMEM_SPEC] * 5,
        [wide_scratch(count), pltpu.VMEM((8 * INNER_ROWS, 128), F32)],
        (here, op, mid, low, high, base), OPERATOR_LIMIT,
    )
    return outs[:4], outs[4]


def second_edges(here, op, mid, low, high, halos, base):
    count = base.shape[0]
    outs = call(
        functools.partial(second_edge_kernel, count), (shaped(EDGE_ROWS, 128),) * 4 + (shaped(4, EDGE_ROWS, 128),),
        [SMEM_SPEC] + [VMEM_SPEC] * 7,
        [wide_scratch(count), pltpu.VMEM((8 * EDGE_ROWS, 128), F32)],
        (here, op, mid, low, high, *halos, base), OPERATOR_LIMIT,
    )
    return outs[:4], outs[4]


def bulk_kernel(*refs):
    inner_refs, edge_refs, inner_got, edge_got, out_refs = refs[:4], refs[4:8], refs[8], refs[9], refs[10:]
    for k, out_ref in zip((1, 3), out_refs):
        for i, m in enumerate(relayed_for(k)):
            out_ref[i, 0, :INNER_ROWS] = inner_refs[m][...]
            out_ref[i, 0, INNER_ROWS:] = edge_refs[m][...]
            out_ref[i, 1, :INNER_ROWS] = inner_got[m]
            out_ref[i, 1, INNER_ROWS:] = edge_got[m]


def relay_kernel(below_ref, above_ref, below_inner, below_edge, above_inner, above_edge, inner_ref, edge_ref, inner_got, edge_got, up_ref, down_ref):
    for out_ref in (up_ref, down_ref):
        out_ref[3, :INNER_ROWS] = inner_ref[...]
        out_ref[3, INNER_ROWS:] = edge_ref[...]
        out_ref[4, :INNER_ROWS] = inner_got[2]
        out_ref[4, INNER_ROWS:] = edge_got[2]
    up_ref[0] = below_ref[relayed_for(1).index(3), 0]
    up_ref[1] = below_ref[relayed_for(1).index(0), 0]
    up_ref[2, :INNER_ROWS] = below_inner[...]
    up_ref[2, INNER_ROWS:] = below_edge[...]
    down_ref[0, :INNER_ROWS] = above_inner[...]
    down_ref[0, INNER_ROWS:] = above_edge[...]
    down_ref[1] = above_ref[relayed_for(3).index(0), 1]
    down_ref[2] = above_ref[relayed_for(3).index(1), 1]


def relayed_for(k):
    return [m for m in (0, 1, 3) if m != k]


def add_kernel(a_ref, b_ref, out_ref):
    out_ref[...] = a_ref[...] + b_ref[...]


def fold_kernel(parts_ref, out_ref):
    total = parts_ref[0]
    for at in range(1, parts_ref.shape[0]):
        total = total + parts_ref[at]
    out_ref[...] = total


def copy_kernel(piece_ref, out_ref):
    for at in range(out_ref.shape[0]):
        out_ref[at] = piece_ref[...]


def lanes(start, size):
    return pl.ds(pl.multiple_of(start, size), size)


def places_of(m):
    if m < 2:
        return [(3 * m, 0, 0), (3 * m + 1, 0, 1), (3 * m + 2, 1, 1)]
    return [(6 + 4 * (m - 2) + 2 * a + b, a, b) for a in range(2) for b in range(2)]


def half_of_gram(half, hi_ref, lo_ref, out_ref, start_ref=None):
    for m in range(5):
        (i0, j0), (i1, j1) = PAIRS[m], PAIRS[m + 5]
        i = lanes(jnp.where(half == 0, i0, i1) * TILE, TILE)
        j = lanes(jnp.where(half == 0, j0, j1) * TILE, TILE)
        left_hi, right_hi = hi_ref[:, i], hi_ref[:, j]
        left = jnp.concatenate([left_hi, left_hi, lo_ref[:, i]], axis=0)
        right = jnp.concatenate([right_hi, lo_ref[:, j], right_hi], axis=0)
        block = lax.dot_general(left, right, (((0,), (0,)), ((), ())), preferred_element_type=F32)
        for at, a, b in places_of(m):
            part = block[a * 128 : (a + 1) * 128, b * 128 : (b + 1) * 128]
            out_ref[at] = part if start_ref is None else start_ref[at] + part


def split_rows(at_ref, mine_ref, got_ref, arrived, hi_ref, lo_ref):
    z, c = at_ref[2], at_ref[3]
    for k in range(4):
        for j in range(2):
            band = lax.rem(z + 4 - k, 4) * 2 + lax.rem(c + j, 2)
            value = arrived[3 * j + k - 1][...] if k else (got_ref[0] if j else mine_ref[...])
            hi, lo = split(value)
            hi_ref[:, lanes(band * 128, 128)] = hi
            lo_ref[:, lanes(band * 128, 128)] = lo


def gram_inner_kernel(at_ref, mine_ref, got_ref, *refs):
    arrived, (send_ref, keep_ref, hi_ref, lo_ref) = refs[:6], refs[6:]
    split_rows(at_ref, mine_ref, got_ref, arrived, hi_ref, lo_ref)
    half_of_gram(1 - at_ref[3], hi_ref, lo_ref, send_ref)
    half_of_gram(at_ref[3], hi_ref, lo_ref, keep_ref)


def gram_send_kernel(at_ref, mine_ref, got_ref, *refs):
    arrived, (start_ref, hi_ref, lo_ref, out_ref) = refs[:6], refs[6:]
    split_rows(at_ref, mine_ref, got_ref, arrived, hi_ref, lo_ref)
    half_of_gram(1 - at_ref[3], hi_ref, lo_ref, out_ref, start_ref)


def gram_keep_kernel(at_ref, hi_ref, lo_ref, start_ref, out_ref):
    half_of_gram(at_ref[3], hi_ref, lo_ref, out_ref, start_ref)


def times_normed(hi, lo, nh, nl):
    return dot(jnp.concatenate([hi, hi, lo], axis=1), jnp.concatenate([nh, nl, nh], axis=0))


def poly_kernel(order, at_ref, mine_ref, theirs_ref, ph_ref, pl_ref, stretch_ref, gram_ref, nh_ref, nl_ref, poly_ref):
    z, c = at_ref[2], at_ref[3]
    gram_ref[c] = mine_ref[...]
    gram_ref[1 - c] = theirs_ref[...]
    row = lax.broadcasted_iota(jnp.int32, (128, 128), 0)
    col = lax.broadcasted_iota(jnp.int32, (128, 128), 1)
    diag = jnp.zeros((128, 128), F32)
    for half in range(2):
        for m in range(2):
            for at, a, b in places_of(m):
                if a == b:
                    diag += jnp.where(row == col, gram_ref[half, at], 0.0)
    scale = jnp.sum(diag) / VECTORS
    for n, (i, j) in enumerate(PAIRS):
        for at, a, b in places_of(n % 5):
            hi, lo = split(gram_ref[n // 5, at] / scale)
            p, q = i * TILE + a * 128, j * TILE + b * 128
            nh_ref[p : p + 128, q : q + 128] = hi
            nl_ref[p : p + 128, q : q + 128] = lo
            if p != q:
                nh_ref[q : q + 128, p : p + 128] = hi.T
                nl_ref[q : q + 128, p : p + 128] = lo.T
    stretch_ref[...] = jnp.sqrt(jnp.full((8, 128), order, F32) / scale)
    right = []
    for j in range(2):
        band = lanes((2 * z + lax.rem(c + j, 2)) * 128, 128)
        right.append((nh_ref[:, band], nl_ref[:, band]))
    nh = jnp.concatenate([right[0][0], right[1][0]], axis=1)
    nl = jnp.concatenate([right[0][1], right[1][1]], axis=1)
    squared = times_normed(nh_ref[...], nl_ref[...], nh, nl)
    poly_ref[...] = 3.0 * squared - 10.0 * (nh.astype(F32) + nl.astype(F32))
    for q in range(4):
        for j in range(2):
            band = lax.rem(z + q, 4) * 2 + lax.rem(c + j, 2)
            part = poly_ref[pl.ds(pl.multiple_of(band * 128, 128), 128)]
            if q == 0:
                r = lax.broadcasted_iota(jnp.int32, (128, 256), 0)
                l = lax.broadcasted_iota(jnp.int32, (128, 256), 1)
                part = part + jnp.where(l == r + 128 * j, 15.0, 0.0)
            hi, lo = split(part / 8.0)
            at = q * 256 + j * 128
            ph_ref[at : at + 128] = hi
            pl_ref[at : at + 128] = lo


def turned_kernel(*refs):
    inner_refs, edge_refs, inner_got, edge_got = refs[:4], refs[4:8], refs[8], refs[9]
    arrived, bulks = refs[10:22], refs[22:26]
    ph_ref, pl_ref, stretch_ref, mine_ref, theirs_ref = refs[26:]

    def piece(r, q, j):
        k = (4 - q) % 4
        if q == 0 and j == 0:
            pair = (inner_refs[r][...], edge_refs[r][...])
        elif q == 0:
            pair = (inner_got[r], edge_got[r])
        elif r == 0:
            pair = (arrived[6 * j + k - 1][...], arrived[6 * j + 3 + k - 1][...])
        elif q == 2:
            return bulks[2 + j][r - 1]
        elif (r + k) % 4 == 2:
            return bulks[2 + k // 2][3 + j]
        else:
            return bulks[k // 2][relayed_for(k).index((r + k) % 4), j]
        return jnp.concatenate(pair, axis=0)

    ph, low = ph_ref[...], pl_ref[...]
    for r in range(4):
        highs, lows = [], []
        for q in range(4):
            for j in range(2):
                hi, lo = split(piece(r, q, j))
                highs.append(hi)
                lows.append(lo)
        out = times_normed(jnp.concatenate(highs, axis=1), jnp.concatenate(lows, axis=1), ph, low)
        stretch = stretch_ref[0:1]
        mine_ref[r] = out[:, :128] * stretch
        theirs_ref[r] = out[:, 128:] * stretch


def place_kernel(theirs, at_ref, rows_ref, *refs):
    out_ref, sem = refs[-2:]
    z, c = at_ref[2], at_ref[3]
    half = 1 - c if theirs else c
    copies = []
    for k in range(4):
        chip = lax.rem(z + k, 4)
        inner = pl.ds(pl.multiple_of(512 + (half * 4 + chip) * INNER_ROWS, 128), INNER_ROWS)
        edge = pl.ds(pl.multiple_of(half * 3584 + chip * EDGE_ROWS, 128), EDGE_ROWS)
        copies.append(pltpu.make_async_copy(rows_ref.at[k, pl.ds(0, INNER_ROWS)], out_ref.at[inner], sem.at[k]))
        copies.append(pltpu.make_async_copy(rows_ref.at[k, pl.ds(INNER_ROWS, EDGE_ROWS)], out_ref.at[edge], sem.at[4 + k]))
    for copy in copies:
        copy.start()
    for copy in copies:
        copy.wait()


def place(here, rows, into=None):
    extra = () if into is None else (into,)
    return call(
        functools.partial(place_kernel, into is not None), shaped(4096, 128), [SMEM_SPEC, ANY_SPEC] + [ANY_SPEC] * len(extra),
        [pltpu.SemaphoreType.DMA((8,))], (here, rows, *extra), STEP_LIMIT,
        out_specs=ANY_SPEC, input_output_aliases={2: 0} if extra else {},
    )


SHIFTS = (2, 1, 3)


def swap_cores(x):
    return lax.ppermute(x, "band", [(i, i ^ 1) for i in range(8)])


def shift_z(x, k):
    return lax.ppermute(x, "band", [(i, (i + 2 * k) % 8) for i in range(8)])


def halos_of(first, last):
    size = lax.axis_size("space")
    up = [(i, (i + 1) % size) for i in range(size)]
    down = [(j, i) for i, j in up]
    before = lax.ppermute(last, "space", up)
    return before, lax.ppermute(first, "space", down)


def steps(vectors, blocks, neighbours):
    elem_dev, basis = blocks.shape[0], blocks.shape[2]
    panel = vectors.shape[1]
    order = float(elem_dev * basis * lax.axis_size("space"))
    space, band = lax.axis_index("space"), lax.axis_index("band")
    x, y, z, c = space & 3, space >> 2, band >> 1, band & 1
    here = jnp.stack([x, y, z, c]).astype(jnp.int32)

    start = vectors.reshape(elem_dev, basis, panel)
    halos = halos_of(start[:REACH], start[-REACH:])
    mid, op = build_operator(neighbours.T, here, blocks, start)
    low, high = first_edges(op, start, halos)
    halos = halos_of(low, high)
    inner, other = second_inner(here, op, mid, low, high, start)
    inner_got = swap_cores(other)
    arrived = {}
    for j, rows in enumerate((inner, inner_got)):
        for k in SHIFTS:
            arrived[j, 0, k] = shift_z(rows[k], k)
    edge, other = second_edges(here, op, mid, low, high, halos, start)
    edge_got = swap_cores(other)
    for j, rows in enumerate((edge, edge_got)):
        for k in SHIFTS:
            arrived[j, 1, k] = shift_z(rows[k], k)
    half = shaped(18, 128, 128)
    wide = pltpu.VMEM((INNER_ROWS, VECTORS), BF16)
    part_send, part_keep = call(
        gram_inner_kernel, (half, half), [SMEM_SPEC] + [VMEM_SPEC] * 8, [wide, wide],
        (here, inner[0], inner_got, *(arrived[j, 0, k] for j in range(2) for k in (1, 2, 3))), STEP_LIMIT,
    )
    arrived = [arrived[j, e, k] for j in range(2) for e in range(2) for k in (1, 2, 3)]

    share = elem_dev * basis // 8
    held = (*inner, *edge, inner_got, edge_got)
    late, arrived = lax.optimization_barrier((held, arrived))
    bulks = call(bulk_kernel, (shaped(2, 2, share, panel),) * 2, [VMEM_SPEC] * 10, [], late, STEP_LIMIT)
    sent = []
    for k, bulk in zip((1, 3), bulks):
        sent.append(shift_z(bulk, k))

    wide = shaped(EDGE_ROWS, VECTORS, dtype=BF16)
    hi, lo, send = call(
        gram_send_kernel, (wide, wide, half), [SMEM_SPEC] + [VMEM_SPEC] * 9, [],
        (here, edge[0], edge_got, *arrived[3:6], *arrived[9:12], part_send), STEP_LIMIT,
    )
    theirs = swap_cores(send)
    keep = call(gram_keep_kernel, half, [SMEM_SPEC] + [VMEM_SPEC] * 3, [], (here, hi, lo, part_keep), STEP_LIMIT)
    total = call(add_kernel, half, [VMEM_SPEC] * 2, [], (keep, theirs), STEP_LIMIT)
    pieces = total.reshape(16, 144, panel)
    pieces = lax.all_to_all(pieces, "space", split_axis=0, concat_axis=0, tiled=True)
    piece = call(fold_kernel, shaped(144, panel), [VMEM_SPEC], [], (pieces,), STEP_LIMIT)
    sums = [shift_z(piece, k) for k in SHIFTS]
    piece = piece + sums[0] + (sums[1] + sums[2])
    below, above, piece = lax.optimization_barrier((*sent, piece))
    relays = call(
        relay_kernel, (shaped(5, share, panel),) * 2, [VMEM_SPEC] * 10, [],
        (below, above, arrived[0], arrived[3], arrived[8], arrived[11], inner[2], edge[2], inner_got, edge_got), STEP_LIMIT,
    )
    bulks = [below, above]
    for k, relay in zip((1, 3), relays):
        bulks.append(shift_z(relay, k))
    copies = call(copy_kernel, shaped(*pieces.shape), [VMEM_SPEC], [], (piece,), STEP_LIMIT)
    mine = lax.all_to_all(copies, "space", split_axis=0, concat_axis=0, tiled=True)
    mine = mine.reshape(half.shape)
    theirs = swap_cores(mine)

    poly = shaped(VECTORS, TILE, dtype=BF16)
    ph, low, stretch = call(
        functools.partial(poly_kernel, order), (poly, poly, shaped(8, 128)), [SMEM_SPEC] + [VMEM_SPEC] * 2,
        [
            pltpu.VMEM((2, *half.shape), F32),
            pltpu.VMEM((VECTORS, VECTORS), BF16),
            pltpu.VMEM((VECTORS, VECTORS), BF16),
            pltpu.VMEM((VECTORS, TILE), F32),
        ],
        (here, mine, theirs), TURN_LIMIT,
    )
    quarter = shaped(4, share, panel)
    mine, theirs = call(
        turned_kernel, (quarter, quarter), [VMEM_SPEC] * 29, [],
        (*held, *arrived, *bulks, ph, low, stretch), TURN_LIMIT,
    )
    theirs = swap_cores(theirs)
    return place(here, theirs, place(here, mine))


def solution(mesh):
    return jax.shard_map(
        steps,
        mesh=mesh,
        in_specs=(P("space", "band"), P("space", None, None, None), P("space", None)),
        out_specs=P("space", "band"),
        check_vma=False,
    )
```

```python
import functools
import jax
import jax.numpy as jnp
from jax import lax
from jax.experimental import pallas as pl
from jax.experimental.pallas import tpu as pltpu
from jax.sharding import PartitionSpec as P


VECTORS = 1024
REACH = 2
TILE = 256
PAIRS = [(0, 0), (1, 1), (0, 1), (0, 2), (0, 3), (2, 2), (3, 3), (1, 2), (1, 3), (2, 3)]
INNER_ROWS = 384
EDGE_ROWS = 128
SPAN = 2 * REACH + 1
TOTAL = 256
RING = 8
BUILD_LIMIT = 30 << 20
STEP_LIMIT = 16 << 20
OPERATOR_LIMIT = 8 << 20
TURN_LIMIT = 32 << 20
F32 = jnp.float32
BF16 = jnp.bfloat16


def split(x):
    hi = x.astype(BF16)
    lo = (x - hi.astype(F32)).astype(BF16)
    return hi, lo


def dot(a, b):
    return jnp.dot(a, b, preferred_element_type=F32)


def spread(wide_ref, slot, value):
    hi, lo = split(value)
    wide_ref[slot, :, 0:128] = hi
    wide_ref[slot, :, 128:256] = lo


def apply_one(op_ref, wide_ref, elem):
    return apply_left(op_ref[elem], wide_ref, elem)


def apply_left(left, wide_ref, elem):
    near = wide_ref[pl.ds(elem, SPAN)].reshape(SPAN * 256, 256)
    prod = dot(left, near)
    return (prod[256:, 128:] + prod[256:, :128]) + (prod[:256, 128:] + prod[:256, :128])


def first_of(total, own):
    return (total - 0.5 * own) / 1.5


def second_of(total, own, base):
    return 2.0 * (total - 0.5 * own) / 1.5 - base


def build_kernel(count, table_ref, at_ref, blocks_ref, vectors_ref, step_ref, op_ref, wide_ref, ring_ref, own_ref, sums_a, sums_b, left_a, left_b, near_ref, sem, own_sem, near_sem):
    def fetch(n):
        elem = lax.rem(n + REACH, count)
        return pltpu.make_async_copy(blocks_ref.at[elem], ring_ref.at[lax.rem(n, RING)], sem.at[lax.rem(n, RING)])

    first = (at_ref[1] * 4 + at_ref[0]) * count
    load = pltpu.make_async_copy(vectors_ref, own_ref, own_sem)
    table = pltpu.make_async_copy(table_ref, near_ref, near_sem)
    table.start()
    load.start()
    for n in range(2):
        fetch(n).start()

    def combine(n, sums_ref, left_ref):
        elem = lax.rem(n + REACH, count)
        at = lax.rem(n, RING)
        sums_ref[0] = ring_ref[at, 1]
        sums_ref[SPAN - 1] = ring_ref[at, 2]
        for o in range(1, SPAN - 1):
            sums_ref[o] = jnp.zeros((256, 256), F32)
        for k in (0, 3, 4, 5, 6):
            o = lax.rem(near_ref[k, elem] - first - elem + REACH + 2 * TOTAL, TOTAL)
            sums_ref[o] = sums_ref[o] + ring_ref[at, k]
        for o in range(SPAN):
            hi, lo = split(sums_ref[o])
            cols = slice(o * 256, (o + 1) * 256)
            op_ref[elem, :256, cols] = hi
            op_ref[elem, 256:, cols] = lo
            left_ref[:256, cols] = hi
            left_ref[256:, cols] = lo

    def refill(n):
        @pl.when(n + RING < count)
        def _():
            fetch(n + RING).start()

    def step(n, left_ref):
        total = apply_left(left_ref[...], wide_ref, n + REACH)
        step_ref[n] = first_of(total, own_ref[n + REACH])

    def inner(g, _):
        n = 2 * g
        fetch(n + 1).wait()
        fetch(n + 2).wait()
        step(n, left_a)
        combine(n + 1, sums_b, left_b)
        step(n + 1, left_b)
        combine(n + 2, sums_a, left_a)
        refill(n + 1)
        refill(n + 2)
        return 0

    def outer(n, _):
        fetch(n).wait()
        combine(n, sums_a, left_a)
        return 0

    table.wait()
    fetch(0).wait()
    for n in range(2, RING):
        fetch(n).start()
    combine(0, sums_a, left_a)
    refill(0)
    load.wait()
    for r in range(count):
        spread(wide_ref, REACH + r, own_ref[r])
    lax.fori_loop(0, (count - 2 * REACH) // 2, inner, 0)
    lax.fori_loop(count - 2 * REACH + 1, count, outer, 0)


def edges_of(count):
    return [*range(REACH), *range(count - REACH, count)]


def first_edge_kernel(count, op_ref, own_ref, before_ref, after_ref, low_ref, high_ref, wide_ref):
    for r in range(REACH):
        spread(wide_ref, r, before_ref[r])
        spread(wide_ref, REACH + count + r, after_ref[r])
    for r in range(2 * REACH):
        spread(wide_ref, REACH + r, own_ref[r])
        spread(wide_ref, count - REACH + r, own_ref[count - 2 * REACH + r])
    for at, elem in enumerate(edges_of(count)):
        out_ref = low_ref if at < REACH else high_ref
        out_ref[at % REACH] = first_of(apply_one(op_ref, wide_ref, elem), own_ref[elem])


def deal(at_ref, all_ref, own_refs, other_ref):
    z, c = at_ref[2], at_ref[3]
    size = own_refs[0].shape[0]
    for k in range(4):
        chip = lax.rem(z + k, 4)
        own_refs[k][...] = all_ref[pl.ds(pl.multiple_of((c * 4 + chip) * size, 128), size)]
        other_ref[k] = all_ref[pl.ds(pl.multiple_of(((1 - c) * 4 + chip) * size, 128), size)]


def second_edge_kernel(count, at_ref, op_ref, mid_ref, low_ref, high_ref, before_ref, after_ref, base_ref, *refs):
    own_refs, (other_ref, wide_ref, all_ref) = refs[:4], refs[4:]
    for r in range(REACH):
        spread(wide_ref, r, before_ref[r])
        spread(wide_ref, REACH + r, low_ref[r])
        spread(wide_ref, 2 * REACH + r, mid_ref[r])
        spread(wide_ref, count - REACH + r, mid_ref[count - 3 * REACH + r])
        spread(wide_ref, count + r, high_ref[r])
        spread(wide_ref, REACH + count + r, after_ref[r])
    for at, elem in enumerate(edges_of(count)):
        own = (low_ref if at < REACH else high_ref)[at % REACH]
        all_ref[at * 256 : (at + 1) * 256] = second_of(apply_one(op_ref, wide_ref, elem), own, base_ref[elem])
    deal(at_ref, all_ref, own_refs, other_ref)


def inner_kernel(count, at_ref, op_ref, mid_ref, low_ref, high_ref, base_ref, *refs):
    own_refs, (other_ref, wide_ref, all_ref) = refs[:4], refs[4:]
    for r in range(REACH):
        spread(wide_ref, REACH + r, low_ref[r])
        spread(wide_ref, count + r, high_ref[r])
    for r in range(count - 2 * REACH):
        spread(wide_ref, 2 * REACH + r, mid_ref[r])

    def body(g, _):
        for u in range(4):
            at = 4 * g + u
            elem = REACH + at
            rows = pl.ds(pl.multiple_of(at * 256, 256), 256)
            all_ref[rows] = second_of(apply_one(op_ref, wide_ref, elem), mid_ref[at], base_ref[elem])
        return 0

    lax.fori_loop(0, (count - 2 * REACH) // 4, body, 0)
    deal(at_ref, all_ref, own_refs, other_ref)


VMEM_SPEC = pl.BlockSpec(memory_space=pltpu.VMEM)
SMEM_SPEC = pl.BlockSpec(memory_space=pltpu.SMEM)
ANY_SPEC = pl.BlockSpec(memory_space=pl.ANY)
HBM_SPEC = pl.BlockSpec(memory_space=pltpu.HBM)


def shaped(*shape, dtype=F32):
    return jax.ShapeDtypeStruct(shape, dtype)


def call(kernel, outs, specs, scratch, args, limit, **kwargs):
    return pl.pallas_call(
        kernel,
        out_shape=outs,
        in_specs=specs,
        out_specs=kwargs.pop("out_specs", jax.tree.map(lambda _: VMEM_SPEC, outs)),
        scratch_shapes=scratch,
        compiler_params=pltpu.CompilerParams(vmem_limit_bytes=limit),
        **kwargs,
    )(*args)


def wide_scratch(count):
    return pltpu.VMEM((count + 2 * REACH, 256, 256), BF16)


def build_operator(near, here, blocks, own):
    count = own.shape[0]
    return call(
        functools.partial(build_kernel, count),
        (shaped(count - 2 * REACH, 256, 128), shaped(count, 512, SPAN * 256, dtype=BF16)),
        [HBM_SPEC, SMEM_SPEC, HBM_SPEC, HBM_SPEC],
        [
            wide_scratch(count),
            pltpu.VMEM((RING, 7, 256, 256), F32),
            pltpu.VMEM(own.shape, F32),
            pltpu.VMEM((SPAN, 256, 256), F32),
            pltpu.VMEM((SPAN, 256, 256), F32),
            pltpu.VMEM((512, SPAN * 256), BF16),
            pltpu.VMEM((512, SPAN * 256), BF16),
            pltpu.SMEM(near.shape, jnp.int32),
            pltpu.SemaphoreType.DMA((RING,)),
            pltpu.SemaphoreType.DMA,
            pltpu.SemaphoreType.DMA,
        ],
        (near, here, blocks, own),
        BUILD_LIMIT,
    )


def first_edges(op, own, halos):
    count = own.shape[0]
    edge = shaped(REACH, 256, 128)
    return call(
        functools.partial(first_edge_kernel, count), (edge, edge), [VMEM_SPEC] * 4,
        [wide_scratch(count)], (op, own, *halos), OPERATOR_LIMIT,
    )


def second_inner(here, op, mid, low, high, base):
    count = base.shape[0]
    outs = call(
        functools.partial(inner_kernel, count), (shaped(INNER_ROWS, 128),) * 4 + (shaped(4, INNER_ROWS, 128),),
        [SMEM_SPEC] + [VMEM_SPEC] * 5,
        [wide_scratch(count), pltpu.VMEM((8 * INNER_ROWS, 128), F32)],
        (here, op, mid, low, high, base), OPERATOR_LIMIT,
    )
    return outs[:4], outs[4]


def second_edges(here, op, mid, low, high, halos, base):
    count = base.shape[0]
    outs = call(
        functools.partial(second_edge_kernel, count), (shaped(EDGE_ROWS, 128),) * 4 + (shaped(4, EDGE_ROWS, 128),),
        [SMEM_SPEC] + [VMEM_SPEC] * 7,
        [wide_scratch(count), pltpu.VMEM((8 * EDGE_ROWS, 128), F32)],
        (here, op, mid, low, high, *halos, base), OPERATOR_LIMIT,
    )
    return outs[:4], outs[4]


def bulk_kernel(*refs):
    inner_refs, edge_refs, inner_got, edge_got, out_refs = refs[:4], refs[4:8], refs[8], refs[9], refs[10:]
    for k, out_ref in zip((1, 3), out_refs):
        for i, m in enumerate(relayed_for(k)):
            out_ref[i, 0, :INNER_ROWS] = inner_refs[m][...]
            out_ref[i, 0, INNER_ROWS:] = edge_refs[m][...]
            out_ref[i, 1, :INNER_ROWS] = inner_got[m]
            out_ref[i, 1, INNER_ROWS:] = edge_got[m]


def relay_kernel(below_ref, above_ref, below_inner, below_edge, above_inner, above_edge, inner_ref, edge_ref, inner_got, edge_got, up_ref, down_ref):
    for out_ref in (up_ref, down_ref):
        out_ref[3, :INNER_ROWS] = inner_ref[...]
        out_ref[3, INNER_ROWS:] = edge_ref[...]
        out_ref[4, :INNER_ROWS] = inner_got[2]
        out_ref[4, INNER_ROWS:] = edge_got[2]
    up_ref[0] = below_ref[relayed_for(1).index(3), 0]
    up_ref[1] = below_ref[relayed_for(1).index(0), 0]
    up_ref[2, :INNER_ROWS] = below_inner[...]
    up_ref[2, INNER_ROWS:] = below_edge[...]
    down_ref[0, :INNER_ROWS] = above_inner[...]
    down_ref[0, INNER_ROWS:] = above_edge[...]
    down_ref[1] = above_ref[relayed_for(3).index(0), 1]
    down_ref[2] = above_ref[relayed_for(3).index(1), 1]


def relayed_for(k):
    return [m for m in (0, 1, 3) if m != k]


def add_kernel(a_ref, b_ref, out_ref):
    out_ref[...] = a_ref[...] + b_ref[...]


def fold_kernel(parts_ref, out_ref):
    total = parts_ref[0]
    for at in range(1, parts_ref.shape[0]):
        total = total + parts_ref[at]
    out_ref[...] = total


def copy_kernel(piece_ref, out_ref):
    for at in range(out_ref.shape[0]):
        out_ref[at] = piece_ref[...]


def lanes(start, size):
    return pl.ds(pl.multiple_of(start, size), size)


def places_of(m):
    if m < 2:
        return [(3 * m, 0, 0), (3 * m + 1, 0, 1), (3 * m + 2, 1, 1)]
    return [(6 + 4 * (m - 2) + 2 * a + b, a, b) for a in range(2) for b in range(2)]


def half_of_gram(half, hi_ref, lo_ref, out_ref, start_ref=None):
    for m in range(5):
        (i0, j0), (i1, j1) = PAIRS[m], PAIRS[m + 5]
        i = lanes(jnp.where(half == 0, i0, i1) * TILE, TILE)
        j = lanes(jnp.where(half == 0, j0, j1) * TILE, TILE)
        left_hi, right_hi = hi_ref[:, i], hi_ref[:, j]
        left = jnp.concatenate([left_hi, left_hi, lo_ref[:, i]], axis=0)
        right = jnp.concatenate([right_hi, lo_ref[:, j], right_hi], axis=0)
        block = lax.dot_general(left, right, (((0,), (0,)), ((), ())), preferred_element_type=F32)
        for at, a, b in places_of(m):
            part = block[a * 128 : (a + 1) * 128, b * 128 : (b + 1) * 128]
            out_ref[at] = part if start_ref is None else start_ref[at] + part


def split_rows(at_ref, mine_ref, got_ref, arrived, hi_ref, lo_ref):
    z, c = at_ref[2], at_ref[3]
    for k in range(4):
        for j in range(2):
            band = lax.rem(z + 4 - k, 4) * 2 + lax.rem(c + j, 2)
            value = arrived[3 * j + k - 1][...] if k else (got_ref[0] if j else mine_ref[...])
            hi, lo = split(value)
            hi_ref[:, lanes(band * 128, 128)] = hi
            lo_ref[:, lanes(band * 128, 128)] = lo


def gram_inner_kernel(at_ref, mine_ref, got_ref, *refs):
    arrived, (send_ref, keep_ref, hi_ref, lo_ref) = refs[:6], refs[6:]
    split_rows(at_ref, mine_ref, got_ref, arrived, hi_ref, lo_ref)
    half_of_gram(1 - at_ref[3], hi_ref, lo_ref, send_ref)
    half_of_gram(at_ref[3], hi_ref, lo_ref, keep_ref)


def gram_send_kernel(at_ref, mine_ref, got_ref, *refs):
    arrived, (start_ref, hi_ref, lo_ref, out_ref) = refs[:6], refs[6:]
    split_rows(at_ref, mine_ref, got_ref, arrived, hi_ref, lo_ref)
    half_of_gram(1 - at_ref[3], hi_ref, lo_ref, out_ref, start_ref)


def gram_keep_kernel(at_ref, hi_ref, lo_ref, start_ref, out_ref):
    half_of_gram(at_ref[3], hi_ref, lo_ref, out_ref, start_ref)


def times_normed(hi, lo, nh, nl):
    return dot(jnp.concatenate([hi, hi, lo], axis=1), jnp.concatenate([nh, nl, nh], axis=0))


def poly_kernel(order, at_ref, mine_ref, theirs_ref, ph_ref, pl_ref, stretch_ref, gram_ref, nh_ref, nl_ref, poly_ref):
    z, c = at_ref[2], at_ref[3]
    gram_ref[c] = mine_ref[...]
    gram_ref[1 - c] = theirs_ref[...]
    row = lax.broadcasted_iota(jnp.int32, (128, 128), 0)
    col = lax.broadcasted_iota(jnp.int32, (128, 128), 1)
    diag = jnp.zeros((128, 128), F32)
    for half in range(2):
        for m in range(2):
            for at, a, b in places_of(m):
                if a == b:
                    diag += jnp.where(row == col, gram_ref[half, at], 0.0)
    scale = jnp.sum(diag) / VECTORS
    for n, (i, j) in enumerate(PAIRS):
        for at, a, b in places_of(n % 5):
            hi, lo = split(gram_ref[n // 5, at] / scale)
            p, q = i * TILE + a * 128, j * TILE + b * 128
            nh_ref[p : p + 128, q : q + 128] = hi
            nl_ref[p : p + 128, q : q + 128] = lo
            if p != q:
                nh_ref[q : q + 128, p : p + 128] = hi.T
                nl_ref[q : q + 128, p : p + 128] = lo.T
    stretch_ref[...] = jnp.sqrt(jnp.full((8, 128), order, F32) / scale)
    right = []
    for j in range(2):
        band = lanes((2 * z + lax.rem(c + j, 2)) * 128, 128)
        right.append((nh_ref[:, band], nl_ref[:, band]))
    nh = jnp.concatenate([right[0][0], right[1][0]], axis=1)
    nl = jnp.concatenate([right[0][1], right[1][1]], axis=1)
    squared = times_normed(nh_ref[...], nl_ref[...], nh, nl)
    poly_ref[...] = 3.0 * squared - 10.0 * (nh.astype(F32) + nl.astype(F32))
    for q in range(4):
        for j in range(2):
            band = lax.rem(z + q, 4) * 2 + lax.rem(c + j, 2)
            part = poly_ref[pl.ds(pl.multiple_of(band * 128, 128), 128)]
            if q == 0:
                r = lax.broadcasted_iota(jnp.int32, (128, 256), 0)
                l = lax.broadcasted_iota(jnp.int32, (128, 256), 1)
                part = part + jnp.where(l == r + 128 * j, 15.0, 0.0)
            hi, lo = split(part / 8.0)
            at = q * 256 + j * 128
            ph_ref[at : at + 128] = hi
            pl_ref[at : at + 128] = lo


def turned_kernel(*refs):
    inner_refs, edge_refs, inner_got, edge_got = refs[:4], refs[4:8], refs[8], refs[9]
    arrived, bulks = refs[10:22], refs[22:26]
    ph_ref, pl_ref, stretch_ref, mine_ref, theirs_ref = refs[26:]

    def piece(r, q, j):
        k = (4 - q) % 4
        if q == 0 and j == 0:
            pair = (inner_refs[r][...], edge_refs[r][...])
        elif q == 0:
            pair = (inner_got[r], edge_got[r])
        elif r == 0:
            pair = (arrived[6 * j + k - 1][...], arrived[6 * j + 3 + k - 1][...])
        elif q == 2:
            return bulks[2 + j][r - 1]
        elif (r + k) % 4 == 2:
            return bulks[2 + k // 2][3 + j]
        else:
            return bulks[k // 2][relayed_for(k).index((r + k) % 4), j]
        return jnp.concatenate(pair, axis=0)

    ph, low = ph_ref[...], pl_ref[...]
    for r in range(4):
        highs, lows = [], []
        for q in range(4):
            for j in range(2):
                hi, lo = split(piece(r, q, j))
                highs.append(hi)
                lows.append(lo)
        out = times_normed(jnp.concatenate(highs, axis=1), jnp.concatenate(lows, axis=1), ph, low)
        stretch = stretch_ref[0:1]
        mine_ref[r] = out[:, :128] * stretch
        theirs_ref[r] = out[:, 128:] * stretch


def place_kernel(theirs, at_ref, rows_ref, *refs):
    out_ref, sem = refs[-2:]
    z, c = at_ref[2], at_ref[3]
    half = 1 - c if theirs else c
    copies = []
    for k in range(4):
        chip = lax.rem(z + k, 4)
        inner = pl.ds(pl.multiple_of(512 + (half * 4 + chip) * INNER_ROWS, 128), INNER_ROWS)
        edge = pl.ds(pl.multiple_of(half * 3584 + chip * EDGE_ROWS, 128), EDGE_ROWS)
        copies.append(pltpu.make_async_copy(rows_ref.at[k, pl.ds(0, INNER_ROWS)], out_ref.at[inner], sem.at[k]))
        copies.append(pltpu.make_async_copy(rows_ref.at[k, pl.ds(INNER_ROWS, EDGE_ROWS)], out_ref.at[edge], sem.at[4 + k]))
    for copy in copies:
        copy.start()
    for copy in copies:
        copy.wait()


def place(here, rows, into=None):
    extra = () if into is None else (into,)
    return call(
        functools.partial(place_kernel, into is not None), shaped(4096, 128), [SMEM_SPEC, ANY_SPEC] + [ANY_SPEC] * len(extra),
        [pltpu.SemaphoreType.DMA((8,))], (here, rows, *extra), STEP_LIMIT,
        out_specs=ANY_SPEC, input_output_aliases={2: 0} if extra else {},
    )


SHIFTS = (2, 1, 3)


def swap_cores(x):
    return lax.ppermute(x, "band", [(i, i ^ 1) for i in range(8)])


def shift_z(x, k):
    return lax.ppermute(x, "band", [(i, (i + 2 * k) % 8) for i in range(8)])


def halos_of(first, last):
    size = lax.axis_size("space")
    up = [(i, (i + 1) % size) for i in range(size)]
    down = [(j, i) for i, j in up]
    before = lax.ppermute(last, "space", up)
    return before, lax.ppermute(first, "space", down)


def steps(vectors, blocks, neighbours):
    elem_dev, basis = blocks.shape[0], blocks.shape[2]
    panel = vectors.shape[1]
    order = float(elem_dev * basis * lax.axis_size("space"))
    space, band = lax.axis_index("space"), lax.axis_index("band")
    x, y, z, c = space & 3, space >> 2, band >> 1, band & 1
    here = jnp.stack([x, y, z, c]).astype(jnp.int32)

    start = vectors.reshape(elem_dev, basis, panel)
    halos = halos_of(start[:REACH], start[-REACH:])
    mid, op = build_operator(pltpu.with_memory_space_constraint(neighbours.T, pltpu.HBM), here, blocks, pltpu.with_memory_space_constraint(start, pltpu.HBM))
    low, high = first_edges(op, start, halos)
    halos = halos_of(low, high)
    inner, other = second_inner(here, op, mid, low, high, start)
    inner_got = swap_cores(other)
    arrived = {}
    for j, rows in enumerate((inner, inner_got)):
        for k in SHIFTS:
            arrived[j, 0, k] = shift_z(rows[k], k)
    edge, other = second_edges(here, op, mid, low, high, halos, start)
    edge_got = swap_cores(other)
    for j, rows in enumerate((edge, edge_got)):
        for k in SHIFTS:
            arrived[j, 1, k] = shift_z(rows[k], k)
    half = shaped(18, 128, 128)
    wide = pltpu.VMEM((INNER_ROWS, VECTORS), BF16)
    part_send, part_keep = call(
        gram_inner_kernel, (half, half), [SMEM_SPEC] + [VMEM_SPEC] * 8, [wide, wide],
        (here, inner[0], inner_got, *(arrived[j, 0, k] for j in range(2) for k in (1, 2, 3))), STEP_LIMIT,
    )
    arrived = [arrived[j, e, k] for j in range(2) for e in range(2) for k in (1, 2, 3)]

    share = elem_dev * basis // 8
    held = (*inner, *edge, inner_got, edge_got)
    late, arrived = lax.optimization_barrier((held, arrived))
    bulks = call(bulk_kernel, (shaped(2, 2, share, panel),) * 2, [VMEM_SPEC] * 10, [], late, STEP_LIMIT)
    sent = []
    for k, bulk in zip((1, 3), bulks):
        sent.append(shift_z(bulk, k))

    wide = shaped(EDGE_ROWS, VECTORS, dtype=BF16)
    hi, lo, send = call(
        gram_send_kernel, (wide, wide, half), [SMEM_SPEC] + [VMEM_SPEC] * 9, [],
        (here, edge[0], edge_got, *arrived[3:6], *arrived[9:12], part_send), STEP_LIMIT,
    )
    theirs = swap_cores(send)
    keep = call(gram_keep_kernel, half, [SMEM_SPEC] + [VMEM_SPEC] * 3, [], (here, hi, lo, part_keep), STEP_LIMIT)
    total = call(add_kernel, half, [VMEM_SPEC] * 2, [], (keep, theirs), STEP_LIMIT)
    pieces = total.reshape(16, 144, panel)
    pieces = lax.all_to_all(pieces, "space", split_axis=0, concat_axis=0, tiled=True)
    piece = call(fold_kernel, shaped(144, panel), [VMEM_SPEC], [], (pieces,), STEP_LIMIT)
    sums = [shift_z(piece, k) for k in SHIFTS]
    piece = piece + sums[0] + (sums[1] + sums[2])
    below, above, piece = lax.optimization_barrier((*sent, piece))
    relays = call(
        relay_kernel, (shaped(5, share, panel),) * 2, [VMEM_SPEC] * 10, [],
        (below, above, arrived[0], arrived[3], arrived[8], arrived[11], inner[2], edge[2], inner_got, edge_got), STEP_LIMIT,
    )
    bulks = [below, above]
    for k, relay in zip((1, 3), relays):
        bulks.append(shift_z(relay, k))
    copies = call(copy_kernel, shaped(*pieces.shape), [VMEM_SPEC], [], (piece,), STEP_LIMIT)
    mine = lax.all_to_all(copies, "space", split_axis=0, concat_axis=0, tiled=True)
    mine = mine.reshape(half.shape)
    theirs = swap_cores(mine)

    poly = shaped(VECTORS, TILE, dtype=BF16)
    ph, low, stretch = call(
        functools.partial(poly_kernel, order), (poly, poly, shaped(8, 128)), [SMEM_SPEC] + [VMEM_SPEC] * 2,
        [
            pltpu.VMEM((2, *half.shape), F32),
            pltpu.VMEM((VECTORS, VECTORS), BF16),
            pltpu.VMEM((VECTORS, VECTORS), BF16),
            pltpu.VMEM((VECTORS, TILE), F32),
        ],
        (here, mine, theirs), TURN_LIMIT,
    )
    quarter = shaped(4, share, panel)
    mine, theirs = call(
        turned_kernel, (quarter, quarter), [VMEM_SPEC] * 29, [],
        (*held, *arrived, *bulks, ph, low, stretch), TURN_LIMIT,
    )
    theirs = swap_cores(theirs)
    return place(here, theirs, place(here, mine))


def solution(mesh):
    return jax.shard_map(
        steps,
        mesh=mesh,
        in_specs=(P("space", "band"), P("space", None, None, None), P("space", None)),
        out_specs=P("space", "band"),
        check_vma=False,
    )
```
